256 devices in a mesh: dp: 8 (over x, core), clique: 32 (over y, z).
Axes of the slice: x: 4, y: 4, z: 8, core: 2. Of those that a mesh axis runs over, the one named last changes fastest.
Arguments:
- table_rows: int32 [33, 524288], P(None, 'dp'), may hold values from 0 to 255
- attribute_order: int32 [33], replicated, may hold values from 0 to 32, each once
- log_potential: float32 [32, 256, 256], P('clique'), may hold values from -4 to 18
- measure_noise: float32 [32, 256, 256], P('clique'), may hold values from -24 to 24
Outputs:
- updated_potentials: float32 [32, 256, 256], P('clique')
- beliefs: float32 [32, 256, 256], P('clique')
The draws below stay inside these ranges and needn't reach their ends.
Inputs may be any that keep to these rules, and one draw needn't show every extreme that they name: `attribute_order`: each of the 33 attributes appears once.
All inputs are finite; a program needn't handle non-finite values.
Results may differ from the reference program's by a relative error of at most 0.0003.
Values sent between devices are 32-bit elements; how exact they have to be, the bound alone decides.
No kernel may reach another device: no remote copies, remote signals or barrier semaphores. Data moves between devices by JAX's collectives and lax.ppermute only.
A program may use at most 128 MiB of HBM per device.

```python
import math
import jax
import jax.numpy as jnp
from jax import lax

DOM = 256
CELLS = 65536
ROUNDS = 1
CLIQUES = 32
ATTRS = 33
ROWS = 524288


def draw_log_potential(key, part):
    first_key, second_key, third_key, fourth_key = jax.random.split(key, 4)
    base = 0.7 * jax.random.normal(first_key, (CLIQUES, DOM, DOM), jnp.float32)
    upper = math.log(10.0)
    row_offset = jax.random.uniform(second_key, (CLIQUES, DOM, 1), jnp.float32, 0.0, upper)
    column_offset = jax.random.uniform(third_key, (CLIQUES, 1, DOM), jnp.float32, 0.0, upper)
    shifts = jax.random.randint(fourth_key, (CLIQUES, 1, 1), 0, DOM)
    row_index = jnp.arange(DOM, dtype=jnp.int32)[:, None]
    column_index = jnp.arange(DOM, dtype=jnp.int32)[None, :]
    distance = (column_index - row_index - shifts) % DOM
    band_width = 2
    band = jnp.where(distance < band_width, 9.0, 0.0).astype(jnp.float32)
    return jnp.clip(base, -3.5, 3.5) + row_offset + column_offset + band


def touch_ends(array, stream_key, smallest, largest):
    spot = [jax.random.randint(jax.random.fold_in(stream_key, axis), (), 0, length) for axis, length in enumerate(array.shape)]
    widest = array.shape.index(max(array.shape))
    neighbour = spot[:widest] + [(spot[widest] + 1) % array.shape[widest]] + spot[widest + 1:]
    return array.at[tuple(spot)].set(smallest).at[tuple(neighbour)].set(largest)


def block_levels(stream_key, dims, cuts, low, largest):
    gain, own = 1.0, jax.random.fold_in(stream_key, 6)
    for position, blocks in cuts:
        heights = jnp.exp(jax.random.uniform(jax.random.fold_in(own, position), (blocks,), jnp.float32, low / len(cuts), largest / len(cuts)))
        gain = gain * jnp.repeat(heights, dims[position] // blocks).reshape([-1 if axis == position else 1 for axis in range(len(dims))])
    return gain


def normal_values(stream_key, shape, scale, bound, shards=(), kind=jnp.bfloat16):
    gain = block_levels(stream_key, shape, shards, -0.22, 0.18) if shards else 1.0
    array = jax.random.normal(stream_key, shape, jnp.float32) * scale * gain
    return jnp.minimum(jnp.maximum(array, -bound), bound).astype(kind)


def setup_inputs(seed: int = 0) -> dict:
    seeds = jax.random.split(jax.random.key(seed), 5)
    return {
        "table_rows": touch_ends(jax.random.randint(seeds[0], (ATTRS, ROWS), 0, DOM), jax.random.fold_in(seeds[0], 1), 0, DOM - 1).astype(jnp.int32),
        "attribute_order": jax.random.permutation(seeds[1], ATTRS).astype(jnp.int32),
        "log_potential": draw_log_potential(jax.random.fold_in(seeds[4], 71), 0),
        "measure_noise": normal_values(seeds[3], (CLIQUES, DOM, DOM), 4.0, 24.0, ((0, 32),), jnp.float32),
    }


HIGH = lax.Precision.HIGHEST
step_size = 0.25


def count_pair(table_rows, attribute_pair):
    left = jnp.take(table_rows, attribute_pair[0], axis=0)
    right = jnp.take(table_rows, attribute_pair[1], axis=0)
    cell_ids = (left * DOM + right).astype(jnp.int32)
    tally = jnp.zeros((DOM * DOM,), jnp.float32).at[cell_ids].add(jnp.ones(cell_ids.shape, jnp.float32))
    return tally.reshape(DOM, DOM)


def marginals(potential):
    kernels = jnp.exp(potential)

    def go_forward(carry, kernel):
        moved = jnp.dot(carry, kernel, precision=HIGH)
        return moved / jnp.sum(moved), carry

    def go_backward(carry, kernel):
        moved = jnp.dot(kernel, carry, precision=HIGH)
        return moved / jnp.sum(moved), carry

    all_ones = jnp.ones((DOM,), jnp.float32)
    unused_last, forward = lax.scan(go_forward, all_ones, kernels)
    unused_first, backward = lax.scan(go_backward, all_ones, kernels, reverse=True)
    joint = forward[:, :, None] * kernels * backward[:, None, :]
    total = jnp.sum(joint, axis=(1, 2), keepdims=True)
    return joint * (DOM * DOM) / total


def reference(table_rows, attribute_order, log_potential, measure_noise):
    attribute_pairs = jnp.stack([attribute_order[:-1], attribute_order[1:]], axis=1)

    def count_one(attribute_pair):
        return count_pair(table_rows, attribute_pair)

    counts = lax.map(count_one, attribute_pairs)
    measured = (counts + measure_noise) * (CELLS / ROWS)
    potential = log_potential
    beliefs = potential
    for round_id in range(ROUNDS):
        beliefs = marginals(potential)
        potential = potential - step_size * (beliefs - measured)
    return potential, beliefs
```

```python
import functools

import jax
import jax.numpy as jnp
from jax import lax
from jax.experimental import pallas as pl
from jax.experimental.pallas import tpu as pltpu
from jax.sharding import PartitionSpec as P

step_size = 0.25
shift = 7.0
Y, Z, QUAD = 4, 8, 4
VMEM_LIMIT = 50 << 20


def place():
    dp, clique = (lax.axis_index("dp"), lax.axis_index("clique"))
    return (lax.rem(dp, 2), lax.div(clique, Z), lax.rem(clique, Z))


def along_clique(where):
    return [(y * Z + z, where(y, z)[0] * Z + where(y, z)[1]) for y in range(Y) for z in range(Z)]


def along_dp(where):
    return [(2 * x + c, 2 * where(x, c)[0] + where(x, c)[1]) for x in range(4) for c in range(2)]


def other_core(value):
    return lax.ppermute(value, "dp", along_dp(lambda x, c: (x, 1 - c)))


def in_quad(z, step):
    return z // QUAD * QUAD + (z + step) % QUAD


def split(value):
    high = value.astype(jnp.bfloat16)
    low = (value - high.astype(jnp.float32)).astype(jnp.bfloat16)
    return (high, low)


def product(left, right):
    left_high, left_low = split(left)
    right_high, right_low = split(right)
    dot = functools.partial(jnp.dot, preferred_element_type=jnp.float32)
    return dot(left_high, right_high) + (dot(left_high, right_low) + dot(left_low, right_high))


def diagonal(size):
    rows = lax.broadcasted_iota(jnp.int32, (size, size), 0)
    return rows == lax.broadcasted_iota(jnp.int32, (size, size), 1)


def as_column(row, eye):
    return jnp.sum(jnp.where(eye, row, 0.0), axis=1, keepdims=True)


def as_row(column, eye):
    return jnp.sum(jnp.where(eye, column, 0.0), axis=0, keepdims=True)


def row_times(row, matrix, eye):
    moved = jnp.sum(as_column(row, eye) * matrix, axis=0, keepdims=True)
    return moved / jnp.sum(moved, axis=1, keepdims=True)


def times_row(matrix, row, eye):
    moved = as_row(jnp.sum(matrix * row, axis=1, keepdims=True), eye)
    return moved / jnp.sum(moved, axis=1, keepdims=True)


def half_kernel(potential_ref, half_ref):
    core, _, _ = place()
    half = half_ref.shape[0]
    half_ref[...] = jnp.exp(potential_ref[pl.ds(core * half, half), :] - shift)


def put_halves(stack_ref, slot, mine_ref, theirs_ref, core):
    half = mine_ref.shape[0]
    stack_ref[slot, pl.ds(core * half, half), :] = mine_ref[...]
    stack_ref[slot, pl.ds((1 - core) * half, half), :] = theirs_ref[...]


def quad_kernel(potential_ref, a1, a2, a3, b1, b2, b3, quad_ref, product_ref, half_ref):
    core, _, z = place()
    mine = lax.rem(z, QUAD)
    half, size = half_ref.shape
    quad_ref[mine] = jnp.exp(potential_ref[...] - shift)
    for step, (own, sibling) in enumerate(((a1, b1), (a2, b2), (a3, b3)), 1):
        put_halves(quad_ref, lax.rem(mine + QUAD - step, QUAD), own, sibling, core)
    scale = 1.0 / size
    left = product(quad_ref[0], quad_ref[1]) * scale
    right = product(quad_ref[2], quad_ref[3]) * scale
    product_ref[...] = product(left, right) * scale
    half_ref[...] = product_ref[pl.ds(core * half, half), :]


def block_kernel(product_ref, a1, a2, a3, b1, b2, b3, block_ref, message_ref):
    core, y, z = place()
    mine = 2 * lax.rem(y, 2) + lax.div(z, QUAD)
    size = product_ref.shape[0]
    block_ref[mine] = product_ref[...]
    for flip, (own, sibling) in enumerate(((a1, b1), (a2, b2), (a3, b3)), 1):
        put_halves(block_ref, mine ^ flip, own, sibling, core)
    eye = diagonal(size)
    ones = jnp.ones((1, size), jnp.float32)

    @pl.when(y < 2)
    def _():
        row = ones
        for position in range(4):
            row = row_times(row, block_ref[position], eye)
        message_ref[...] = jnp.broadcast_to(row, message_ref.shape)

    @pl.when(y >= 2)
    def _():
        row = ones
        for position in range(4):
            row = times_row(block_ref[3 - position], row, eye)
        message_ref[...] = jnp.broadcast_to(row, message_ref.shape)


def final_kernel(
    scale, potential_ref, noise_ref, quad_ref, block_ref, message_ref, mine_ref, theirs_ref,
    updated_ref, beliefs_ref, counts_ref
):
    core, y, z = place()
    size = potential_ref.shape[0]
    half = mine_ref.shape[0]
    counts_ref[pl.ds(core * half, half), :] = mine_ref[...]
    counts_ref[pl.ds((1 - core) * half, half), :] = theirs_ref[...]
    eye = diagonal(size)
    ones = jnp.ones((1, size), jnp.float32)
    arrived = message_ref[0:1, :]
    in_block = 2 * lax.rem(y, 2) + lax.div(z, QUAD)
    mine = lax.rem(z, QUAD)
    forward = jnp.where(y >= 2, arrived, ones)
    backward = jnp.where(y >= 2, ones, arrived)
    forward = lax.fori_loop(
        0, in_block, lambda i, row: row_times(row, block_ref[i], eye), forward
    )
    forward = lax.fori_loop(0, mine, lambda i, row: row_times(row, quad_ref[i], eye), forward)
    backward = lax.fori_loop(
        0, 3 - in_block, lambda i, row: times_row(block_ref[3 - i], row, eye), backward
    )
    backward = lax.fori_loop(
        0, 3 - mine, lambda i, row: times_row(quad_ref[3 - i], row, eye), backward
    )
    joint = as_column(forward, eye) * quad_ref[mine] * backward
    total = jnp.sum(jnp.sum(joint, axis=0, keepdims=True), axis=1, keepdims=True)
    beliefs = joint * (size * size / total)
    beliefs_ref[...] = beliefs
    measured = (counts_ref[...] + noise_ref[...]) * scale
    updated_ref[...] = potential_ref[...] - step_size * (beliefs - measured)


def count_kernel(part, order_ref, left_ref, right_ref, mine_ref, theirs_ref, total_ref):
    core, y, z = place()
    clique = y * Z + z
    half, size = mine_ref.shape
    step = pl.program_id(0)

    @pl.when(step == 0)
    def _():
        total_ref[...] = jnp.zeros_like(total_ref)

    levels = lax.broadcasted_iota(jnp.int32, (size, part), 0).astype(jnp.bfloat16)
    one = jnp.ones((size, part), jnp.bfloat16)
    zero = jnp.zeros((size, part), jnp.bfloat16)

    def onehot(ref, attribute, begin):
        values = ref[pl.ds(lax.rem(attribute, 8), 1), begin : begin + part]
        values = values.astype(jnp.float32).astype(jnp.bfloat16)
        return jnp.where(values == levels, one, zero).astype(jnp.float8_e4m3fn)

    total = total_ref[...]
    for begin in range(0, left_ref.shape[1], part):
        total = total + lax.dot_general(
            onehot(left_ref, order_ref[clique], begin),
            onehot(right_ref, order_ref[clique + 1], begin),
            (((1,), (1,)), ((), ())),
            preferred_element_type=jnp.float32,
        )
    total_ref[...] = total

    @pl.when(step == pl.num_programs(0) - 1)
    def _():
        mine_ref[...] = total_ref[pl.ds(core * half, half), :]
        theirs_ref[...] = total_ref[pl.ds((1 - core) * half, half), :]


def shape(*dims):
    return jax.ShapeDtypeStruct(dims, jnp.float32)


PARAMS = pltpu.CompilerParams(vmem_limit_bytes=VMEM_LIMIT)


def count_halves(order, table_rows, size):
    window, part = 16384, 8192

    def rows_of(offset):
        def block(step, order_ref):
            return (lax.div(order_ref[lax.axis_index("clique") + offset], 8), step)

        return pl.BlockSpec((8, window), block)

    half = pl.BlockSpec((size // 2, size), lambda step, order_ref: (0, 0))
    return pl.pallas_call(
        functools.partial(count_kernel, part),
        out_shape=(shape(size // 2, size), shape(size // 2, size)),
        grid_spec=pltpu.PrefetchScalarGridSpec(
            num_scalar_prefetch=1,
            grid=(table_rows.shape[1] // window,),
            in_specs=[rows_of(0), rows_of(1)],
            out_specs=(half, half),
            scratch_shapes=[pltpu.VMEM((size, size), jnp.float32)],
        ),
        compiler_params=PARAMS,
        name="counts",
    )(order, table_rows, table_rows)


def per_device(table_rows, attribute_order, log_potential, measure_noise):
    size = log_potential.shape[1]
    potential = log_potential[0]
    call = functools.partial(pl.pallas_call, compiler_params=PARAMS)
    half = call(half_kernel, out_shape=shape(size // 2, size), name="half")(potential)
    quads = [
        lax.ppermute(half, "clique", along_clique(lambda y, z, s=s: (y, in_quad(z, s))))
        for s in (1, 2, 3)
    ]
    mine, theirs = count_halves(attribute_order, table_rows, size)
    sibling_quads = [other_core(value) for value in quads]
    quad, quad_product, half_product = call(
        quad_kernel,
        out_shape=(shape(QUAD, size, size), shape(size, size), shape(size // 2, size)),
        name="quad",
    )(potential, *quads, *sibling_quads)
    moves = (
        lambda y, z: (y, Z - 1 - z),
        lambda y, z: (y ^ 1, z),
        lambda y, z: (y ^ 1, Z - 1 - z),
    )
    blocks = [lax.ppermute(half_product, "clique", along_clique(move)) for move in moves]
    chip_counts = mine + other_core(theirs)
    spread = [
        lax.ppermute(chip_counts, "dp", along_dp(lambda x, c, s=s: ((x + s) % 4, c)))
        for s in (1, 2, 3)
    ]
    sibling_blocks = [other_core(value) for value in blocks]
    block, message = call(
        block_kernel, out_shape=(shape(4, size, size), shape(8, size)), name="block"
    )(quad_product, *blocks, *sibling_blocks)
    message = lax.ppermute(message, "clique", along_clique(lambda y, z: (y ^ 2, z)))
    counts = chip_counts + spread[0] + spread[1] + spread[2]
    sibling_counts = other_core(counts)
    total_rows = table_rows.shape[1] * lax.axis_size("dp")
    updated, beliefs = call(
        functools.partial(final_kernel, size * size / total_rows),
        out_shape=(shape(size, size), shape(size, size)),
        scratch_shapes=[pltpu.VMEM((size, size), jnp.float32)],
        name="final",
    )(potential, measure_noise[0], quad, block, message, counts, sibling_counts)
    return (updated[None], beliefs[None])


def solution(mesh):
    in_specs = (P(None, "dp"), P(), P("clique", None, None), P("clique", None, None))
    out_specs = (P("clique", None, None), P("clique", None, None))
    return jax.shard_map(
        per_device, mesh=mesh, in_specs=in_specs, out_specs=out_specs, check_vma=False
    )
```

```python
import functools

import jax
import jax.numpy as jnp
from jax import lax
from jax.experimental import pallas as pl
from jax.experimental.pallas import tpu as pltpu
from jax.sharding import PartitionSpec as P

step_size = 0.25
shift = 7.0
Y, Z, QUAD = 4, 8, 4
VMEM_LIMIT = 50 << 20


def place():
    dp, clique = (lax.axis_index("dp"), lax.axis_index("clique"))
    return (lax.rem(dp, 2), lax.div(clique, Z), lax.rem(clique, Z))


def along_clique(where):
    return [(y * Z + z, where(y, z)[0] * Z + where(y, z)[1]) for y in range(Y) for z in range(Z)]


def along_dp(where):
    return [(2 * x + c, 2 * where(x, c)[0] + where(x, c)[1]) for x in range(4) for c in range(2)]


def other_core(value):
    return lax.ppermute(value, "dp", along_dp(lambda x, c: (x, 1 - c)))


def in_quad(z, step):
    return z // QUAD * QUAD + (z + step) % QUAD


def split(value):
    high = value.astype(jnp.bfloat16)
    low = (value - high.astype(jnp.float32)).astype(jnp.bfloat16)
    return (high, low)


def product(left, right):
    left_high, left_low = split(left)
    right_high, right_low = split(right)
    dot = functools.partial(jnp.dot, preferred_element_type=jnp.float32)
    return dot(left_high, right_high) + (dot(left_high, right_low) + dot(left_low, right_high))


def diagonal(size):
    rows = lax.broadcasted_iota(jnp.int32, (size, size), 0)
    return rows == lax.broadcasted_iota(jnp.int32, (size, size), 1)


def as_column(row, eye):
    return jnp.sum(jnp.where(eye, row, 0.0), axis=1, keepdims=True)


def as_row(column, eye):
    return jnp.sum(jnp.where(eye, column, 0.0), axis=0, keepdims=True)


def row_times(row, matrix, eye):
    moved = jnp.sum(as_column(row, eye) * matrix, axis=0, keepdims=True)
    return moved / jnp.sum(moved, axis=1, keepdims=True)


def times_row(matrix, row, eye):
    moved = as_row(jnp.sum(matrix * row, axis=1, keepdims=True), eye)
    return moved / jnp.sum(moved, axis=1, keepdims=True)


def half_kernel(order_ref, potential_ref, order_out_ref, half_ref, copied_ref, semaphore):
    core, _, _ = place()
    half = half_ref.shape[0]
    copy = pltpu.make_async_copy(
        potential_ref.at[pl.ds(core * half, half), :], copied_ref, semaphore
    )
    copy.start()
    order_out_ref[...] = order_ref[...]
    copy.wait()
    half_ref[...] = jnp.exp(copied_ref[...] - shift)


def put_halves(stack_ref, slot, mine_ref, theirs_ref, core):
    half = mine_ref.shape[0]
    stack_ref[slot, pl.ds(core * half, half), :] = mine_ref[...]
    stack_ref[slot, pl.ds((1 - core) * half, half), :] = theirs_ref[...]


def quad_kernel(potential_ref, a1, a2, a3, b1, b2, b3, quad_ref, product_ref, half_ref):
    core, _, z = place()
    mine = lax.rem(z, QUAD)
    half, size = half_ref.shape
    quad_ref[mine] = jnp.exp(potential_ref[...] - shift)
    for step, (own, sibling) in enumerate(((a1, b1), (a2, b2), (a3, b3)), 1):
        put_halves(quad_ref, lax.rem(mine + QUAD - step, QUAD), own, sibling, core)
    scale = 1.0 / size
    left = product(quad_ref[0], quad_ref[1]) * scale
    right = product(quad_ref[2], quad_ref[3]) * scale
    whole = product(left, right) * scale
    largest = jnp.max(jnp.max(whole, axis=0, keepdims=True), axis=1, keepdims=True)
    product_ref[...] = whole / largest
    half_ref[...] = product_ref[pl.ds(core * half, half), :]


def octet_kernel(product_ref, own_ref, sibling_ref, other_ref, half_ref):
    core, _, z = place()
    half = half_ref.shape[0]
    rows = pl.ds(core * half, half)
    other_ref[rows, :] = own_ref[...]
    other_ref[pl.ds((1 - core) * half, half), :] = sibling_ref[...]

    @pl.when(z < QUAD)
    def _():
        half_ref[...] = product(product_ref[rows, :], other_ref[...])

    @pl.when(z >= QUAD)
    def _():
        half_ref[...] = product(other_ref[rows, :], product_ref[...])


def final_kernel(
    scale, potential_ref, noise_ref, quad_ref, other_ref, a1, a2, a3, b1, b2, b3, mine_ref, theirs_ref,
    updated_ref, beliefs_ref, octet_ref
):
    core, y, z = place()
    size = potential_ref.shape[0]
    half = mine_ref.shape[0]
    for step, (own, sibling) in enumerate(((a1, b1), (a2, b2), (a3, b3)), 1):
        put_halves(octet_ref, lax.rem(y + Y - step, Y), own, sibling, core)
    eye = diagonal(size)
    ones = jnp.ones((1, size), jnp.float32)
    later_quad = lax.div(z, QUAD)
    mine = lax.rem(z, QUAD)
    forward = lax.fori_loop(0, y, lambda i, row: row_times(row, octet_ref[i], eye), ones)
    forward = lax.fori_loop(
        0, later_quad, lambda i, row: row_times(row, other_ref[...], eye), forward
    )
    forward = lax.fori_loop(0, mine, lambda i, row: row_times(row, quad_ref[i], eye), forward)
    backward = lax.fori_loop(
        0, Y - 1 - y, lambda i, row: times_row(octet_ref[Y - 1 - i], row, eye), ones
    )
    backward = lax.fori_loop(
        0, 1 - later_quad, lambda i, row: times_row(other_ref[...], row, eye), backward
    )
    backward = lax.fori_loop(
        0, 3 - mine, lambda i, row: times_row(quad_ref[3 - i], row, eye), backward
    )
    joint = as_column(forward, eye) * quad_ref[mine] * backward
    total = jnp.sum(jnp.sum(joint, axis=0, keepdims=True), axis=1, keepdims=True)
    beliefs_ref[...] = joint * (size * size / total)
    for place_at, counts_ref in ((core, mine_ref), (1 - core, theirs_ref)):
        rows = pl.ds(place_at * half, half)
        measured = (counts_ref[...] + noise_ref[rows, :]) * scale
        updated_ref[rows, :] = potential_ref[rows, :] - step_size * (beliefs_ref[rows, :] - measured)


def count_kernel(part, order_ref, left_ref, right_ref, *refs):
    _, y, z = place()
    clique = y * Z + z
    step = pl.program_id(0)
    total_ref = refs[-1]
    size = total_ref.shape[0]

    @pl.when(step == 0)
    def _():
        total_ref[...] = refs[0][...] if len(refs) > 2 else jnp.zeros_like(total_ref)

    levels = lax.broadcasted_iota(jnp.int32, (size, part), 0).astype(jnp.bfloat16)
    one = jnp.ones((size, part), jnp.bfloat16)
    zero = jnp.zeros((size, part), jnp.bfloat16)

    def onehot(ref, attribute, begin):
        values = ref[pl.ds(lax.rem(attribute, 8), 1), begin : begin + part]
        values = values.astype(jnp.float32).astype(jnp.bfloat16)
        return jnp.where(values == levels, one, zero).astype(jnp.float8_e4m3fn)

    total = total_ref[...]
    for begin in range(0, left_ref.shape[1], part):
        total = total + lax.dot_general(
            onehot(left_ref, order_ref[clique], begin),
            onehot(right_ref, order_ref[clique + 1], begin),
            (((1,), (1,)), ((), ())),
            preferred_element_type=jnp.float32,
        )
    total_ref[...] = total

    if len(refs) > 2:

        @pl.when(step == pl.num_programs(0) - 1)
        def _():
            core, _, _ = place()
            mine_ref, theirs_ref = refs[1:3]
            half = size // 2
            mine_ref[...] = total_ref[pl.ds(core * half, half), :]
            theirs_ref[...] = total_ref[pl.ds((1 - core) * half, half), :]


def shape(*dims):
    return jax.ShapeDtypeStruct(dims, jnp.float32)


PARAMS = pltpu.CompilerParams(vmem_limit_bytes=VMEM_LIMIT)


def count_rows(order, table_rows, size, first, last, window, part, earlier=None):
    def rows_of(offset):
        def block(step, order_ref):
            return (lax.div(order_ref[lax.axis_index("clique") + offset], 8), first + step)

        return pl.BlockSpec((8, window), block)

    half = pl.BlockSpec((size // 2, size), lambda step, order_ref: (0, 0))
    whole = pl.BlockSpec((size, size), lambda step, order_ref: (0, 0))
    resumed = earlier is not None
    return pl.pallas_call(
        functools.partial(count_kernel, part),
        out_shape=(shape(size // 2, size),) * 2 if resumed else shape(size, size),
        grid_spec=pltpu.PrefetchScalarGridSpec(
            num_scalar_prefetch=1,
            grid=(last - first,),
            in_specs=[rows_of(0), rows_of(1)] + [whole] * resumed,
            out_specs=(half, half) if resumed else whole,
            scratch_shapes=[pltpu.VMEM((size, size), jnp.float32)] * resumed,
        ),
        compiler_params=PARAMS,
        name="counts",
    )(order, table_rows, table_rows, *((earlier,) if resumed else ()))


def per_device(table_rows, attribute_order, log_potential, measure_noise):
    size = log_potential.shape[1]
    potential = log_potential[0]
    call = functools.partial(pl.pallas_call, compiler_params=PARAMS)
    vmem = pl.BlockSpec(memory_space=pltpu.VMEM)
    order, half = call(
        half_kernel,
        in_specs=[vmem, pl.BlockSpec(memory_space=pl.ANY)],
        out_specs=(vmem, vmem),
        out_shape=(jax.ShapeDtypeStruct(attribute_order.shape, jnp.int32), shape(size // 2, size)),
        scratch_shapes=[pltpu.VMEM((size // 2, size), jnp.float32), pltpu.SemaphoreType.DMA],
        name="half",
    )(attribute_order, potential)
    quads = [
        lax.ppermute(half, "clique", along_clique(lambda y, z, s=s: (y, in_quad(z, s))))
        for s in (1, 2, 3)
    ]
    window, part = 16384, 8192
    windows = table_rows.shape[1] // window
    first_part = windows // 2
    early = count_rows(order, table_rows, size, 0, first_part, window, part)
    quads, early = lax.optimization_barrier((quads, early))
    sibling_quads = [other_core(value) for value in quads]
    quad, quad_product, half_product = call(
        quad_kernel,
        out_shape=(shape(QUAD, size, size), shape(size, size), shape(size // 2, size)),
        name="quad",
    )(potential, *quads, *sibling_quads)
    other = lax.ppermute(half_product, "clique", along_clique(lambda y, z: (y, Z - 1 - z)))
    early, quad_product = lax.optimization_barrier((early, quad_product))
    mine, theirs = count_rows(
        order, table_rows, size, first_part, windows, window, part, early
    )
    other, mine, theirs = lax.optimization_barrier((other, mine, theirs))
    sibling_other = other_core(other)
    other_product, half_octet = call(
        octet_kernel, out_shape=(shape(size, size), shape(size // 2, size)), name="octet"
    )(quad_product, other, sibling_other)
    octets = [
        lax.ppermute(half_octet, "clique", along_clique(lambda y, z, s=s: ((y + s) % Y, z)))
        for s in (1, 2, 3)
    ]
    chip_counts = mine + other_core(theirs)
    chip_counts, other_product = lax.optimization_barrier((chip_counts, other_product))
    spread = [
        lax.ppermute(chip_counts, "dp", along_dp(lambda x, c, s=s: ((x + s) % 4, c)))
        for s in (1, 2, 3)
    ]
    sibling_octets = [other_core(value) for value in octets]
    counts = chip_counts + spread[0] + spread[1] + spread[2]
    sibling_counts = other_core(counts)
    total_rows = table_rows.shape[1] * lax.axis_size("dp")
    updated, beliefs = call(
        functools.partial(final_kernel, size * size / total_rows),
        out_shape=(shape(size, size), shape(size, size)),
        scratch_shapes=[pltpu.VMEM((Y, size, size), jnp.float32)],
        name="final",
    )(
        potential, measure_noise[0], quad, other_product, *octets, *sibling_octets,
        counts, sibling_counts,
    )
    return (updated[None], beliefs[None])


def solution(mesh):
    in_specs = (P(None, "dp"), P(), P("clique", None, None), P("clique", None, None))
    out_specs = (P("clique", None, None), P("clique", None, None))
    return jax.shard_map(
        per_device, mesh=mesh, in_specs=in_specs, out_specs=out_specs, check_vma=False
    )
```

```python
import functools

import jax
import jax.numpy as jnp
from jax import lax
from jax.experimental import pallas as pl
from jax.experimental.pallas import tpu as pltpu
from jax.sharding import PartitionSpec as P

step_size = 0.25
shift = 7.0
Y, Z, QUAD = 4, 8, 4
VMEM_LIMIT = 50 << 20


def place():
    dp, clique = (lax.axis_index("dp"), lax.axis_index("clique"))
    return (lax.rem(dp, 2), lax.div(clique, Z), lax.rem(clique, Z))


def along_clique(where):
    return [(y * Z + z, where(y, z)[0] * Z + where(y, z)[1]) for y in range(Y) for z in range(Z)]


def along_dp(where):
    return [(2 * x + c, 2 * where(x, c)[0] + where(x, c)[1]) for x in range(4) for c in range(2)]


def other_core(value):
    return lax.ppermute(value, "dp", along_dp(lambda x, c: (x, 1 - c)))


def in_quad(z, step):
    return z // QUAD * QUAD + (z + step) % QUAD


def split(value):
    high = value.astype(jnp.bfloat16)
    low = (value - high.astype(jnp.float32)).astype(jnp.bfloat16)
    return (high, low)


def product(left, right):
    left_high, left_low = split(left)
    right_high, right_low = split(right)
    dot = functools.partial(jnp.dot, preferred_element_type=jnp.float32)
    return dot(left_high, right_high) + (dot(left_high, right_low) + dot(left_low, right_high))


def diagonal(size):
    rows = lax.broadcasted_iota(jnp.int32, (size, size), 0)
    return rows == lax.broadcasted_iota(jnp.int32, (size, size), 1)


def as_column(row, eye):
    return jnp.sum(jnp.where(eye, row, 0.0), axis=1, keepdims=True)


def as_row(column, eye):
    return jnp.sum(jnp.where(eye, column, 0.0), axis=0, keepdims=True)


def row_times(row, matrix, eye):
    column = as_column(row, eye) / jnp.sum(row, axis=1, keepdims=True)
    return jnp.sum(column * matrix, axis=0, keepdims=True)


def times_row(matrix, row, eye):
    column = jnp.sum(matrix * row, axis=1, keepdims=True)
    return as_row(column, eye) / jnp.sum(column, axis=0, keepdims=True)


def read_kernel(order_hbm, potential_hbm, order_ref, kernel_ref, half_ref, copied_ref, semaphores):
    core, _, _ = place()
    copies = (
        pltpu.make_async_copy(order_hbm, order_ref, semaphores.at[0]),
        pltpu.make_async_copy(potential_hbm, copied_ref, semaphores.at[1]),
    )
    for copy in copies:
        copy.start()
    for copy in copies:
        copy.wait()
    half = half_ref.shape[0]
    kernel_ref[...] = jnp.exp(copied_ref[...] - shift)
    half_ref[...] = kernel_ref[pl.ds(core * half, half), :]


def put_others(stack_ref, mine, near, near_sibling, far, far_sibling, core):
    count = stack_ref.shape[0]
    half = far.shape[0]
    before, after, across = (lax.rem(mine + count + move, count) for move in (-1, 1, 2))
    stack_ref[jnp.where(core == 0, before, after)] = near[...]
    stack_ref[jnp.where(core == 0, after, before)] = near_sibling[...]
    stack_ref[across, pl.ds(core * half, half), :] = far[...]
    stack_ref[across, pl.ds((1 - core) * half, half), :] = far_sibling[...]


def quad_kernel(kernel_ref, near, near_sibling, far, far_sibling, quad_ref, product_ref, half_ref):
    core, _, z = place()
    mine = lax.rem(z, QUAD)
    half, size = half_ref.shape
    quad_ref[mine] = kernel_ref[...]
    put_others(quad_ref, mine, near, near_sibling, far, far_sibling, core)
    scale = 1.0 / size
    left = product(quad_ref[0], quad_ref[1]) * scale
    right = product(quad_ref[2], quad_ref[3]) * scale
    whole = product(left, right) * scale
    largest = jnp.max(jnp.max(whole, axis=0, keepdims=True), axis=1, keepdims=True)
    product_ref[...] = whole / largest
    half_ref[...] = product_ref[pl.ds(core * half, half), :]


def octet_kernel(product_ref, own_ref, sibling_ref, other_ref, octet_ref, half_ref):
    core, _, z = place()
    half = half_ref.shape[0]
    rows = pl.ds(core * half, half)
    other_ref[rows, :] = own_ref[...]
    other_ref[pl.ds((1 - core) * half, half), :] = sibling_ref[...]

    @pl.when(z < QUAD)
    def _():
        octet_ref[...] = product(product_ref[...], other_ref[...])

    @pl.when(z >= QUAD)
    def _():
        octet_ref[...] = product(other_ref[...], product_ref[...])

    half_ref[...] = octet_ref[rows, :]


def chip_kernel(own_ref, sibling_ref, both_ref, half_ref):
    core, _, _ = place()
    half = half_ref.shape[0]
    both_ref[...] = own_ref[...] + sibling_ref[...]
    half_ref[...] = both_ref[pl.ds(core * half, half), :]


def join_kernel(near_ref, far_ref, sum_ref):
    core, _, _ = place()
    half = far_ref.shape[0]
    sum_ref[...] = near_ref[...]
    sum_ref[pl.ds(core * half, half), :] += far_ref[...]


def final_kernel(
    scale, potential_ref, noise_ref, quad_ref, other_ref, near, near_sibling, far, far_sibling,
    chip_ref, join_ref, sibling_join_ref, updated_ref, beliefs_ref, octet_ref
):
    core, y, z = place()
    size = potential_ref.shape[0]
    put_others(octet_ref, y, near, near_sibling, far, far_sibling, core)
    eye = diagonal(size)
    ones = jnp.ones((1, size), jnp.float32)
    later_quad = lax.div(z, QUAD)
    mine = lax.rem(z, QUAD)
    forward = lax.fori_loop(0, y, lambda i, row: row_times(row, octet_ref[i], eye), ones)
    forward = lax.fori_loop(
        0, later_quad, lambda i, row: row_times(row, other_ref[...], eye), forward
    )
    forward = lax.fori_loop(0, mine, lambda i, row: row_times(row, quad_ref[i], eye), forward)
    backward = lax.fori_loop(
        0, Y - 1 - y, lambda i, row: times_row(octet_ref[Y - 1 - i], row, eye), ones
    )
    backward = lax.fori_loop(
        0, 1 - later_quad, lambda i, row: times_row(other_ref[...], row, eye), backward
    )
    backward = lax.fori_loop(
        0, 3 - mine, lambda i, row: times_row(quad_ref[3 - i], row, eye), backward
    )
    column = as_column(forward, eye) / jnp.sum(forward, axis=1, keepdims=True)
    joint = column * quad_ref[mine] * backward
    total = jnp.sum(jnp.sum(joint, axis=0, keepdims=True), axis=1, keepdims=True)
    beliefs = joint * (size * size / total)
    beliefs_ref[...] = beliefs
    counts = chip_ref[...] + join_ref[...] + sibling_join_ref[...]
    measured = (counts + noise_ref[...]) * scale
    updated_ref[...] = potential_ref[...] - step_size * (beliefs - measured)


def count_kernel(part, order_ref, left_ref, right_ref, total_ref):
    _, y, z = place()
    clique = y * Z + z
    size = total_ref.shape[0]

    @pl.when(pl.program_id(0) == 0)
    def _():
        total_ref[...] = jnp.zeros_like(total_ref)

    levels = lax.broadcasted_iota(jnp.int32, (size, part), 0).astype(jnp.bfloat16)
    one = jnp.ones((size, part), jnp.bfloat16)
    zero = jnp.zeros((size, part), jnp.bfloat16)

    def onehot(ref, attribute, begin):
        values = ref[pl.ds(lax.rem(attribute, 8), 1), begin : begin + part]
        values = values.astype(jnp.float32).astype(jnp.bfloat16)
        return jnp.where(values == levels, one, zero).astype(jnp.float8_e4m3fn)

    total = total_ref[...]
    for begin in range(0, left_ref.shape[1], part):
        total = total + lax.dot_general(
            onehot(left_ref, order_ref[clique], begin),
            onehot(right_ref, order_ref[clique + 1], begin),
            (((1,), (1,)), ((), ())),
            preferred_element_type=jnp.float32,
        )
    total_ref[...] = total


def shape(*dims):
    return jax.ShapeDtypeStruct(dims, jnp.float32)


PARAMS = pltpu.CompilerParams(vmem_limit_bytes=VMEM_LIMIT)


def count_pairs(order, table_rows, size):
    window, part = 16384, 8192

    def rows_of(offset):
        def block(step, order_ref):
            return (lax.div(order_ref[lax.axis_index("clique") + offset], 8), step)

        return pl.BlockSpec((8, window), block)

    return pl.pallas_call(
        functools.partial(count_kernel, part),
        out_shape=shape(size, size),
        grid_spec=pltpu.PrefetchScalarGridSpec(
            num_scalar_prefetch=1,
            grid=(table_rows.shape[1] // window,),
            in_specs=[rows_of(0), rows_of(1)],
            out_specs=pl.BlockSpec((size, size), lambda step, order_ref: (0, 0)),
        ),
        compiler_params=PARAMS,
        name="counts",
    )(order, table_rows, table_rows)


def everywhere(move):
    pairs = []
    for x in range(4):
        for c in range(2):
            for y in range(Y):
                for z in range(Z):
                    to_x, to_y, to_z = move(x, c, y, z)
                    source = (2 * x + c) * Y * Z + y * Z + z
                    pairs.append((source, (2 * to_x + c) * Y * Z + to_y * Z + to_z))
    return pairs


def exchange(whole, half, step):
    axes = ("dp", "clique")
    near = lax.ppermute(whole, axes, everywhere(lambda x, c, y, z: step(x, y, z, 1 - 2 * c)))
    far = lax.ppermute(half, axes, everywhere(lambda x, c, y, z: step(x, y, z, 2)))
    return (near, far)


def per_device(table_rows, attribute_order, log_potential, measure_noise):
    size = log_potential.shape[1]
    potential = log_potential[0]
    call = functools.partial(pl.pallas_call, compiler_params=PARAMS)
    vmem = pl.BlockSpec(memory_space=pltpu.VMEM)
    hbm = pl.BlockSpec(memory_space=pltpu.HBM)
    whole, half = (shape(size, size), shape(size // 2, size))
    order, kernel, half_of_kernel = call(
        read_kernel,
        in_specs=[hbm, hbm],
        out_specs=(vmem, vmem, vmem),
        out_shape=(jax.ShapeDtypeStruct(attribute_order.shape, jnp.int32), whole, half),
        scratch_shapes=[pltpu.VMEM((size, size), jnp.float32), pltpu.SemaphoreType.DMA((2,))],
        name="read",
    )(
        pltpu.with_memory_space_constraint(attribute_order, pltpu.HBM),
        pltpu.with_memory_space_constraint(potential, pltpu.HBM),
    )
    near, far = exchange(
        kernel, half_of_kernel, lambda x, y, z, s: (x, y, z // QUAD * QUAD + (z + s) % QUAD)
    )
    counts = count_pairs(order, table_rows, size)
    near, far, counts = lax.optimization_barrier((near, far, counts))
    quad, quad_product, half_product = call(
        quad_kernel, out_shape=(shape(QUAD, size, size), whole, half), name="quad"
    )(kernel, near, other_core(near), far, other_core(far))
    other = lax.ppermute(half_product, "clique", along_clique(lambda y, z: (y, Z - 1 - z)))
    counts, quad_product = lax.optimization_barrier((counts, quad_product))
    chip_counts, half_counts = call(chip_kernel, out_shape=(whole, half), name="chip")(
        counts, other_core(counts)
    )
    near_counts, far_counts = exchange(
        chip_counts, half_counts, lambda x, y, z, s: ((x + s) % 4, y, z)
    )
    other, chip_counts = lax.optimization_barrier((other, chip_counts))
    other_product, octet, half_octet = call(
        octet_kernel, out_shape=(whole, whole, half), name="octet"
    )(quad_product, other, other_core(other))
    near, far = exchange(octet, half_octet, lambda x, y, z, s: (x, (y + s) % Y, z))
    joined = call(join_kernel, out_shape=whole, name="join")(near_counts, far_counts)
    total_rows = table_rows.shape[1] * lax.axis_size("dp")
    updated, beliefs = call(
        functools.partial(final_kernel, size * size / total_rows),
        out_shape=(whole, whole),
        scratch_shapes=[pltpu.VMEM((Y, size, size), jnp.float32)],
        name="final",
    )(
        potential, measure_noise[0], quad, other_product, near, other_core(near), far,
        other_core(far), chip_counts, joined, other_core(joined),
    )
    return (updated[None], beliefs[None])


def solution(mesh):
    in_specs = (P(None, "dp"), P(), P("clique", None, None), P("clique", None, None))
    out_specs = (P("clique", None, None), P("clique", None, None))
    return jax.shard_map(
        per_device, mesh=mesh, in_specs=in_specs, out_specs=out_specs, check_vma=False
    )
```

```python
import functools

import jax
import jax.numpy as jnp
from jax import lax
from jax.experimental import pallas as pl
from jax.experimental.pallas import tpu as pltpu
from jax.sharding import PartitionSpec as P

step_size = 0.25
shift = 7.0
Y, Z, QUAD = 4, 8, 4
VMEM_LIMIT = 50 << 20


def place():
    dp, clique = (lax.axis_index("dp"), lax.axis_index("clique"))
    return (lax.rem(dp, 2), lax.div(clique, Z), lax.rem(clique, Z))


def along_clique(where):
    return [(y * Z + z, where(y, z)[0] * Z + where(y, z)[1]) for y in range(Y) for z in range(Z)]


def along_dp(where):
    return [(2 * x + c, 2 * where(x, c)[0] + where(x, c)[1]) for x in range(4) for c in range(2)]


def other_core(value):
    return lax.ppermute(value, "dp", along_dp(lambda x, c: (x, 1 - c)))


def in_quad(z, step):
    return z // QUAD * QUAD + (z + step) % QUAD


def split(value):
    high = value.astype(jnp.bfloat16)
    low = (value - high.astype(jnp.float32)).astype(jnp.bfloat16)
    return (high, low)


def product(left, right):
    left_high, left_low = split(left)
    right_high, right_low = split(right)
    dot = functools.partial(jnp.dot, preferred_element_type=jnp.float32)
    return dot(left_high, right_high) + (dot(left_high, right_low) + dot(left_low, right_high))


def diagonal(size):
    rows = lax.broadcasted_iota(jnp.int32, (size, size), 0)
    return rows == lax.broadcasted_iota(jnp.int32, (size, size), 1)


def as_column(row, eye):
    return jnp.sum(jnp.where(eye, row, 0.0), axis=1, keepdims=True)


def as_row(column, eye):
    return jnp.sum(jnp.where(eye, column, 0.0), axis=0, keepdims=True)


def row_times(row, matrix, eye):
    column = as_column(row, eye) / jnp.sum(row, axis=1, keepdims=True)
    return jnp.sum(column * matrix, axis=0, keepdims=True)


def times_row(matrix, row, eye):
    column = jnp.sum(matrix * row, axis=1, keepdims=True)
    return as_row(column, eye) / jnp.sum(column, axis=0, keepdims=True)


def read_kernel(order_hbm, potential_hbm, order_ref, kernel_ref, half_ref, copied_ref, semaphores):
    core, _, _ = place()
    copies = (
        pltpu.make_async_copy(order_hbm, order_ref, semaphores.at[0]),
        pltpu.make_async_copy(potential_hbm, copied_ref, semaphores.at[1]),
    )
    for copy in copies:
        copy.start()
    for copy in copies:
        copy.wait()
    half = half_ref.shape[0]
    kernel_ref[...] = jnp.exp(copied_ref[...] - shift)
    half_ref[...] = kernel_ref[pl.ds(core * half, half), :]


def put_others(stack_ref, mine, near, near_sibling, far, far_sibling, core):
    count = stack_ref.shape[0]
    half = far.shape[0]
    before, after, across = (lax.rem(mine + count + move, count) for move in (-1, 1, 2))
    stack_ref[jnp.where(core == 0, before, after)] = near[...]
    stack_ref[jnp.where(core == 0, after, before)] = near_sibling[...]
    stack_ref[across, pl.ds(core * half, half), :] = far[...]
    stack_ref[across, pl.ds((1 - core) * half, half), :] = far_sibling[...]


def quad_kernel(kernel_ref, near, near_sibling, far, far_sibling, quad_ref, product_ref, half_ref):
    core, _, z = place()
    mine = lax.rem(z, QUAD)
    half, size = half_ref.shape
    quad_ref[mine] = kernel_ref[...]
    put_others(quad_ref, mine, near, near_sibling, far, far_sibling, core)
    scale = 1.0 / size
    left = product(quad_ref[0], quad_ref[1]) * scale
    right = product(quad_ref[2], quad_ref[3]) * scale
    whole = product(left, right) * scale
    largest = jnp.max(jnp.max(whole, axis=0, keepdims=True), axis=1, keepdims=True)
    product_ref[...] = whole / largest
    half_ref[...] = product_ref[pl.ds(core * half, half), :]


def spots():
    core, y, z = place()
    return (core, y, 2 * lax.rem(y, 2) + lax.div(z, QUAD), lax.rem(z, QUAD))


def block_kernel(product_ref, near, near_sibling, far, far_sibling, block_ref, message_ref):
    core, y, mine, _ = spots()
    size, half = (product_ref.shape[0], far.shape[0])
    block_ref[mine] = product_ref[...]
    block_ref[mine ^ (1 + core)] = near[...]
    block_ref[mine ^ (2 - core)] = near_sibling[...]
    block_ref[mine ^ 3, pl.ds(core * half, half), :] = far[...]
    block_ref[mine ^ 3, pl.ds((1 - core) * half, half), :] = far_sibling[...]
    eye = diagonal(size)
    ones = jnp.ones((1, size), jnp.float32)

    @pl.when(y < Y // 2)
    def _():
        row = ones
        for position in range(4):
            row = row_times(row, block_ref[position], eye)
        message_ref[...] = jnp.broadcast_to(row, message_ref.shape)

    @pl.when(y >= Y // 2)
    def _():
        row = ones
        for position in range(4):
            row = times_row(block_ref[3 - position], row, eye)
        message_ref[...] = jnp.broadcast_to(row, message_ref.shape)


def unit_product(left, right):
    moved = product(left, right)
    return moved / jnp.max(jnp.max(moved, axis=0, keepdims=True), axis=1, keepdims=True)


def sides_kernel(quad_ref, block_ref, path_ref, known_ref):
    _, y, in_block, mine = spots()
    size = path_ref.shape[0]
    eye = diagonal(size)
    ones = jnp.ones((1, size), jnp.float32)
    start = jnp.where(eye, 1.0, 0.0)

    @pl.when(y >= Y // 2)
    def _():
        path = lax.fori_loop(0, in_block, lambda i, m: unit_product(m, block_ref[i]), start)
        path_ref[...] = lax.fori_loop(0, mine, lambda i, m: unit_product(m, quad_ref[i]), path)
        row = lax.fori_loop(
            0, 3 - in_block, lambda i, row: times_row(block_ref[3 - i], row, eye), ones
        )
        row = lax.fori_loop(
            0, QUAD - 1 - mine, lambda i, row: times_row(quad_ref[QUAD - 1 - i], row, eye), row
        )
        known_ref[...] = jnp.broadcast_to(row, known_ref.shape)

    @pl.when(y < Y // 2)
    def _():
        path = lax.fori_loop(
            0, 3 - in_block, lambda i, m: unit_product(block_ref[3 - i], m), start
        )
        path_ref[...] = lax.fori_loop(
            0, QUAD - 1 - mine, lambda i, m: unit_product(quad_ref[QUAD - 1 - i], m), path
        )
        row = lax.fori_loop(0, in_block, lambda i, row: row_times(row, block_ref[i], eye), ones)
        row = lax.fori_loop(0, mine, lambda i, row: row_times(row, quad_ref[i], eye), row)
        known_ref[...] = jnp.broadcast_to(row, known_ref.shape)


def chip_kernel(own_ref, sibling_ref, both_ref, half_ref):
    core, _, _ = place()
    half = half_ref.shape[0]
    both_ref[...] = own_ref[...] + sibling_ref[...]
    half_ref[...] = both_ref[pl.ds(core * half, half), :]


def join_kernel(near_ref, far_ref, sum_ref):
    core, _, _ = place()
    half = far_ref.shape[0]
    sum_ref[...] = near_ref[...]
    sum_ref[pl.ds(core * half, half), :] += far_ref[...]


def final_kernel(
    scale, potential_ref, noise_ref, kernel_ref, path_ref, known_ref, message_ref, chip_ref,
    join_ref, sibling_join_ref, updated_ref, beliefs_ref, column_ref, row_ref
):
    _, y, _, _ = spots()
    size = potential_ref.shape[0]
    eye = diagonal(size)
    known, message = (known_ref[0:1, :], message_ref[0:1, :])

    @pl.when(y >= Y // 2)
    def _():
        forward = row_times(message, path_ref[...], eye)
        column_ref[...] = as_column(forward, eye) / jnp.sum(forward, axis=1, keepdims=True)
        row_ref[...] = known

    @pl.when(y < Y // 2)
    def _():
        column_ref[...] = as_column(known, eye) / jnp.sum(known, axis=1, keepdims=True)
        row_ref[...] = times_row(path_ref[...], message, eye)

    joint = column_ref[...] * kernel_ref[...] * row_ref[...]
    total = jnp.sum(jnp.sum(joint, axis=0, keepdims=True), axis=1, keepdims=True)
    beliefs = joint * (size * size / total)
    beliefs_ref[...] = beliefs
    counts = chip_ref[...] + join_ref[...] + sibling_join_ref[...]
    measured = (counts + noise_ref[...]) * scale
    updated_ref[...] = potential_ref[...] - step_size * (beliefs - measured)


def count_kernel(part, order_ref, left_ref, right_ref, total_ref):
    _, y, z = place()
    clique = y * Z + z
    size = total_ref.shape[0]

    @pl.when(pl.program_id(0) == 0)
    def _():
        total_ref[...] = jnp.zeros_like(total_ref)

    levels = lax.broadcasted_iota(jnp.int32, (size, part), 0).astype(jnp.bfloat16)
    one = jnp.ones((size, part), jnp.bfloat16)
    zero = jnp.zeros((size, part), jnp.bfloat16)

    def onehot(ref, attribute, begin):
        values = ref[pl.ds(lax.rem(attribute, 8), 1), begin : begin + part]
        values = values.astype(jnp.float32).astype(jnp.bfloat16)
        return jnp.where(values == levels, one, zero).astype(jnp.float8_e4m3fn)

    total = total_ref[...]
    for begin in range(0, left_ref.shape[1], part):
        total = total + lax.dot_general(
            onehot(left_ref, order_ref[clique], begin),
            onehot(right_ref, order_ref[clique + 1], begin),
            (((1,), (1,)), ((), ())),
            preferred_element_type=jnp.float32,
        )
    total_ref[...] = total


def shape(*dims):
    return jax.ShapeDtypeStruct(dims, jnp.float32)


PARAMS = pltpu.CompilerParams(vmem_limit_bytes=VMEM_LIMIT)


def count_pairs(order, table_rows, size):
    window, part = 16384, 8192

    def rows_of(offset):
        def block(step, order_ref):
            return (lax.div(order_ref[lax.axis_index("clique") + offset], 8), step)

        return pl.BlockSpec((8, window), block)

    return pl.pallas_call(
        functools.partial(count_kernel, part),
        out_shape=shape(size, size),
        grid_spec=pltpu.PrefetchScalarGridSpec(
            num_scalar_prefetch=1,
            grid=(table_rows.shape[1] // window,),
            in_specs=[rows_of(0), rows_of(1)],
            out_specs=pl.BlockSpec((size, size), lambda step, order_ref: (0, 0)),
        ),
        compiler_params=PARAMS,
        name="counts",
    )(order, table_rows, table_rows)


def everywhere(move):
    pairs = []
    for x in range(4):
        for c in range(2):
            for y in range(Y):
                for z in range(Z):
                    to_x, to_y, to_z = move(x, c, y, z)
                    source = (2 * x + c) * Y * Z + y * Z + z
                    pairs.append((source, (2 * to_x + c) * Y * Z + to_y * Z + to_z))
    return pairs


def exchange(whole, half, near_step, far_step):
    axes = ("dp", "clique")
    return (
        lax.ppermute(whole, axes, everywhere(near_step)),
        lax.ppermute(half, axes, everywhere(lambda x, c, y, z: far_step(x, y, z))),
    )


def per_device(table_rows, attribute_order, log_potential, measure_noise):
    size = log_potential.shape[1]
    potential = log_potential[0]
    call = functools.partial(pl.pallas_call, compiler_params=PARAMS)
    vmem = pl.BlockSpec(memory_space=pltpu.VMEM)
    hbm = pl.BlockSpec(memory_space=pltpu.HBM)
    whole, half = (shape(size, size), shape(size // 2, size))
    order, kernel, half_of_kernel = call(
        read_kernel,
        in_specs=[hbm, hbm],
        out_specs=(vmem, vmem, vmem),
        out_shape=(jax.ShapeDtypeStruct(attribute_order.shape, jnp.int32), whole, half),
        scratch_shapes=[pltpu.VMEM((size, size), jnp.float32), pltpu.SemaphoreType.DMA((2,))],
        name="read",
    )(
        pltpu.with_memory_space_constraint(attribute_order, pltpu.HBM),
        pltpu.with_memory_space_constraint(potential, pltpu.HBM),
    )
    near, far = exchange(
        kernel,
        half_of_kernel,
        lambda x, c, y, z: (x, y, z // QUAD * QUAD + (z + 1 - 2 * c) % QUAD),
        lambda x, y, z: (x, y, z ^ 2),
    )
    counts = count_pairs(order, table_rows, size)
    near, far, counts = lax.optimization_barrier((near, far, counts))
    quad, quad_product, half_product = call(
        quad_kernel, out_shape=(shape(QUAD, size, size), whole, half), name="quad"
    )(kernel, near, other_core(near), far, other_core(far))
    near, far = exchange(
        quad_product,
        half_product,
        lambda x, c, y, z: (x, y ^ 1, z) if c else (x, y, Z - 1 - z),
        lambda x, y, z: (x, y ^ 1, Z - 1 - z),
    )
    counts, quad = lax.optimization_barrier((counts, quad))
    chip_counts, half_counts = call(chip_kernel, out_shape=(whole, half), name="chip")(
        counts, other_core(counts)
    )
    near_counts, far_counts = exchange(
        chip_counts,
        half_counts,
        lambda x, c, y, z: ((x + 1 - 2 * c) % 4, y, z),
        lambda x, y, z: (x ^ 2, y, z),
    )
    near, far, near_counts, far_counts = lax.optimization_barrier(
        (near, far, near_counts, far_counts)
    )
    block, message = call(
        block_kernel, out_shape=(shape(4, size, size), shape(8, size)), name="block"
    )(quad_product, near, other_core(near), far, other_core(far))
    joined = call(join_kernel, out_shape=whole, name="join")(near_counts, far_counts)
    arrived = lax.ppermute(message, "clique", along_clique(lambda y, z: (y ^ 2, z)))
    path, known = call(sides_kernel, out_shape=(whole, shape(8, size)), name="sides")(quad, block)
    total_rows = table_rows.shape[1] * lax.axis_size("dp")
    updated, beliefs = call(
        functools.partial(final_kernel, size * size / total_rows),
        out_shape=(whole, whole),
        scratch_shapes=[
            pltpu.VMEM((size, 1), jnp.float32),
            pltpu.VMEM((1, size), jnp.float32),
        ],
        name="final",
    )(
        potential, measure_noise[0], kernel, path, known, arrived, chip_counts, joined,
        other_core(joined),
    )
    return (updated[None], beliefs[None])


def solution(mesh):
    in_specs = (P(None, "dp"), P(), P("clique", None, None), P("clique", None, None))
    out_specs = (P("clique", None, None), P("clique", None, None))
    return jax.shard_map(
        per_device, mesh=mesh, in_specs=in_specs, out_specs=out_specs, check_vma=False
    )
```

```python
import functools

import jax
import jax.numpy as jnp
from jax import lax
from jax.experimental import pallas as pl
from jax.experimental.pallas import tpu as pltpu
from jax.sharding import PartitionSpec as P

step_size = 0.25
shift = 7.0
Y, Z, QUAD = 4, 8, 4
VMEM_LIMIT = 50 << 20


def place():
    dp, clique = (lax.axis_index("dp"), lax.axis_index("clique"))
    return (lax.rem(dp, 2), lax.div(clique, Z), lax.rem(clique, Z))


def along_clique(where):
    return [(y * Z + z, where(y, z)[0] * Z + where(y, z)[1]) for y in range(Y) for z in range(Z)]


def along_dp(where):
    return [(2 * x + c, 2 * where(x, c)[0] + where(x, c)[1]) for x in range(4) for c in range(2)]


def other_core(value):
    return lax.ppermute(value, "dp", along_dp(lambda x, c: (x, 1 - c)))


def in_quad(z, step):
    return z // QUAD * QUAD + (z + step) % QUAD


def split(value):
    high = value.astype(jnp.bfloat16)
    low = (value - high.astype(jnp.float32)).astype(jnp.bfloat16)
    return (high, low)


def product(left, right):
    left_high, left_low = split(left)
    right_high, right_low = split(right)
    dot = functools.partial(jnp.dot, preferred_element_type=jnp.float32)
    return dot(left_high, right_high) + (dot(left_high, right_low) + dot(left_low, right_high))


def diagonal(size):
    rows = lax.broadcasted_iota(jnp.int32, (size, size), 0)
    return rows == lax.broadcasted_iota(jnp.int32, (size, size), 1)


def as_column(row, eye):
    return jnp.sum(jnp.where(eye, row, 0.0), axis=1, keepdims=True)


def as_row(column, eye):
    return jnp.sum(jnp.where(eye, column, 0.0), axis=0, keepdims=True)


def row_times(row, matrix, eye):
    column = as_column(row, eye) / jnp.sum(row, axis=1, keepdims=True)
    return jnp.sum(column * matrix, axis=0, keepdims=True)


def times_row(matrix, row, eye):
    column = jnp.sum(matrix * row, axis=1, keepdims=True)
    return as_row(column, eye) / jnp.sum(column, axis=0, keepdims=True)


def read_kernel(order_hbm, potential_hbm, order_ref, kernel_ref, half_ref, copied_ref, semaphores):
    core, _, _ = place()
    copies = (
        pltpu.make_async_copy(order_hbm, order_ref, semaphores.at[0]),
        pltpu.make_async_copy(potential_hbm, copied_ref, semaphores.at[1]),
    )
    for copy in copies:
        copy.start()
    for copy in copies:
        copy.wait()
    half = half_ref.shape[0]
    kernel_ref[...] = jnp.exp(copied_ref[...] - shift)
    half_ref[...] = kernel_ref[pl.ds(core * half, half), :]


def put_others(stack_ref, mine, near, near_sibling, far, far_sibling, core):
    count = stack_ref.shape[0]
    half = far.shape[0]
    before, after, across = (lax.rem(mine + count + move, count) for move in (-1, 1, 2))
    stack_ref[jnp.where(core == 0, before, after)] = near[...]
    stack_ref[jnp.where(core == 0, after, before)] = near_sibling[...]
    stack_ref[across, pl.ds(core * half, half), :] = far[...]
    stack_ref[across, pl.ds((1 - core) * half, half), :] = far_sibling[...]


def quad_kernel(kernel_ref, near, near_sibling, far, far_sibling, quad_ref, product_ref, half_ref):
    core, _, z = place()
    mine = lax.rem(z, QUAD)
    half, size = half_ref.shape
    quad_ref[mine] = kernel_ref[...]
    put_others(quad_ref, mine, near, near_sibling, far, far_sibling, core)
    scale = 1.0 / size
    left = product(quad_ref[0], quad_ref[1]) * scale
    right = product(quad_ref[2], quad_ref[3]) * scale
    whole = product(left, right) * scale
    largest = jnp.max(jnp.max(whole, axis=0, keepdims=True), axis=1, keepdims=True)
    product_ref[...] = whole / largest
    half_ref[...] = product_ref[pl.ds(core * half, half), :]


def spots():
    core, y, z = place()
    return (core, y, 2 * lax.rem(y, 2) + lax.div(z, QUAD), lax.rem(z, QUAD))


def block_kernel(product_ref, near, near_sibling, far, far_sibling, block_ref, message_ref):
    core, y, mine, _ = spots()
    size, half = (product_ref.shape[0], far.shape[0])
    block_ref[mine] = product_ref[...]
    block_ref[mine ^ (1 + core)] = near[...]
    block_ref[mine ^ (2 - core)] = near_sibling[...]
    block_ref[mine ^ 3, pl.ds(core * half, half), :] = far[...]
    block_ref[mine ^ 3, pl.ds((1 - core) * half, half), :] = far_sibling[...]
    eye = diagonal(size)
    ones = jnp.ones((1, size), jnp.float32)

    @pl.when(y < Y // 2)
    def _():
        row = ones
        for position in range(4):
            row = row_times(row, block_ref[position], eye)
        message_ref[...] = jnp.broadcast_to(row, message_ref.shape)

    @pl.when(y >= Y // 2)
    def _():
        row = ones
        for position in range(4):
            row = times_row(block_ref[3 - position], row, eye)
        message_ref[...] = jnp.broadcast_to(row, message_ref.shape)


def unit_product(left, right):
    moved = product(left, right)
    return moved / jnp.max(jnp.max(moved, axis=0, keepdims=True), axis=1, keepdims=True)


def sides_kernel(quad_ref, block_ref, path_ref, known_ref):
    _, y, in_block, mine = spots()
    size = path_ref.shape[0]
    eye = diagonal(size)
    ones = jnp.ones((1, size), jnp.float32)
    start = jnp.where(eye, 1.0, 0.0)

    @pl.when(y >= Y // 2)
    def _():
        path = lax.fori_loop(0, in_block, lambda i, m: unit_product(m, block_ref[i]), start)
        path_ref[...] = lax.fori_loop(0, mine, lambda i, m: unit_product(m, quad_ref[i]), path)
        row = lax.fori_loop(
            0, 3 - in_block, lambda i, row: times_row(block_ref[3 - i], row, eye), ones
        )
        row = lax.fori_loop(
            0, QUAD - 1 - mine, lambda i, row: times_row(quad_ref[QUAD - 1 - i], row, eye), row
        )
        known_ref[...] = jnp.broadcast_to(row, known_ref.shape)

    @pl.when(y < Y // 2)
    def _():
        path = lax.fori_loop(
            0, 3 - in_block, lambda i, m: unit_product(block_ref[3 - i], m), start
        )
        path_ref[...] = lax.fori_loop(
            0, QUAD - 1 - mine, lambda i, m: unit_product(quad_ref[QUAD - 1 - i], m), path
        )
        row = lax.fori_loop(0, in_block, lambda i, row: row_times(row, block_ref[i], eye), ones)
        row = lax.fori_loop(0, mine, lambda i, row: row_times(row, quad_ref[i], eye), row)
        known_ref[...] = jnp.broadcast_to(row, known_ref.shape)


def chip_kernel(own_ref, sibling_ref, both_ref, half_ref):
    core, _, _ = place()
    half = half_ref.shape[0]
    both_ref[...] = own_ref[...] + sibling_ref[...]
    half_ref[...] = both_ref[pl.ds(core * half, half), :]


def join_kernel(near_ref, far_ref, sum_ref):
    core, _, _ = place()
    half = far_ref.shape[0]
    sum_ref[...] = near_ref[...]
    sum_ref[pl.ds(core * half, half), :] += far_ref[...]


def final_kernel(
    scale, potential_ref, noise_ref, kernel_ref, path_ref, known_ref, message_ref, chip_ref,
    join_ref, sibling_join_ref, updated_ref, beliefs_ref, column_ref, row_ref
):
    _, y, _, _ = spots()
    size = potential_ref.shape[0]
    eye = diagonal(size)
    known, message = (known_ref[0:1, :], message_ref[0:1, :])

    @pl.when(y >= Y // 2)
    def _():
        forward = row_times(message, path_ref[...], eye)
        column_ref[...] = as_column(forward, eye) / jnp.sum(forward, axis=1, keepdims=True)
        row_ref[...] = known

    @pl.when(y < Y // 2)
    def _():
        column_ref[...] = as_column(known, eye) / jnp.sum(known, axis=1, keepdims=True)
        row_ref[...] = times_row(path_ref[...], message, eye)

    joint = column_ref[...] * kernel_ref[...] * row_ref[...]
    total = jnp.sum(jnp.sum(joint, axis=0, keepdims=True), axis=1, keepdims=True)
    beliefs = joint * (size * size / total)
    beliefs_ref[...] = beliefs
    counts = chip_ref[...] + join_ref[...] + sibling_join_ref[...]
    measured = (counts + noise_ref[...]) * scale
    updated_ref[...] = potential_ref[...] - step_size * (beliefs - measured)


def count_kernel(part, order_ref, left_ref, right_ref, total_ref):
    _, y, z = place()
    clique = y * Z + z
    size = total_ref.shape[0]

    @pl.when(pl.program_id(0) == 0)
    def _():
        total_ref[...] = jnp.zeros_like(total_ref)

    levels = lax.broadcasted_iota(jnp.int32, (size, part), 0).astype(jnp.bfloat16)
    one = jnp.ones((size, part), jnp.bfloat16)
    zero = jnp.zeros((size, part), jnp.bfloat16)

    def onehot(ref, attribute, begin):
        values = ref[pl.ds(lax.rem(attribute, 8), 1), begin : begin + part]
        values = values.astype(jnp.float32).astype(jnp.bfloat16)
        return jnp.where(values == levels, one, zero).astype(jnp.float8_e4m3fn)

    total = total_ref[...]
    for begin in range(0, left_ref.shape[1], part):
        total = total + lax.dot_general(
            onehot(left_ref, order_ref[clique], begin),
            onehot(right_ref, order_ref[clique + 1], begin),
            (((1,), (1,)), ((), ())),
            preferred_element_type=jnp.float32,
        )
    total_ref[...] = total


def shape(*dims):
    return jax.ShapeDtypeStruct(dims, jnp.float32)


PARAMS = pltpu.CompilerParams(vmem_limit_bytes=VMEM_LIMIT)


def count_pairs(order, table_rows, size):
    window, part = 16384, 8192

    def rows_of(offset):
        def block(step, order_ref):
            return (lax.div(order_ref[lax.axis_index("clique") + offset], 8), step)

        return pl.BlockSpec((8, window), block)

    return pl.pallas_call(
        functools.partial(count_kernel, part),
        out_shape=shape(size, size),
        grid_spec=pltpu.PrefetchScalarGridSpec(
            num_scalar_prefetch=1,
            grid=(table_rows.shape[1] // window,),
            in_specs=[rows_of(0), rows_of(1)],
            out_specs=pl.BlockSpec((size, size), lambda step, order_ref: (0, 0)),
        ),
        compiler_params=PARAMS,
        name="counts",
    )(order, table_rows, table_rows)


def everywhere(move):
    pairs = []
    for x in range(4):
        for c in range(2):
            for y in range(Y):
                for z in range(Z):
                    to_x, to_y, to_z = move(x, c, y, z)
                    source = (2 * x + c) * Y * Z + y * Z + z
                    pairs.append((source, (2 * to_x + c) * Y * Z + to_y * Z + to_z))
    return pairs


def exchange(whole, half, near_step, far_step):
    axes = ("dp", "clique")
    return (
        lax.ppermute(whole, axes, everywhere(near_step)),
        lax.ppermute(half, axes, everywhere(lambda x, c, y, z: far_step(x, y, z))),
    )


def per_device(table_rows, attribute_order, log_potential, measure_noise):
    size = log_potential.shape[1]
    potential = log_potential[0]
    call = functools.partial(pl.pallas_call, compiler_params=PARAMS)
    vmem = pl.BlockSpec(memory_space=pltpu.VMEM)
    hbm = pl.BlockSpec(memory_space=pltpu.HBM)
    whole, half = (shape(size, size), shape(size // 2, size))
    order, kernel, half_of_kernel = call(
        read_kernel,
        in_specs=[hbm, hbm],
        out_specs=(vmem, vmem, vmem),
        out_shape=(jax.ShapeDtypeStruct(attribute_order.shape, jnp.int32), whole, half),
        scratch_shapes=[pltpu.VMEM((size, size), jnp.float32), pltpu.SemaphoreType.DMA((2,))],
        name="read",
    )(
        pltpu.with_memory_space_constraint(attribute_order, pltpu.HBM),
        pltpu.with_memory_space_constraint(potential, pltpu.HBM),
    )
    near, far = exchange(
        kernel,
        half_of_kernel,
        lambda x, c, y, z: (x, y, z // QUAD * QUAD + (z + 1 - 2 * c) % QUAD),
        lambda x, y, z: (x, y, z ^ 2),
    )
    counts = count_pairs(order, table_rows, size)
    near, far, counts = lax.optimization_barrier((near, far, counts))
    quad, quad_product, half_product = call(
        quad_kernel, out_shape=(shape(QUAD, size, size), whole, half), name="quad"
    )(kernel, near, other_core(near), far, other_core(far))
    near, far = exchange(
        quad_product,
        half_product,
        lambda x, c, y, z: (x, y ^ 1, z) if c else (x, y, Z - 1 - z),
        lambda x, y, z: (x, y ^ 1, Z - 1 - z),
    )
    counts, quad = lax.optimization_barrier((counts, quad))
    chip_counts, half_counts = call(chip_kernel, out_shape=(whole, half), name="chip")(
        counts, other_core(counts)
    )
    near_counts, far_counts = exchange(
        chip_counts,
        half_counts,
        lambda x, c, y, z: ((x + 1 - 2 * c) % 4, y, z),
        lambda x, y, z: (x ^ 2, y, z),
    )
    near, far, far_counts = lax.optimization_barrier((near, far, far_counts))
    near_sibling, far_sibling = (other_core(near), other_core(far))
    near_sibling, far_sibling, near_counts = lax.optimization_barrier(
        (near_sibling, far_sibling, near_counts)
    )
    block, message = call(
        block_kernel, out_shape=(shape(4, size, size), shape(8, size)), name="block"
    )(quad_product, near, near_sibling, far, far_sibling)
    joined = call(join_kernel, out_shape=whole, name="join")(near_counts, far_counts)
    arrived = lax.ppermute(message, "clique", along_clique(lambda y, z: (y ^ 2, z)))
    path, known = call(sides_kernel, out_shape=(whole, shape(8, size)), name="sides")(quad, block)
    total_rows = table_rows.shape[1] * lax.axis_size("dp")
    updated, beliefs = call(
        functools.partial(final_kernel, size * size / total_rows),
        out_shape=(whole, whole),
        scratch_shapes=[
            pltpu.VMEM((size, 1), jnp.float32),
            pltpu.VMEM((1, size), jnp.float32),
        ],
        name="final",
    )(
        potential, measure_noise[0], kernel, path, known, arrived, chip_counts, joined,
        other_core(joined),
    )
    return (updated[None], beliefs[None])


def solution(mesh):
    in_specs = (P(None, "dp"), P(), P("clique", None, None), P("clique", None, None))
    out_specs = (P("clique", None, None), P("clique", None, None))
    return jax.shard_map(
        per_device, mesh=mesh, in_specs=in_specs, out_specs=out_specs, check_vma=False
    )
```

```python
import functools

import jax
import jax.numpy as jnp
from jax import lax
from jax.experimental import pallas as pl
from jax.experimental.pallas import tpu as pltpu
from jax.sharding import PartitionSpec as P

step_size = 0.25
shift = 7.0
Y, Z, QUAD, QUADS = 4, 8, 4, 8
VMEM_LIMIT = 50 << 20


def place():
    dp, clique = (lax.axis_index("dp"), lax.axis_index("clique"))
    return (lax.rem(dp, 2), lax.div(clique, Z), lax.rem(clique, Z))


def along_clique(where):
    return [(y * Z + z, where(y, z)[0] * Z + where(y, z)[1]) for y in range(Y) for z in range(Z)]


def along_dp(where):
    return [(2 * x + c, 2 * where(x, c)[0] + where(x, c)[1]) for x in range(4) for c in range(2)]


def other_core(value):
    return lax.ppermute(value, "dp", along_dp(lambda x, c: (x, 1 - c)))


def in_quad(z, step):
    return z // QUAD * QUAD + (z + step) % QUAD


def split(value):
    high = value.astype(jnp.bfloat16)
    low = (value - high.astype(jnp.float32)).astype(jnp.bfloat16)
    return (high, low)


def product(left, right):
    left_high, left_low = split(left)
    right_high, right_low = split(right)
    dot = functools.partial(jnp.dot, preferred_element_type=jnp.float32)
    return dot(left_high, right_high) + (dot(left_high, right_low) + dot(left_low, right_high))


def diagonal(size):
    rows = lax.broadcasted_iota(jnp.int32, (size, size), 0)
    return rows == lax.broadcasted_iota(jnp.int32, (size, size), 1)


def as_column(row, eye):
    return jnp.sum(jnp.where(eye, row, 0.0), axis=1, keepdims=True)


def as_row(column, eye):
    return jnp.sum(jnp.where(eye, column, 0.0), axis=0, keepdims=True)


def row_times(row, matrix, eye):
    column = as_column(row, eye) / jnp.sum(row, axis=1, keepdims=True)
    return jnp.sum(column * matrix, axis=0, keepdims=True)


def times_row(matrix, row, eye):
    column = jnp.sum(matrix * row, axis=1, keepdims=True)
    return as_row(column, eye) / jnp.sum(column, axis=0, keepdims=True)


def read_kernel(order_hbm, potential_hbm, order_ref, kernel_ref, half_ref, copied_ref, semaphores):
    core, _, _ = place()
    copies = (
        pltpu.make_async_copy(order_hbm, order_ref, semaphores.at[0]),
        pltpu.make_async_copy(potential_hbm, copied_ref, semaphores.at[1]),
    )
    for copy in copies:
        copy.start()
    for copy in copies:
        copy.wait()
    half = half_ref.shape[0]
    kernel_ref[...] = jnp.exp(copied_ref[...] - shift)
    half_ref[...] = kernel_ref[pl.ds(core * half, half), :]


def put_others(stack_ref, mine, near, near_sibling, far, far_sibling, core):
    count = stack_ref.shape[0]
    half = far.shape[0]
    before, after, across = (lax.rem(mine + count + move, count) for move in (-1, 1, 2))
    stack_ref[jnp.where(core == 0, before, after)] = near[...]
    stack_ref[jnp.where(core == 0, after, before)] = near_sibling[...]
    stack_ref[across, pl.ds(core * half, half), :] = far[...]
    stack_ref[across, pl.ds((1 - core) * half, half), :] = far_sibling[...]


def quad_kernel(kernel_ref, near, near_sibling, far, far_sibling, quad_ref, product_ref):
    core, _, z = place()
    mine = lax.rem(z, QUAD)
    size = product_ref.shape[0]
    quad_ref[mine] = kernel_ref[...]
    put_others(quad_ref, mine, near, near_sibling, far, far_sibling, core)
    scale = 1.0 / size
    left = product(quad_ref[0], quad_ref[1]) * scale
    right = product(quad_ref[2], quad_ref[3]) * scale
    whole = product(left, right) * scale
    largest = jnp.max(jnp.max(whole, axis=0, keepdims=True), axis=1, keepdims=True)
    product_ref[...] = whole / largest


def spots():
    _, y, z = place()
    return (y * (Z // QUAD) + lax.div(z, QUAD), lax.rem(z, QUAD))


def hop_kernel(hop, product_ref, *refs):
    here, _ = spots()
    message_ref = refs[-1]
    size = product_ref.shape[0]
    eye = diagonal(size)

    def arrived():
        return refs[0][0:1, :] if len(refs) > 1 else jnp.ones((1, size), jnp.float32)

    @pl.when(here == hop - 1)
    def _():
        row = row_times(arrived(), product_ref[...], eye)
        message_ref[...] = jnp.broadcast_to(row, message_ref.shape)

    @pl.when(here == QUADS - hop)
    def _():
        row = times_row(product_ref[...], arrived(), eye)
        message_ref[...] = jnp.broadcast_to(row, message_ref.shape)


def hop_pairs(hop):
    def quad_at(index, x, c, z):
        y, half = divmod(index, Z // QUAD)
        return (2 * x + c) * Y * Z + y * Z + (z if half == 0 else Z - 1 - z)

    pairs = []
    for x in range(4):
        for c in range(2):
            for z in range(QUAD):
                for source, target in ((hop - 1, hop), (QUADS - hop, QUADS - 1 - hop)):
                    pairs.append((quad_at(source, x, c, z), quad_at(target, x, c, z)))
    return pairs


def chip_kernel(own_ref, sibling_ref, both_ref, half_ref):
    core, _, _ = place()
    half = half_ref.shape[0]
    both_ref[...] = own_ref[...] + sibling_ref[...]
    half_ref[...] = both_ref[pl.ds(core * half, half), :]


def join_kernel(near_ref, far_ref, sum_ref):
    core, _, _ = place()
    half = far_ref.shape[0]
    sum_ref[...] = near_ref[...]
    sum_ref[pl.ds(core * half, half), :] += far_ref[...]


def final_kernel(scale, potential_ref, noise_ref, quad_ref, chip_ref, join_ref, sibling_join_ref, *refs):
    messages, (updated_ref, beliefs_ref, carried_ref) = (refs[:-3], refs[-3:])
    here, mine = spots()
    size = potential_ref.shape[0]
    ones = jnp.ones((1, size), jnp.float32)
    carried_ref[0] = ones
    for hop, message_ref in enumerate(messages, 1):
        carried_ref[hop] = message_ref[0:1, :]
    eye = diagonal(size)
    forward = lax.fori_loop(
        0, mine, lambda i, row: row_times(row, quad_ref[i], eye), carried_ref[here]
    )
    backward = lax.fori_loop(
        0,
        QUAD - 1 - mine,
        lambda i, row: times_row(quad_ref[QUAD - 1 - i], row, eye),
        carried_ref[QUADS - 1 - here],
    )
    column = as_column(forward, eye) / jnp.sum(forward, axis=1, keepdims=True)
    joint = column * quad_ref[mine] * backward
    total = jnp.sum(jnp.sum(joint, axis=0, keepdims=True), axis=1, keepdims=True)
    beliefs = joint * (size * size / total)
    beliefs_ref[...] = beliefs
    counts = chip_ref[...] + join_ref[...] + sibling_join_ref[...]
    measured = (counts + noise_ref[...]) * scale
    updated_ref[...] = potential_ref[...] - step_size * (beliefs - measured)


def count_kernel(part, order_ref, left_ref, right_ref, total_ref):
    _, y, z = place()
    clique = y * Z + z
    size = total_ref.shape[0]

    @pl.when(pl.program_id(0) == 0)
    def _():
        total_ref[...] = jnp.zeros_like(total_ref)

    levels = lax.broadcasted_iota(jnp.int32, (size, part), 0).astype(jnp.bfloat16)
    one = jnp.ones((size, part), jnp.bfloat16)
    zero = jnp.zeros((size, part), jnp.bfloat16)

    def onehot(ref, attribute, begin):
        values = ref[pl.ds(lax.rem(attribute, 8), 1), begin : begin + part]
        values = values.astype(jnp.float32).astype(jnp.bfloat16)
        return jnp.where(values == levels, one, zero).astype(jnp.float8_e4m3fn)

    total = total_ref[...]
    for begin in range(0, left_ref.shape[1], part):
        total = total + lax.dot_general(
            onehot(left_ref, order_ref[clique], begin),
            onehot(right_ref, order_ref[clique + 1], begin),
            (((1,), (1,)), ((), ())),
            preferred_element_type=jnp.float32,
        )
    total_ref[...] = total


def shape(*dims):
    return jax.ShapeDtypeStruct(dims, jnp.float32)


PARAMS = pltpu.CompilerParams(vmem_limit_bytes=VMEM_LIMIT)


def count_pairs(order, table_rows, size):
    window, part = 16384, 8192

    def rows_of(offset):
        def block(step, order_ref):
            return (lax.div(order_ref[lax.axis_index("clique") + offset], 8), step)

        return pl.BlockSpec((8, window), block)

    return pl.pallas_call(
        functools.partial(count_kernel, part),
        out_shape=shape(size, size),
        grid_spec=pltpu.PrefetchScalarGridSpec(
            num_scalar_prefetch=1,
            grid=(table_rows.shape[1] // window,),
            in_specs=[rows_of(0), rows_of(1)],
            out_specs=pl.BlockSpec((size, size), lambda step, order_ref: (0, 0)),
        ),
        compiler_params=PARAMS,
        name="counts",
    )(order, table_rows, table_rows)


def everywhere(move):
    pairs = []
    for x in range(4):
        for c in range(2):
            for y in range(Y):
                for z in range(Z):
                    to_x, to_y, to_z = move(x, c, y, z)
                    source = (2 * x + c) * Y * Z + y * Z + z
                    pairs.append((source, (2 * to_x + c) * Y * Z + to_y * Z + to_z))
    return pairs


def exchange(whole, half, near_step, far_step):
    axes = ("dp", "clique")
    return (
        lax.ppermute(whole, axes, everywhere(near_step)),
        lax.ppermute(half, axes, everywhere(lambda x, c, y, z: far_step(x, y, z))),
    )


def per_device(table_rows, attribute_order, log_potential, measure_noise):
    size = log_potential.shape[1]
    potential = log_potential[0]
    call = functools.partial(pl.pallas_call, compiler_params=PARAMS)
    vmem = pl.BlockSpec(memory_space=pltpu.VMEM)
    hbm = pl.BlockSpec(memory_space=pltpu.HBM)
    whole, half = (shape(size, size), shape(size // 2, size))
    order, kernel, half_of_kernel = call(
        read_kernel,
        in_specs=[hbm, hbm],
        out_specs=(vmem, vmem, vmem),
        out_shape=(jax.ShapeDtypeStruct(attribute_order.shape, jnp.int32), whole, half),
        scratch_shapes=[pltpu.VMEM((size, size), jnp.float32), pltpu.SemaphoreType.DMA((2,))],
        name="read",
    )(
        pltpu.with_memory_space_constraint(attribute_order, pltpu.HBM),
        pltpu.with_memory_space_constraint(potential, pltpu.HBM),
    )
    near, far = exchange(
        kernel,
        half_of_kernel,
        lambda x, c, y, z: (x, y, z // QUAD * QUAD + (z + 1 - 2 * c) % QUAD),
        lambda x, y, z: (x, y, z ^ 2),
    )
    counts = count_pairs(order, table_rows, size)
    near, far, counts = lax.optimization_barrier((near, far, counts))
    sibling_counts = other_core(counts)
    quad, quad_product = call(
        quad_kernel, out_shape=(shape(QUAD, size, size), whole), name="quad"
    )(kernel, near, other_core(near), far, other_core(far))
    chip_counts, half_counts = call(chip_kernel, out_shape=(whole, half), name="chip")(
        counts, sibling_counts
    )
    messages = []
    for hop in range(1, QUADS):
        message = call(
            functools.partial(hop_kernel, hop), out_shape=shape(8, size), name="hop"
        )(quad_product, *messages[-1:])
        messages.append(lax.ppermute(message, ("dp", "clique"), hop_pairs(hop)))
        if hop == 2:
            messages[-1], chip_counts, half_counts = lax.optimization_barrier(
                (messages[-1], chip_counts, half_counts)
            )
            near_counts, far_counts = exchange(
                chip_counts,
                half_counts,
                lambda x, c, y, z: ((x + 1 - 2 * c) % 4, y, z),
                lambda x, y, z: (x ^ 2, y, z),
            )
        if hop == 5:
            messages[-1], near_counts, far_counts = lax.optimization_barrier(
                (messages[-1], near_counts, far_counts)
            )
    joined = call(join_kernel, out_shape=whole, name="join")(near_counts, far_counts)
    total_rows = table_rows.shape[1] * lax.axis_size("dp")
    updated, beliefs = call(
        functools.partial(final_kernel, size * size / total_rows),
        out_shape=(whole, whole),
        scratch_shapes=[pltpu.VMEM((QUADS, 1, size), jnp.float32)],
        name="final",
    )(
        potential, measure_noise[0], quad, chip_counts, joined, other_core(joined), *messages
    )
    return (updated[None], beliefs[None])


def solution(mesh):
    in_specs = (P(None, "dp"), P(), P("clique", None, None), P("clique", None, None))
    out_specs = (P("clique", None, None), P("clique", None, None))
    return jax.shard_map(
        per_device, mesh=mesh, in_specs=in_specs, out_specs=out_specs, check_vma=False
    )
```

```python
import functools

import jax
import jax.numpy as jnp
from jax import lax
from jax.experimental import pallas as pl
from jax.experimental.pallas import tpu as pltpu
from jax.sharding import PartitionSpec as P

step_size = 0.25
shift = 7.0
Y, Z, QUAD = 4, 8, 4
VMEM_LIMIT = 50 << 20


def place():
    dp, clique = (lax.axis_index("dp"), lax.axis_index("clique"))
    return (lax.rem(dp, 2), lax.div(clique, Z), lax.rem(clique, Z))


def along_clique(where):
    return [(y * Z + z, where(y, z)[0] * Z + where(y, z)[1]) for y in range(Y) for z in range(Z)]


def along_dp(where):
    return [(2 * x + c, 2 * where(x, c)[0] + where(x, c)[1]) for x in range(4) for c in range(2)]


def other_core(value):
    return lax.ppermute(value, "dp", along_dp(lambda x, c: (x, 1 - c)))


def in_quad(z, step):
    return z // QUAD * QUAD + (z + step) % QUAD


def split(value):
    high = value.astype(jnp.bfloat16)
    low = (value - high.astype(jnp.float32)).astype(jnp.bfloat16)
    return (high, low)


def product(left, right):
    left_high, left_low = split(left)
    right_high, right_low = split(right)
    dot = functools.partial(jnp.dot, preferred_element_type=jnp.float32)
    return dot(left_high, right_high) + (dot(left_high, right_low) + dot(left_low, right_high))


def diagonal(size):
    rows = lax.broadcasted_iota(jnp.int32, (size, size), 0)
    return rows == lax.broadcasted_iota(jnp.int32, (size, size), 1)


def as_column(row, eye):
    return jnp.sum(jnp.where(eye, row, 0.0), axis=1, keepdims=True)


def as_row(column, eye):
    return jnp.sum(jnp.where(eye, column, 0.0), axis=0, keepdims=True)


def row_times(row, matrix, eye):
    column = as_column(row, eye) / jnp.sum(row, axis=1, keepdims=True)
    return jnp.sum(column * matrix, axis=0, keepdims=True)


def times_row(matrix, row, eye):
    column = jnp.sum(matrix * row, axis=1, keepdims=True)
    return as_row(column, eye) / jnp.sum(column, axis=0, keepdims=True)


def read_kernel(order_hbm, potential_hbm, order_ref, kernel_ref, copied_ref, semaphores):
    copies = (
        pltpu.make_async_copy(order_hbm, order_ref, semaphores.at[0]),
        pltpu.make_async_copy(potential_hbm, copied_ref, semaphores.at[1]),
    )
    for copy in copies:
        copy.start()
    for copy in copies:
        copy.wait()
    kernel_ref[...] = jnp.exp(copied_ref[...] - shift)


def quad_kernel(kernel_ref, first, second, third, quad_ref, product_ref):
    _, _, z = place()
    mine = lax.rem(z, QUAD)
    size = product_ref.shape[0]
    quad_ref[mine] = kernel_ref[...]
    for step, arrived in enumerate((first, second, third), 1):
        quad_ref[lax.rem(mine + QUAD - step, QUAD)] = arrived[...]
    scale = 1.0 / size
    left = product(quad_ref[0], quad_ref[1]) * scale
    right = product(quad_ref[2], quad_ref[3]) * scale
    whole = product(left, right) * scale
    largest = jnp.max(jnp.max(whole, axis=0, keepdims=True), axis=1, keepdims=True)
    product_ref[...] = whole / largest


def spots():
    core, y, z = place()
    return (core, y, 2 * lax.rem(y, 2) + lax.div(z, QUAD), lax.rem(z, QUAD))


def block_kernel(product_ref, first, second, third, block_ref, message_ref):
    _, y, mine, _ = spots()
    size = product_ref.shape[0]
    block_ref[mine] = product_ref[...]
    for flip, arrived in enumerate((first, second, third), 1):
        block_ref[mine ^ flip] = arrived[...]
    eye = diagonal(size)
    ones = jnp.ones((1, size), jnp.float32)

    @pl.when(y < Y // 2)
    def _():
        row = ones
        for position in range(4):
            row = row_times(row, block_ref[position], eye)
        message_ref[...] = jnp.broadcast_to(row, message_ref.shape)

    @pl.when(y >= Y // 2)
    def _():
        row = ones
        for position in range(4):
            row = times_row(block_ref[3 - position], row, eye)
        message_ref[...] = jnp.broadcast_to(row, message_ref.shape)


def unit_product(left, right):
    moved = product(left, right)
    return moved / jnp.max(jnp.max(moved, axis=0, keepdims=True), axis=1, keepdims=True)


def sides_kernel(quad_ref, block_ref, path_ref, known_ref):
    _, y, in_block, mine = spots()
    size = path_ref.shape[0]
    eye = diagonal(size)
    ones = jnp.ones((1, size), jnp.float32)
    start = jnp.where(eye, 1.0, 0.0)

    @pl.when(y >= Y // 2)
    def _():
        path = lax.fori_loop(0, in_block, lambda i, m: unit_product(m, block_ref[i]), start)
        path_ref[...] = lax.fori_loop(0, mine, lambda i, m: unit_product(m, quad_ref[i]), path)
        row = lax.fori_loop(
            0, 3 - in_block, lambda i, row: times_row(block_ref[3 - i], row, eye), ones
        )
        row = lax.fori_loop(
            0, QUAD - 1 - mine, lambda i, row: times_row(quad_ref[QUAD - 1 - i], row, eye), row
        )
        known_ref[...] = jnp.broadcast_to(row, known_ref.shape)

    @pl.when(y < Y // 2)
    def _():
        path = lax.fori_loop(
            0, 3 - in_block, lambda i, m: unit_product(block_ref[3 - i], m), start
        )
        path_ref[...] = lax.fori_loop(
            0, QUAD - 1 - mine, lambda i, m: unit_product(quad_ref[QUAD - 1 - i], m), path
        )
        row = lax.fori_loop(0, in_block, lambda i, row: row_times(row, block_ref[i], eye), ones)
        row = lax.fori_loop(0, mine, lambda i, row: row_times(row, quad_ref[i], eye), row)
        known_ref[...] = jnp.broadcast_to(row, known_ref.shape)


def vectors_kernel(path_ref, known_ref, message_ref, vectors_ref):
    _, y, _, _ = spots()
    size = path_ref.shape[0]
    eye = diagonal(size)
    known, message = (known_ref[0:1, :], message_ref[0:1, :])

    @pl.when(y >= Y // 2)
    def _():
        vectors_ref[0:1, :] = row_times(message, path_ref[...], eye)
        vectors_ref[1:2, :] = known

    @pl.when(y < Y // 2)
    def _():
        vectors_ref[0:1, :] = known
        vectors_ref[1:2, :] = times_row(path_ref[...], message, eye)

    vectors_ref[2:, :] = jnp.zeros((vectors_ref.shape[0] - 2, size), jnp.float32)


def final_kernel(
    scale, potential_ref, noise_ref, vectors_ref, sibling_vectors_ref, counts_ref, sibling_counts_ref,
    updated_ref, beliefs_ref
):
    core, _, _, _ = spots()
    size = potential_ref.shape[0]
    eye = diagonal(size)
    vectors = jnp.where(core == 0, vectors_ref[...], sibling_vectors_ref[...])
    forward, backward = (vectors[0:1, :], vectors[1:2, :])
    column = as_column(forward, eye) / jnp.sum(forward, axis=1, keepdims=True)
    joint = column * jnp.exp(potential_ref[...] - shift) * backward
    total = jnp.sum(jnp.sum(joint, axis=0, keepdims=True), axis=1, keepdims=True)
    beliefs = joint * (size * size / total)
    beliefs_ref[...] = beliefs
    counts = jnp.where(core == 0, sibling_counts_ref[...], counts_ref[...])
    measured = (counts + noise_ref[...]) * scale
    updated_ref[...] = potential_ref[...] - step_size * (beliefs - measured)


def count_kernel(part, order_ref, left_ref, right_ref, total_ref):
    _, y, z = place()
    clique = y * Z + z
    size = total_ref.shape[0]

    @pl.when(pl.program_id(0) == 0)
    def _():
        total_ref[...] = jnp.zeros_like(total_ref)

    levels = lax.broadcasted_iota(jnp.int32, (size, part), 0).astype(jnp.bfloat16)
    one = jnp.ones((size, part), jnp.bfloat16)
    zero = jnp.zeros((size, part), jnp.bfloat16)

    def onehot(ref, attribute, begin):
        values = ref[pl.ds(lax.rem(attribute, 8), 1), begin : begin + part]
        values = values.astype(jnp.float32).astype(jnp.bfloat16)
        return jnp.where(values == levels, one, zero).astype(jnp.float8_e4m3fn)

    total = total_ref[...]
    for begin in range(0, left_ref.shape[1], part):
        total = total + lax.dot_general(
            onehot(left_ref, order_ref[clique], begin),
            onehot(right_ref, order_ref[clique + 1], begin),
            (((1,), (1,)), ((), ())),
            preferred_element_type=jnp.float32,
        )
    total_ref[...] = total


def shape(*dims):
    return jax.ShapeDtypeStruct(dims, jnp.float32)


PARAMS = pltpu.CompilerParams(vmem_limit_bytes=VMEM_LIMIT)


def count_pairs(order, table_rows, size):
    window, part = 16384, 8192

    def rows_of(offset):
        def block(step, order_ref):
            return (lax.div(order_ref[lax.axis_index("clique") + offset], 8), step)

        return pl.BlockSpec((8, window), block)

    return pl.pallas_call(
        functools.partial(count_kernel, part),
        out_shape=shape(size, size),
        grid_spec=pltpu.PrefetchScalarGridSpec(
            num_scalar_prefetch=1,
            grid=(table_rows.shape[1] // window,),
            in_specs=[rows_of(0), rows_of(1)],
            out_specs=pl.BlockSpec((size, size), lambda step, order_ref: (0, 0)),
        ),
        compiler_params=PARAMS,
        name="counts",
    )(order, table_rows, table_rows)


def on_core(value, mover, move):
    pairs = []
    for x in range(4):
        for c in range(2):
            for y in range(Y):
                for z in range(Z):
                    to_x, to_y, to_z = move(x, y, z) if c == mover else (x, y, z)
                    source = (2 * x + c) * Y * Z + y * Z + z
                    pairs.append((source, (2 * to_x + c) * Y * Z + to_y * Z + to_z))
    return lax.ppermute(value, ("dp", "clique"), pairs)


def per_device(table_rows, attribute_order, log_potential, measure_noise):
    size = log_potential.shape[1]
    potential = log_potential[0]
    call = functools.partial(pl.pallas_call, compiler_params=PARAMS)
    vmem = pl.BlockSpec(memory_space=pltpu.VMEM)
    hbm = pl.BlockSpec(memory_space=pltpu.HBM)
    whole = shape(size, size)
    order, kernel = call(
        read_kernel,
        in_specs=[hbm, hbm],
        out_specs=(vmem, vmem),
        out_shape=(jax.ShapeDtypeStruct(attribute_order.shape, jnp.int32), whole),
        scratch_shapes=[pltpu.VMEM((size, size), jnp.float32), pltpu.SemaphoreType.DMA((2,))],
        name="read",
    )(
        pltpu.with_memory_space_constraint(attribute_order, pltpu.HBM),
        pltpu.with_memory_space_constraint(potential, pltpu.HBM),
    )
    quads = [
        on_core(kernel, 0, lambda x, y, z, s=s: (x, y, z // QUAD * QUAD + (z + s) % QUAD))
        for s in (1, 2, 3)
    ]
    counts = count_pairs(order, table_rows, size)
    quads, counts = lax.optimization_barrier((quads, counts))
    quad, quad_product = call(
        quad_kernel, out_shape=(shape(QUAD, size, size), whole), name="quad"
    )(kernel, *quads)
    blocks = [
        on_core(quad_product, 0, move)
        for move in (
            lambda x, y, z: (x, y, Z - 1 - z),
            lambda x, y, z: (x, y ^ 1, z),
            lambda x, y, z: (x, y ^ 1, Z - 1 - z),
        )
    ]
    counts, quad = lax.optimization_barrier((counts, quad))
    chip_counts = counts + other_core(counts)
    spread = [
        on_core(chip_counts, 1, lambda x, y, z, s=s: ((x + s) % 4, y, z)) for s in (1, 2, 3)
    ]
    counts = chip_counts + spread[0] + spread[1] + spread[2]
    block, message = call(
        block_kernel, out_shape=(shape(4, size, size), shape(8, size)), name="block"
    )(quad_product, *blocks)
    arrived = on_core(message, 0, lambda x, y, z: (x, y ^ 2, z))
    path, known = call(sides_kernel, out_shape=(whole, shape(8, size)), name="sides")(quad, block)
    arrived, path, counts = lax.optimization_barrier((arrived, path, counts))
    sibling_counts = other_core(counts)
    vectors = call(vectors_kernel, out_shape=shape(8, size), name="vectors")(path, known, arrived)
    total_rows = table_rows.shape[1] * lax.axis_size("dp")
    updated, beliefs = call(
        functools.partial(final_kernel, size * size / total_rows),
        out_shape=(whole, whole),
        name="final",
    )(potential, measure_noise[0], vectors, other_core(vectors), counts, sibling_counts)
    return (updated[None], beliefs[None])


def solution(mesh):
    in_specs = (P(None, "dp"), P(), P("clique", None, None), P("clique", None, None))
    out_specs = (P("clique", None, None), P("clique", None, None))
    return jax.shard_map(
        per_device, mesh=mesh, in_specs=in_specs, out_specs=out_specs, check_vma=False
    )
```

```python
import functools

import jax
import jax.numpy as jnp
from jax import lax
from jax.experimental import pallas as pl
from jax.experimental.pallas import tpu as pltpu
from jax.sharding import PartitionSpec as P

step_size = 0.25
shift = 7.0
Y, Z, QUAD = 4, 8, 4
VMEM_LIMIT = 50 << 20


def place():
    dp, clique = (lax.axis_index("dp"), lax.axis_index("clique"))
    return (lax.rem(dp, 2), lax.div(clique, Z), lax.rem(clique, Z))


def along_clique(where):
    return [(y * Z + z, where(y, z)[0] * Z + where(y, z)[1]) for y in range(Y) for z in range(Z)]


def along_dp(where):
    return [(2 * x + c, 2 * where(x, c)[0] + where(x, c)[1]) for x in range(4) for c in range(2)]


def other_core(value):
    return lax.ppermute(value, "dp", along_dp(lambda x, c: (x, 1 - c)))


def in_quad(z, step):
    return z // QUAD * QUAD + (z + step) % QUAD


def split(value):
    high = value.astype(jnp.bfloat16)
    low = (value - high.astype(jnp.float32)).astype(jnp.bfloat16)
    return (high, low)


def product(left, right):
    left_high, left_low = split(left)
    right_high, right_low = split(right)
    dot = functools.partial(jnp.dot, preferred_element_type=jnp.float32)
    return dot(left_high, right_high) + (dot(left_high, right_low) + dot(left_low, right_high))


def diagonal(size):
    rows = lax.broadcasted_iota(jnp.int32, (size, size), 0)
    return rows == lax.broadcasted_iota(jnp.int32, (size, size), 1)


def as_column(row, eye):
    return jnp.sum(jnp.where(eye, row, 0.0), axis=1, keepdims=True)


def as_row(column, eye):
    return jnp.sum(jnp.where(eye, column, 0.0), axis=0, keepdims=True)


def row_times(row, matrix, eye):
    column = as_column(row, eye) / jnp.sum(row, axis=1, keepdims=True)
    return jnp.sum(column * matrix, axis=0, keepdims=True)


def times_row(matrix, row, eye):
    column = jnp.sum(matrix * row, axis=1, keepdims=True)
    return as_row(column, eye) / jnp.sum(column, axis=0, keepdims=True)


def read_kernel(order_hbm, potential_hbm, order_ref, kernel_ref, half_ref, copied_ref, semaphores):
    core, _, _ = place()
    copies = (
        pltpu.make_async_copy(order_hbm, order_ref, semaphores.at[0]),
        pltpu.make_async_copy(potential_hbm, copied_ref, semaphores.at[1]),
    )
    for copy in copies:
        copy.start()
    for copy in copies:
        copy.wait()
    half = half_ref.shape[0]
    kernel_ref[...] = jnp.exp(copied_ref[...] - shift)
    half_ref[...] = kernel_ref[pl.ds(core * half, half), :]


def put_halves(stack_ref, slot, own, sibling, core):
    half = own.shape[0]
    stack_ref[slot, pl.ds(core * half, half), :] = own[...]
    stack_ref[slot, pl.ds((1 - core) * half, half), :] = sibling[...]


def quad_kernel(kernel_ref, a1, a2, a3, b1, b2, b3, quad_ref, product_ref, half_ref):
    core, _, z = place()
    mine = lax.rem(z, QUAD)
    half, size = half_ref.shape
    quad_ref[mine] = kernel_ref[...]
    for step, (own, sibling) in enumerate(((a1, b1), (a2, b2), (a3, b3)), 1):
        put_halves(quad_ref, lax.rem(mine + QUAD - step, QUAD), own, sibling, core)
    scale = 1.0 / size
    left = product(quad_ref[0], quad_ref[1]) * scale
    right = product(quad_ref[2], quad_ref[3]) * scale
    whole = product(left, right) * scale
    largest = jnp.max(jnp.max(whole, axis=0, keepdims=True), axis=1, keepdims=True)
    product_ref[...] = whole / largest
    half_ref[...] = product_ref[pl.ds(core * half, half), :]


def unit_product(left, right):
    moved = product(left, right)
    return moved / jnp.max(jnp.max(moved, axis=0, keepdims=True), axis=1, keepdims=True)


def paths_kernel(quad_ref, other_ref, before_ref, after_ref):
    _, _, z = place()
    later_quad, mine = (lax.div(z, QUAD), lax.rem(z, QUAD))
    size = before_ref.shape[0]
    unit = jnp.where(diagonal(size), 1.0, 0.0)
    other = other_ref[...]
    before_ref[...] = lax.fori_loop(
        0, mine, lambda i, m: unit_product(m, quad_ref[i]), jnp.where(later_quad == 1, other, unit)
    )
    after_ref[...] = lax.fori_loop(
        0,
        QUAD - 1 - mine,
        lambda i, m: unit_product(m, quad_ref[mine + 1 + i]),
        unit,
    )

    @pl.when(later_quad == 0)
    def _():
        after_ref[...] = unit_product(after_ref[...], other)


def octet_kernel(product_ref, own_ref, sibling_ref, other_ref, half_ref):
    core, _, z = place()
    half = half_ref.shape[0]
    rows = pl.ds(core * half, half)
    other_ref[rows, :] = own_ref[...]
    other_ref[pl.ds((1 - core) * half, half), :] = sibling_ref[...]

    @pl.when(z < QUAD)
    def _():
        half_ref[...] = product(product_ref[rows, :], other_ref[...])

    @pl.when(z >= QUAD)
    def _():
        half_ref[...] = product(other_ref[rows, :], product_ref[...])


def chip_kernel(own_ref, sibling_ref, both_ref, half_ref):
    core, _, _ = place()
    half = half_ref.shape[0]
    both_ref[...] = own_ref[...] + sibling_ref[...]
    half_ref[...] = both_ref[pl.ds(core * half, half), :]


def join_kernel(near_ref, far_ref, sum_ref):
    core, _, _ = place()
    half = far_ref.shape[0]
    sum_ref[...] = near_ref[...]
    sum_ref[pl.ds(core * half, half), :] += far_ref[...]


def final_kernel(
    scale, potential_ref, noise_ref, kernel_ref, before_ref, after_ref, a1, a2, a3, b1, b2, b3,
    chip_ref, join_ref, sibling_join_ref, updated_ref, beliefs_ref, octet_ref
):
    core, y, _ = place()
    size = potential_ref.shape[0]
    for step, (own, sibling) in enumerate(((a1, b1), (a2, b2), (a3, b3)), 1):
        put_halves(octet_ref, lax.rem(y + Y - step, Y), own, sibling, core)
    eye = diagonal(size)
    ones = jnp.ones((1, size), jnp.float32)
    forward = lax.fori_loop(0, y, lambda i, row: row_times(row, octet_ref[i], eye), ones)
    forward = row_times(forward, before_ref[...], eye)
    backward = lax.fori_loop(
        0, Y - 1 - y, lambda i, row: times_row(octet_ref[Y - 1 - i], row, eye), ones
    )
    backward = times_row(after_ref[...], backward, eye)
    column = as_column(forward, eye) / jnp.sum(forward, axis=1, keepdims=True)
    joint = column * kernel_ref[...] * backward
    total = jnp.sum(jnp.sum(joint, axis=0, keepdims=True), axis=1, keepdims=True)
    beliefs = joint * (size * size / total)
    beliefs_ref[...] = beliefs
    counts = chip_ref[...] + join_ref[...] + sibling_join_ref[...]
    measured = (counts + noise_ref[...]) * scale
    updated_ref[...] = potential_ref[...] - step_size * (beliefs - measured)


def count_kernel(part, order_ref, left_ref, right_ref, total_ref):
    _, y, z = place()
    clique = y * Z + z
    size = total_ref.shape[0]

    @pl.when(pl.program_id(0) == 0)
    def _():
        total_ref[...] = jnp.zeros_like(total_ref)

    levels = lax.broadcasted_iota(jnp.int32, (size, part), 0).astype(jnp.bfloat16)
    one = jnp.ones((size, part), jnp.bfloat16)
    zero = jnp.zeros((size, part), jnp.bfloat16)

    def onehot(ref, attribute, begin):
        values = ref[pl.ds(lax.rem(attribute, 8), 1), begin : begin + part]
        values = values.astype(jnp.float32).astype(jnp.bfloat16)
        return jnp.where(values == levels, one, zero).astype(jnp.float8_e4m3fn)

    total = total_ref[...]
    for begin in range(0, left_ref.shape[1], part):
        total = total + lax.dot_general(
            onehot(left_ref, order_ref[clique], begin),
            onehot(right_ref, order_ref[clique + 1], begin),
            (((1,), (1,)), ((), ())),
            preferred_element_type=jnp.float32,
        )
    total_ref[...] = total


def shape(*dims):
    return jax.ShapeDtypeStruct(dims, jnp.float32)


PARAMS = pltpu.CompilerParams(vmem_limit_bytes=VMEM_LIMIT)


def count_pairs(order, table_rows, size):
    window, part = 16384, 8192

    def rows_of(offset):
        def block(step, order_ref):
            return (lax.div(order_ref[lax.axis_index("clique") + offset], 8), step)

        return pl.BlockSpec((8, window), block)

    return pl.pallas_call(
        functools.partial(count_kernel, part),
        out_shape=shape(size, size),
        grid_spec=pltpu.PrefetchScalarGridSpec(
            num_scalar_prefetch=1,
            grid=(table_rows.shape[1] // window,),
            in_specs=[rows_of(0), rows_of(1)],
            out_specs=pl.BlockSpec((size, size), lambda step, order_ref: (0, 0)),
        ),
        compiler_params=PARAMS,
        name="counts",
    )(order, table_rows, table_rows)


def everywhere(move):
    pairs = []
    for x in range(4):
        for c in range(2):
            for y in range(Y):
                for z in range(Z):
                    to_x, to_y, to_z = move(x, c, y, z)
                    source = (2 * x + c) * Y * Z + y * Z + z
                    pairs.append((source, (2 * to_x + c) * Y * Z + to_y * Z + to_z))
    return pairs


def exchange(whole, half, step):
    axes = ("dp", "clique")
    near = lax.ppermute(whole, axes, everywhere(lambda x, c, y, z: step(x, y, z, 1 - 2 * c)))
    far = lax.ppermute(half, axes, everywhere(lambda x, c, y, z: step(x, y, z, 2)))
    return (near, far)


def per_device(table_rows, attribute_order, log_potential, measure_noise):
    size = log_potential.shape[1]
    potential = log_potential[0]
    call = functools.partial(pl.pallas_call, compiler_params=PARAMS)
    vmem = pl.BlockSpec(memory_space=pltpu.VMEM)
    hbm = pl.BlockSpec(memory_space=pltpu.HBM)
    whole, half = (shape(size, size), shape(size // 2, size))
    order, kernel, half_of_kernel = call(
        read_kernel,
        in_specs=[hbm, hbm],
        out_specs=(vmem, vmem, vmem),
        out_shape=(jax.ShapeDtypeStruct(attribute_order.shape, jnp.int32), whole, half),
        scratch_shapes=[pltpu.VMEM((size, size), jnp.float32), pltpu.SemaphoreType.DMA((2,))],
        name="read",
    )(
        pltpu.with_memory_space_constraint(attribute_order, pltpu.HBM),
        pltpu.with_memory_space_constraint(potential, pltpu.HBM),
    )
    quads = [
        lax.ppermute(half_of_kernel, "clique", along_clique(lambda y, z, s=s: (y, in_quad(z, s))))
        for s in (1, 2, 3)
    ]
    counts = count_pairs(order, table_rows, size)
    quads, counts = lax.optimization_barrier((quads, counts))
    quad, quad_product, half_product = call(
        quad_kernel, out_shape=(shape(QUAD, size, size), whole, half), name="quad"
    )(kernel, *quads, *[other_core(value) for value in quads])
    other = lax.ppermute(half_product, "clique", along_clique(lambda y, z: (y, Z - 1 - z)))
    counts, quad = lax.optimization_barrier((counts, quad))
    chip_counts, half_counts = call(chip_kernel, out_shape=(whole, half), name="chip")(
        counts, other_core(counts)
    )
    near_counts, far_counts = exchange(
        chip_counts, half_counts, lambda x, y, z, s: ((x + s) % 4, y, z)
    )
    other, far_counts = lax.optimization_barrier((other, far_counts))
    sibling_other = other_core(other)
    sibling_other, near_counts = lax.optimization_barrier((sibling_other, near_counts))
    other_product, half_octet = call(octet_kernel, out_shape=(whole, half), name="octet")(
        quad_product, other, sibling_other
    )
    octets = [
        lax.ppermute(half_octet, "clique", along_clique(lambda y, z, s=s: ((y + s) % Y, z)))
        for s in (1, 2, 3)
    ]
    before, after = call(paths_kernel, out_shape=(whole, whole), name="paths")(quad, other_product)
    joined = call(join_kernel, out_shape=whole, name="join")(near_counts, far_counts)
    octets, before, joined = lax.optimization_barrier((octets, before, joined))
    total_rows = table_rows.shape[1] * lax.axis_size("dp")
    updated, beliefs = call(
        functools.partial(final_kernel, size * size / total_rows),
        out_shape=(whole, whole),
        scratch_shapes=[pltpu.VMEM((Y, size, size), jnp.float32)],
        name="final",
    )(
        potential, measure_noise[0], kernel, before, after, *octets,
        *[other_core(value) for value in octets], chip_counts, joined, other_core(joined),
    )
    return (updated[None], beliefs[None])


def solution(mesh):
    in_specs = (P(None, "dp"), P(), P("clique", None, None), P("clique", None, None))
    out_specs = (P("clique", None, None), P("clique", None, None))
    return jax.shard_map(
        per_device, mesh=mesh, in_specs=in_specs, out_specs=out_specs, check_vma=False
    )
```

```python
import functools

import jax
import jax.numpy as jnp
from jax import lax
from jax.experimental import pallas as pl
from jax.experimental.pallas import tpu as pltpu
from jax.sharding import PartitionSpec as P

step_size = 0.25
shift = 7.0
Y, Z, QUAD = 4, 8, 4
VMEM_LIMIT = 50 << 20


def place():
    dp, clique = (lax.axis_index("dp"), lax.axis_index("clique"))
    return (lax.rem(dp, 2), lax.div(clique, Z), lax.rem(clique, Z))


def along_clique(where):
    return [(y * Z + z, where(y, z)[0] * Z + where(y, z)[1]) for y in range(Y) for z in range(Z)]


def along_dp(where):
    return [(2 * x + c, 2 * where(x, c)[0] + where(x, c)[1]) for x in range(4) for c in range(2)]


def other_core(value):
    return lax.ppermute(value, "dp", along_dp(lambda x, c: (x, 1 - c)))


def in_quad(z, step):
    return z // QUAD * QUAD + (z + step) % QUAD


def split(value):
    high = value.astype(jnp.bfloat16)
    low = (value - high.astype(jnp.float32)).astype(jnp.bfloat16)
    return (high, low)


def product(left, right):
    left_high, left_low = split(left)
    right_high, right_low = split(right)
    dot = functools.partial(jnp.dot, preferred_element_type=jnp.float32)
    return dot(left_high, right_high) + (dot(left_high, right_low) + dot(left_low, right_high))


def diagonal(size):
    rows = lax.broadcasted_iota(jnp.int32, (size, size), 0)
    return rows == lax.broadcasted_iota(jnp.int32, (size, size), 1)


def as_column(row, eye):
    return jnp.sum(jnp.where(eye, row, 0.0), axis=1, keepdims=True)


def as_row(column, eye):
    return jnp.sum(jnp.where(eye, column, 0.0), axis=0, keepdims=True)


def row_times(row, matrix, eye):
    column = as_column(row, eye) / jnp.sum(row, axis=1, keepdims=True)
    return jnp.sum(column * matrix, axis=0, keepdims=True)


def times_row(matrix, row, eye):
    column = jnp.sum(matrix * row, axis=1, keepdims=True)
    return as_row(column, eye) / jnp.sum(column, axis=0, keepdims=True)


def read_kernel(order_hbm, potential_hbm, order_ref, kernel_ref, half_ref, copied_ref, semaphores):
    core, _, _ = place()
    copies = (
        pltpu.make_async_copy(order_hbm, order_ref, semaphores.at[0]),
        pltpu.make_async_copy(potential_hbm, copied_ref, semaphores.at[1]),
    )
    for copy in copies:
        copy.start()
    for copy in copies:
        copy.wait()
    half = half_ref.shape[0]
    kernel_ref[...] = jnp.exp(copied_ref[...] - shift)
    half_ref[...] = kernel_ref[pl.ds(core * half, half), :]


def put_others(stack_ref, mine, near, near_sibling, far, far_sibling, core):
    half = far.shape[0]
    across = mine ^ 2
    stack_ref[mine ^ (1 + 2 * core)] = near[...]
    stack_ref[mine ^ (3 - 2 * core)] = near_sibling[...]
    stack_ref[across, pl.ds(core * half, half), :] = far[...]
    stack_ref[across, pl.ds((1 - core) * half, half), :] = far_sibling[...]


def quad_kernel(kernel_ref, near, near_sibling, far, far_sibling, quad_ref, product_ref, half_ref):
    core, _, z = place()
    mine = lax.rem(z, QUAD)
    half, size = half_ref.shape
    quad_ref[mine] = kernel_ref[...]
    put_others(quad_ref, mine, near, near_sibling, far, far_sibling, core)
    scale = 1.0 / size
    left = product(quad_ref[0], quad_ref[1]) * scale
    right = product(quad_ref[2], quad_ref[3]) * scale
    whole = product(left, right) * scale
    largest = jnp.max(jnp.max(whole, axis=0, keepdims=True), axis=1, keepdims=True)
    product_ref[...] = whole / largest
    half_ref[...] = product_ref[pl.ds(core * half, half), :]


def spots():
    core, y, z = place()
    return (core, y, 2 * lax.rem(y, 2) + lax.div(z, QUAD), lax.rem(z, QUAD))


def block_kernel(product_ref, near, near_sibling, far, far_sibling, block_ref, message_ref):
    core, y, mine, _ = spots()
    size, half = (product_ref.shape[0], far.shape[0])
    block_ref[mine] = product_ref[...]
    block_ref[mine ^ (1 + core)] = near[...]
    block_ref[mine ^ (2 - core)] = near_sibling[...]
    block_ref[mine ^ 3, pl.ds(core * half, half), :] = far[...]
    block_ref[mine ^ 3, pl.ds((1 - core) * half, half), :] = far_sibling[...]
    eye = diagonal(size)
    ones = jnp.ones((1, size), jnp.float32)

    @pl.when(y < Y // 2)
    def _():
        row = ones
        for position in range(4):
            row = row_times(row, block_ref[position], eye)
        message_ref[...] = jnp.broadcast_to(row, message_ref.shape)

    @pl.when(y >= Y // 2)
    def _():
        row = ones
        for position in range(4):
            row = times_row(block_ref[3 - position], row, eye)
        message_ref[...] = jnp.broadcast_to(row, message_ref.shape)


def unit_product(left, right):
    moved = product(left, right)
    return moved / jnp.max(jnp.max(moved, axis=0, keepdims=True), axis=1, keepdims=True)


def sides_kernel(quad_ref, block_ref, path_ref, known_ref):
    _, y, in_block, mine = spots()
    size = path_ref.shape[0]
    eye = diagonal(size)
    ones = jnp.ones((1, size), jnp.float32)
    start = jnp.where(eye, 1.0, 0.0)

    @pl.when(y >= Y // 2)
    def _():
        path = lax.fori_loop(0, in_block, lambda i, m: unit_product(m, block_ref[i]), start)
        path_ref[...] = lax.fori_loop(0, mine, lambda i, m: unit_product(m, quad_ref[i]), path)
        row = lax.fori_loop(
            0, 3 - in_block, lambda i, row: times_row(block_ref[3 - i], row, eye), ones
        )
        row = lax.fori_loop(
            0, QUAD - 1 - mine, lambda i, row: times_row(quad_ref[QUAD - 1 - i], row, eye), row
        )
        known_ref[...] = jnp.broadcast_to(row, known_ref.shape)

    @pl.when(y < Y // 2)
    def _():
        path = lax.fori_loop(
            0, 3 - in_block, lambda i, m: unit_product(block_ref[3 - i], m), start
        )
        path_ref[...] = lax.fori_loop(
            0, QUAD - 1 - mine, lambda i, m: unit_product(quad_ref[QUAD - 1 - i], m), path
        )
        row = lax.fori_loop(0, in_block, lambda i, row: row_times(row, block_ref[i], eye), ones)
        row = lax.fori_loop(0, mine, lambda i, row: row_times(row, quad_ref[i], eye), row)
        known_ref[...] = jnp.broadcast_to(row, known_ref.shape)


def chip_kernel(own_ref, sibling_ref, both_ref, half_ref):
    core, _, _ = place()
    half = half_ref.shape[0]
    both_ref[...] = own_ref[...] + sibling_ref[...]
    half_ref[...] = both_ref[pl.ds(core * half, half), :]


def join_kernel(near_ref, far_ref, sum_ref):
    core, _, _ = place()
    half = far_ref.shape[0]
    sum_ref[...] = near_ref[...]
    sum_ref[pl.ds(core * half, half), :] += far_ref[...]


def final_kernel(
    scale, potential_ref, noise_ref, kernel_ref, path_ref, known_ref, message_ref, chip_ref,
    join_ref, sibling_join_ref, updated_ref, beliefs_ref, column_ref, row_ref
):
    _, y, _, _ = spots()
    size = potential_ref.shape[0]
    eye = diagonal(size)
    known, message = (known_ref[0:1, :], message_ref[0:1, :])

    @pl.when(y >= Y // 2)
    def _():
        forward = row_times(message, path_ref[...], eye)
        column_ref[...] = as_column(forward, eye) / jnp.sum(forward, axis=1, keepdims=True)
        row_ref[...] = known

    @pl.when(y < Y // 2)
    def _():
        column_ref[...] = as_column(known, eye) / jnp.sum(known, axis=1, keepdims=True)
        row_ref[...] = times_row(path_ref[...], message, eye)

    joint = column_ref[...] * kernel_ref[...] * row_ref[...]
    total = jnp.sum(jnp.sum(joint, axis=0, keepdims=True), axis=1, keepdims=True)
    beliefs = joint * (size * size / total)
    beliefs_ref[...] = beliefs
    counts = chip_ref[...] + join_ref[...] + sibling_join_ref[...]
    measured = (counts + noise_ref[...]) * scale
    updated_ref[...] = potential_ref[...] - step_size * (beliefs - measured)


def count_kernel(part, order_ref, left_ref, right_ref, total_ref):
    _, y, z = place()
    clique = y * Z + z
    size = total_ref.shape[0]

    @pl.when(pl.program_id(0) == 0)
    def _():
        total_ref[...] = jnp.zeros_like(total_ref)

    levels = lax.broadcasted_iota(jnp.int32, (size, part), 0).astype(jnp.bfloat16)
    one = jnp.ones((size, part), jnp.bfloat16)
    zero = jnp.zeros((size, part), jnp.bfloat16)

    def onehot(ref, attribute, begin):
        values = ref[pl.ds(lax.rem(attribute, 8), 1), begin : begin + part]
        values = values.astype(jnp.float32).astype(jnp.bfloat16)
        return jnp.where(values == levels, one, zero).astype(jnp.float8_e4m3fn)

    total = total_ref[...]
    for begin in range(0, left_ref.shape[1], part):
        total = total + lax.dot_general(
            onehot(left_ref, order_ref[clique], begin),
            onehot(right_ref, order_ref[clique + 1], begin),
            (((1,), (1,)), ((), ())),
            preferred_element_type=jnp.float32,
        )
    total_ref[...] = total


def shape(*dims):
    return jax.ShapeDtypeStruct(dims, jnp.float32)


PARAMS = pltpu.CompilerParams(vmem_limit_bytes=VMEM_LIMIT)


def count_pairs(order, table_rows, size):
    window, part = 16384, 8192

    def rows_of(offset):
        def block(step, order_ref):
            return (lax.div(order_ref[lax.axis_index("clique") + offset], 8), step)

        return pl.BlockSpec((8, window), block)

    return pl.pallas_call(
        functools.partial(count_kernel, part),
        out_shape=shape(size, size),
        grid_spec=pltpu.PrefetchScalarGridSpec(
            num_scalar_prefetch=1,
            grid=(table_rows.shape[1] // window,),
            in_specs=[rows_of(0), rows_of(1)],
            out_specs=pl.BlockSpec((size, size), lambda step, order_ref: (0, 0)),
        ),
        compiler_params=PARAMS,
        name="counts",
    )(order, table_rows, table_rows)


def everywhere(move):
    pairs = []
    for x in range(4):
        for c in range(2):
            for y in range(Y):
                for z in range(Z):
                    to_x, to_y, to_z = move(x, c, y, z)
                    source = (2 * x + c) * Y * Z + y * Z + z
                    pairs.append((source, (2 * to_x + c) * Y * Z + to_y * Z + to_z))
    return pairs


def exchange(whole, half, near_step, far_step):
    axes = ("dp", "clique")
    return (
        lax.ppermute(whole, axes, everywhere(near_step)),
        lax.ppermute(half, axes, everywhere(lambda x, c, y, z: far_step(x, y, z))),
    )


def per_device(table_rows, attribute_order, log_potential, measure_noise):
    size = log_potential.shape[1]
    potential = log_potential[0]
    call = functools.partial(pl.pallas_call, compiler_params=PARAMS)
    vmem = pl.BlockSpec(memory_space=pltpu.VMEM)
    hbm = pl.BlockSpec(memory_space=pltpu.HBM)
    whole, half = (shape(size, size), shape(size // 2, size))
    order, kernel, half_of_kernel = call(
        read_kernel,
        in_specs=[hbm, hbm],
        out_specs=(vmem, vmem, vmem),
        out_shape=(jax.ShapeDtypeStruct(attribute_order.shape, jnp.int32), whole, half),
        scratch_shapes=[pltpu.VMEM((size, size), jnp.float32), pltpu.SemaphoreType.DMA((2,))],
        name="read",
    )(
        pltpu.with_memory_space_constraint(attribute_order, pltpu.HBM),
        pltpu.with_memory_space_constraint(potential, pltpu.HBM),
    )
    near, far = exchange(
        kernel,
        half_of_kernel,
        lambda x, c, y, z: (x, y, z ^ (1 + 2 * c)),
        lambda x, y, z: (x, y, z ^ 2),
    )
    counts = count_pairs(order, table_rows, size)
    near, far, counts = lax.optimization_barrier((near, far, counts))
    quad, quad_product, half_product = call(
        quad_kernel, out_shape=(shape(QUAD, size, size), whole, half), name="quad"
    )(kernel, near, other_core(near), far, other_core(far))
    near, far = exchange(
        quad_product,
        half_product,
        lambda x, c, y, z: (x, y ^ 1, z) if c else (x, y, z ^ 6),
        lambda x, y, z: (x, y ^ 1, z ^ 6),
    )
    counts, quad = lax.optimization_barrier((counts, quad))
    chip_counts, half_counts = call(chip_kernel, out_shape=(whole, half), name="chip")(
        counts, other_core(counts)
    )
    near_counts, far_counts = exchange(
        chip_counts,
        half_counts,
        lambda x, c, y, z: (x ^ (1 + 2 * c), y, z),
        lambda x, y, z: (x ^ 2, y, z),
    )
    near, far, far_counts = lax.optimization_barrier((near, far, far_counts))
    near_sibling, far_sibling = (other_core(near), other_core(far))
    near_sibling, far_sibling, near_counts = lax.optimization_barrier(
        (near_sibling, far_sibling, near_counts)
    )
    block, message = call(
        block_kernel, out_shape=(shape(4, size, size), shape(8, size)), name="block"
    )(quad_product, near, near_sibling, far, far_sibling)
    joined = call(join_kernel, out_shape=whole, name="join")(near_counts, far_counts)
    arrived = lax.ppermute(message, "clique", along_clique(lambda y, z: (y ^ 2, z)))
    path, known = call(sides_kernel, out_shape=(whole, shape(8, size)), name="sides")(quad, block)
    total_rows = table_rows.shape[1] * lax.axis_size("dp")
    updated, beliefs = call(
        functools.partial(final_kernel, size * size / total_rows),
        out_shape=(whole, whole),
        scratch_shapes=[
            pltpu.VMEM((size, 1), jnp.float32),
            pltpu.VMEM((1, size), jnp.float32),
        ],
        name="final",
    )(
        potential, measure_noise[0], kernel, path, known, arrived, chip_counts, joined,
        other_core(joined),
    )
    return (updated[None], beliefs[None])


def solution(mesh):
    in_specs = (P(None, "dp"), P(), P("clique", None, None), P("clique", None, None))
    out_specs = (P("clique", None, None), P("clique", None, None))
    return jax.shard_map(
        per_device, mesh=mesh, in_specs=in_specs, out_specs=out_specs, check_vma=False
    )
```

```python
import functools

import jax
import jax.numpy as jnp
from jax import lax
from jax.experimental import pallas as pl
from jax.experimental.pallas import tpu as pltpu
from jax.sharding import PartitionSpec as P

step_size = 0.25
shift = 7.0
Y, Z, QUAD = 4, 8, 4
VMEM_LIMIT = 50 << 20


def place():
    dp, clique = (lax.axis_index("dp"), lax.axis_index("clique"))
    return (lax.rem(dp, 2), lax.div(clique, Z), lax.rem(clique, Z))


def along_clique(where):
    return [(y * Z + z, where(y, z)[0] * Z + where(y, z)[1]) for y in range(Y) for z in range(Z)]


def along_dp(where):
    return [(2 * x + c, 2 * where(x, c)[0] + where(x, c)[1]) for x in range(4) for c in range(2)]


def other_core(value):
    return lax.ppermute(value, "dp", along_dp(lambda x, c: (x, 1 - c)))


def in_quad(z, step):
    return z // QUAD * QUAD + (z + step) % QUAD


def split(value):
    high = value.astype(jnp.bfloat16)
    low = (value - high.astype(jnp.float32)).astype(jnp.bfloat16)
    return (high, low)


def product(left, right):
    left_high, left_low = split(left)
    right_high, right_low = split(right)
    dot = functools.partial(jnp.dot, preferred_element_type=jnp.float32)
    return dot(left_high, right_high) + (dot(left_high, right_low) + dot(left_low, right_high))


def diagonal(size):
    rows = lax.broadcasted_iota(jnp.int32, (size, size), 0)
    return rows == lax.broadcasted_iota(jnp.int32, (size, size), 1)


def as_column(row, eye):
    return jnp.sum(jnp.where(eye, row, 0.0), axis=1, keepdims=True)


def as_row(column, eye):
    return jnp.sum(jnp.where(eye, column, 0.0), axis=0, keepdims=True)


def row_times(row, matrix, eye):
    column = as_column(row, eye) / jnp.sum(row, axis=1, keepdims=True)
    return jnp.sum(column * matrix, axis=0, keepdims=True)


def times_row(matrix, row, eye):
    column = jnp.sum(matrix * row, axis=1, keepdims=True)
    return as_row(column, eye) / jnp.sum(column, axis=0, keepdims=True)


def read_kernel(order_hbm, potential_hbm, order_ref, kernel_ref, half_ref, copied_ref, semaphores):
    core, _, _ = place()
    copies = (
        pltpu.make_async_copy(order_hbm, order_ref, semaphores.at[0]),
        pltpu.make_async_copy(potential_hbm, copied_ref, semaphores.at[1]),
    )
    for copy in copies:
        copy.start()
    for copy in copies:
        copy.wait()
    half = half_ref.shape[0]
    kernel_ref[...] = jnp.exp(copied_ref[...] - shift)
    half_ref[...] = kernel_ref[pl.ds(core * half, half), :]


def put_others(stack_ref, mine, near, near_sibling, far, far_sibling, core):
    half = far.shape[0]
    across = mine ^ 2
    stack_ref[mine ^ (1 + 2 * core)] = near[...]
    stack_ref[mine ^ (3 - 2 * core)] = near_sibling[...]
    stack_ref[across, pl.ds(core * half, half), :] = far[...]
    stack_ref[across, pl.ds((1 - core) * half, half), :] = far_sibling[...]


def quad_kernel(kernel_ref, near, near_sibling, far, far_sibling, quad_ref, product_ref):
    core, _, z = place()
    mine = lax.rem(z, QUAD)
    size = product_ref.shape[0]
    quad_ref[mine] = kernel_ref[...]
    put_others(quad_ref, mine, near, near_sibling, far, far_sibling, core)
    scale = 1.0 / size
    left = product(quad_ref[0], quad_ref[1]) * scale
    right = product(quad_ref[2], quad_ref[3]) * scale
    whole = product(left, right) * scale
    largest = jnp.max(jnp.max(whole, axis=0, keepdims=True), axis=1, keepdims=True)
    product_ref[...] = whole / largest


def spots():
    core, y, z = place()
    return (core, y, 2 * lax.rem(y, 2) + lax.div(z, QUAD), lax.rem(z, QUAD))


def block_kernel(product_ref, near, near_sibling, far, far_sibling, block_ref, message_ref):
    core, y, mine, _ = spots()
    size, half = (product_ref.shape[0], far.shape[0])
    block_ref[mine] = product_ref[...]
    block_ref[mine ^ (1 + core)] = near[...]
    block_ref[mine ^ (2 - core)] = near_sibling[...]
    block_ref[mine ^ 3, pl.ds(core * half, half), :] = far[...]
    block_ref[mine ^ 3, pl.ds((1 - core) * half, half), :] = far_sibling[...]
    eye = diagonal(size)
    ones = jnp.ones((1, size), jnp.float32)

    @pl.when(y < Y // 2)
    def _():
        row = ones
        for position in range(4):
            row = row_times(row, block_ref[position], eye)
        message_ref[...] = jnp.broadcast_to(row, message_ref.shape)

    @pl.when(y >= Y // 2)
    def _():
        row = ones
        for position in range(4):
            row = times_row(block_ref[3 - position], row, eye)
        message_ref[...] = jnp.broadcast_to(row, message_ref.shape)


def unit_product(left, right):
    moved = product(left, right)
    return moved / jnp.max(jnp.max(moved, axis=0, keepdims=True), axis=1, keepdims=True)


def sides_kernel(quad_ref, block_ref, path_ref, known_ref):
    _, y, in_block, mine = spots()
    size = path_ref.shape[0]
    eye = diagonal(size)
    ones = jnp.ones((1, size), jnp.float32)
    start = jnp.where(eye, 1.0, 0.0)

    @pl.when(y >= Y // 2)
    def _():
        path = lax.fori_loop(0, in_block, lambda i, m: unit_product(m, block_ref[i]), start)
        path_ref[...] = lax.fori_loop(0, mine, lambda i, m: unit_product(m, quad_ref[i]), path)
        row = lax.fori_loop(
            0, 3 - in_block, lambda i, row: times_row(block_ref[3 - i], row, eye), ones
        )
        row = lax.fori_loop(
            0, QUAD - 1 - mine, lambda i, row: times_row(quad_ref[QUAD - 1 - i], row, eye), row
        )
        known_ref[...] = jnp.broadcast_to(row, known_ref.shape)

    @pl.when(y < Y // 2)
    def _():
        path = lax.fori_loop(
            0, 3 - in_block, lambda i, m: unit_product(block_ref[3 - i], m), start
        )
        path_ref[...] = lax.fori_loop(
            0, QUAD - 1 - mine, lambda i, m: unit_product(quad_ref[QUAD - 1 - i], m), path
        )
        row = lax.fori_loop(0, in_block, lambda i, row: row_times(row, block_ref[i], eye), ones)
        row = lax.fori_loop(0, mine, lambda i, row: row_times(row, quad_ref[i], eye), row)
        known_ref[...] = jnp.broadcast_to(row, known_ref.shape)


def relay_kernel(whole_ref, half_ref):
    core, _, _ = place()
    half = half_ref.shape[0]
    half_ref[...] = whole_ref[pl.ds(core * half, half), :]


def chip_kernel(own_ref, sibling_ref, both_ref, half_ref):
    core, _, _ = place()
    half = half_ref.shape[0]
    both_ref[...] = own_ref[...] + sibling_ref[...]
    half_ref[...] = both_ref[pl.ds(core * half, half), :]


def join_kernel(near_ref, far_ref, sum_ref):
    core, _, _ = place()
    half = far_ref.shape[0]
    sum_ref[...] = near_ref[...]
    sum_ref[pl.ds(core * half, half), :] += far_ref[...]


def final_kernel(
    scale, potential_ref, noise_ref, kernel_ref, path_ref, known_ref, message_ref, chip_ref,
    join_ref, sibling_join_ref, updated_ref, beliefs_ref, column_ref, row_ref
):
    _, y, _, _ = spots()
    size = potential_ref.shape[0]
    eye = diagonal(size)
    known, message = (known_ref[0:1, :], message_ref[0:1, :])

    @pl.when(y >= Y // 2)
    def _():
        forward = row_times(message, path_ref[...], eye)
        column_ref[...] = as_column(forward, eye) / jnp.sum(forward, axis=1, keepdims=True)
        row_ref[...] = known

    @pl.when(y < Y // 2)
    def _():
        column_ref[...] = as_column(known, eye) / jnp.sum(known, axis=1, keepdims=True)
        row_ref[...] = times_row(path_ref[...], message, eye)

    joint = column_ref[...] * kernel_ref[...] * row_ref[...]
    total = jnp.sum(jnp.sum(joint, axis=0, keepdims=True), axis=1, keepdims=True)
    beliefs = joint * (size * size / total)
    beliefs_ref[...] = beliefs
    counts = chip_ref[...] + join_ref[...] + sibling_join_ref[...]
    measured = (counts + noise_ref[...]) * scale
    updated_ref[...] = potential_ref[...] - step_size * (beliefs - measured)


def count_kernel(part, order_ref, left_ref, right_ref, total_ref):
    _, y, z = place()
    clique = y * Z + z
    size = total_ref.shape[0]

    @pl.when(pl.program_id(0) == 0)
    def _():
        total_ref[...] = jnp.zeros_like(total_ref)

    levels = lax.broadcasted_iota(jnp.int32, (size, part), 0).astype(jnp.bfloat16)
    one = jnp.ones((size, part), jnp.bfloat16)
    zero = jnp.zeros((size, part), jnp.bfloat16)

    def onehot(ref, attribute, begin):
        values = ref[pl.ds(lax.rem(attribute, 8), 1), begin : begin + part]
        values = values.astype(jnp.float32).astype(jnp.bfloat16)
        return jnp.where(values == levels, one, zero).astype(jnp.float8_e4m3fn)

    total = total_ref[...]
    for begin in range(0, left_ref.shape[1], part):
        total = total + lax.dot_general(
            onehot(left_ref, order_ref[clique], begin),
            onehot(right_ref, order_ref[clique + 1], begin),
            (((1,), (1,)), ((), ())),
            preferred_element_type=jnp.float32,
        )
    total_ref[...] = total


def shape(*dims):
    return jax.ShapeDtypeStruct(dims, jnp.float32)


PARAMS = pltpu.CompilerParams(vmem_limit_bytes=VMEM_LIMIT)


def count_pairs(order, table_rows, size):
    window, part = 16384, 8192

    def rows_of(offset):
        def block(step, order_ref):
            return (lax.div(order_ref[lax.axis_index("clique") + offset], 8), step)

        return pl.BlockSpec((8, window), block)

    return pl.pallas_call(
        functools.partial(count_kernel, part),
        out_shape=shape(size, size),
        grid_spec=pltpu.PrefetchScalarGridSpec(
            num_scalar_prefetch=1,
            grid=(table_rows.shape[1] // window,),
            in_specs=[rows_of(0), rows_of(1)],
            out_specs=pl.BlockSpec((size, size), lambda step, order_ref: (0, 0)),
        ),
        compiler_params=PARAMS,
        name="counts",
    )(order, table_rows, table_rows)


def everywhere(move):
    pairs = []
    for x in range(4):
        for c in range(2):
            for y in range(Y):
                for z in range(Z):
                    to_x, to_y, to_z = move(x, c, y, z)
                    source = (2 * x + c) * Y * Z + y * Z + z
                    pairs.append((source, (2 * to_x + c) * Y * Z + to_y * Z + to_z))
    return pairs


def exchange(whole, half, near_step, far_step):
    axes = ("dp", "clique")
    return (
        lax.ppermute(whole, axes, everywhere(near_step)),
        lax.ppermute(half, axes, everywhere(lambda x, c, y, z: far_step(x, y, z))),
    )


def per_device(table_rows, attribute_order, log_potential, measure_noise):
    size = log_potential.shape[1]
    potential = log_potential[0]
    call = functools.partial(pl.pallas_call, compiler_params=PARAMS)
    vmem = pl.BlockSpec(memory_space=pltpu.VMEM)
    hbm = pl.BlockSpec(memory_space=pltpu.HBM)
    whole, half = (shape(size, size), shape(size // 2, size))
    order, kernel, half_of_kernel = call(
        read_kernel,
        in_specs=[hbm, hbm],
        out_specs=(vmem, vmem, vmem),
        out_shape=(jax.ShapeDtypeStruct(attribute_order.shape, jnp.int32), whole, half),
        scratch_shapes=[pltpu.VMEM((size, size), jnp.float32), pltpu.SemaphoreType.DMA((2,))],
        name="read",
    )(
        pltpu.with_memory_space_constraint(attribute_order, pltpu.HBM),
        pltpu.with_memory_space_constraint(potential, pltpu.HBM),
    )
    near, far = exchange(
        kernel,
        half_of_kernel,
        lambda x, c, y, z: (x, y, z ^ (1 + 2 * c)),
        lambda x, y, z: (x, y, z ^ 2),
    )
    counts = count_pairs(order, table_rows, size)
    near, far, counts = lax.optimization_barrier((near, far, counts))
    quad, quad_product = call(
        quad_kernel, out_shape=(shape(QUAD, size, size), whole), name="quad"
    )(kernel, near, other_core(near), far, other_core(far))
    axes = ("dp", "clique")
    near = lax.ppermute(
        quad_product,
        axes,
        everywhere(lambda x, c, y, z: (x, y ^ 1, z) if c else (x, y, z ^ 6)),
    )
    counts, quad = lax.optimization_barrier((counts, quad))
    chip_counts, half_counts = call(chip_kernel, out_shape=(whole, half), name="chip")(
        counts, other_core(counts)
    )
    near_counts, far_counts = exchange(
        chip_counts,
        half_counts,
        lambda x, c, y, z: (x ^ (1 + 2 * c), y, z),
        lambda x, y, z: (x ^ 2, y, z),
    )
    near, far_counts = lax.optimization_barrier((near, far_counts))
    half_near = call(relay_kernel, out_shape=half, name="relay")(near)
    far = lax.ppermute(
        half_near,
        axes,
        everywhere(lambda x, c, y, z: (x, y, z ^ 6) if c else (x, y ^ 1, z)),
    )
    near_sibling = other_core(near)
    far, near_sibling, near_counts = lax.optimization_barrier((far, near_sibling, near_counts))
    far_sibling = other_core(far)
    block, message = call(
        block_kernel, out_shape=(shape(4, size, size), shape(8, size)), name="block"
    )(quad_product, near, near_sibling, far, far_sibling)
    joined = call(join_kernel, out_shape=whole, name="join")(near_counts, far_counts)
    arrived = lax.ppermute(message, "clique", along_clique(lambda y, z: (y ^ 2, z)))
    path, known = call(sides_kernel, out_shape=(whole, shape(8, size)), name="sides")(quad, block)
    total_rows = table_rows.shape[1] * lax.axis_size("dp")
    updated, beliefs = call(
        functools.partial(final_kernel, size * size / total_rows),
        out_shape=(whole, whole),
        scratch_shapes=[
            pltpu.VMEM((size, 1), jnp.float32),
            pltpu.VMEM((1, size), jnp.float32),
        ],
        name="final",
    )(
        potential, measure_noise[0], kernel, path, known, arrived, chip_counts, joined,
        other_core(joined),
    )
    return (updated[None], beliefs[None])


def solution(mesh):
    in_specs = (P(None, "dp"), P(), P("clique", None, None), P("clique", None, None))
    out_specs = (P("clique", None, None), P("clique", None, None))
    return jax.shard_map(
        per_device, mesh=mesh, in_specs=in_specs, out_specs=out_specs, check_vma=False
    )
```

```python
import functools

import jax
import jax.numpy as jnp
from jax import lax
from jax.experimental import pallas as pl
from jax.experimental.pallas import tpu as pltpu
from jax.sharding import PartitionSpec as P

step_size = 0.25
shift = 7.0
Y, Z, QUAD = 4, 8, 4
VMEM_LIMIT = 50 << 20


def place():
    dp, clique = (lax.axis_index("dp"), lax.axis_index("clique"))
    return (lax.rem(dp, 2), lax.div(clique, Z), lax.rem(clique, Z))


def along_clique(where):
    return [(y * Z + z, where(y, z)[0] * Z + where(y, z)[1]) for y in range(Y) for z in range(Z)]


def along_dp(where):
    return [(2 * x + c, 2 * where(x, c)[0] + where(x, c)[1]) for x in range(4) for c in range(2)]


def other_core(value):
    return lax.ppermute(value, "dp", along_dp(lambda x, c: (x, 1 - c)))


def in_quad(z, step):
    return z // QUAD * QUAD + (z + step) % QUAD


def split(value):
    high = value.astype(jnp.bfloat16)
    low = (value - high.astype(jnp.float32)).astype(jnp.bfloat16)
    return (high, low)


def product(left, right):
    left_high, left_low = split(left)
    right_high, right_low = split(right)
    dot = functools.partial(jnp.dot, preferred_element_type=jnp.float32)
    return dot(left_high, right_high) + (dot(left_high, right_low) + dot(left_low, right_high))


def diagonal(size):
    rows = lax.broadcasted_iota(jnp.int32, (size, size), 0)
    return rows == lax.broadcasted_iota(jnp.int32, (size, size), 1)


def as_column(row, eye):
    return jnp.sum(jnp.where(eye, row, 0.0), axis=1, keepdims=True)


def as_row(column, eye):
    return jnp.sum(jnp.where(eye, column, 0.0), axis=0, keepdims=True)


def row_times(row, matrix, eye):
    column = as_column(row, eye) / jnp.sum(row, axis=1, keepdims=True)
    return jnp.sum(column * matrix, axis=0, keepdims=True)


def times_row(matrix, row, eye):
    column = jnp.sum(matrix * row, axis=1, keepdims=True)
    return as_row(column, eye) / jnp.sum(column, axis=0, keepdims=True)


def read_kernel(order_hbm, potential_hbm, order_ref, kernel_ref, half_ref, copied_ref, semaphores):
    core, _, _ = place()
    copies = (
        pltpu.make_async_copy(order_hbm, order_ref, semaphores.at[0]),
        pltpu.make_async_copy(potential_hbm, copied_ref, semaphores.at[1]),
    )
    for copy in copies:
        copy.start()
    for copy in copies:
        copy.wait()
    half = half_ref.shape[0]
    kernel_ref[...] = jnp.exp(copied_ref[...] - shift)
    half_ref[...] = kernel_ref[pl.ds(core * half, half), :]


def put_others(stack_ref, mine, near, near_sibling, far, far_sibling, core):
    half = far.shape[0]
    across = mine ^ 2
    stack_ref[mine ^ (1 + 2 * core)] = near[...]
    stack_ref[mine ^ (3 - 2 * core)] = near_sibling[...]
    stack_ref[across, pl.ds(core * half, half), :] = far[...]
    stack_ref[across, pl.ds((1 - core) * half, half), :] = far_sibling[...]


def quad_kernel(kernel_ref, near, near_sibling, far, far_sibling, quad_ref, product_ref):
    core, _, z = place()
    mine = lax.rem(z, QUAD)
    size = product_ref.shape[0]
    quad_ref[mine] = kernel_ref[...]
    put_others(quad_ref, mine, near, near_sibling, far, far_sibling, core)
    scale = 1.0 / size
    left = product(quad_ref[0], quad_ref[1]) * scale
    right = product(quad_ref[2], quad_ref[3]) * scale
    whole = product(left, right) * scale
    largest = jnp.max(jnp.max(whole, axis=0, keepdims=True), axis=1, keepdims=True)
    product_ref[...] = whole / largest


def spots():
    core, y, z = place()
    return (core, y, 2 * lax.rem(y, 2) + lax.div(z, QUAD), lax.rem(z, QUAD))


def block_kernel(product_ref, near, near_sibling, far, far_sibling, block_ref, message_ref):
    core, y, mine, _ = spots()
    size, half = (product_ref.shape[0], far.shape[0])
    block_ref[mine] = product_ref[...]
    block_ref[mine ^ (1 + core)] = near[...]
    block_ref[mine ^ (2 - core)] = near_sibling[...]
    block_ref[mine ^ 3, pl.ds(core * half, half), :] = far[...]
    block_ref[mine ^ 3, pl.ds((1 - core) * half, half), :] = far_sibling[...]
    eye = diagonal(size)
    ones = jnp.ones((1, size), jnp.float32)

    @pl.when(y < Y // 2)
    def _():
        row = ones
        for position in range(4):
            row = row_times(row, block_ref[position], eye)
        message_ref[...] = jnp.broadcast_to(row, message_ref.shape)

    @pl.when(y >= Y // 2)
    def _():
        row = ones
        for position in range(4):
            row = times_row(block_ref[3 - position], row, eye)
        message_ref[...] = jnp.broadcast_to(row, message_ref.shape)


def unit_product(left, right):
    moved = product(left, right)
    return moved / jnp.max(jnp.max(moved, axis=0, keepdims=True), axis=1, keepdims=True)


def sides_kernel(quad_ref, block_ref, path_ref, known_ref):
    _, y, in_block, mine = spots()
    size = path_ref.shape[0]
    eye = diagonal(size)
    ones = jnp.ones((1, size), jnp.float32)
    start = jnp.where(eye, 1.0, 0.0)

    @pl.when(y >= Y // 2)
    def _():
        path = lax.fori_loop(0, in_block, lambda i, m: unit_product(m, block_ref[i]), start)
        path_ref[...] = lax.fori_loop(0, mine, lambda i, m: unit_product(m, quad_ref[i]), path)
        row = lax.fori_loop(
            0, 3 - in_block, lambda i, row: times_row(block_ref[3 - i], row, eye), ones
        )
        row = lax.fori_loop(
            0, QUAD - 1 - mine, lambda i, row: times_row(quad_ref[QUAD - 1 - i], row, eye), row
        )
        known_ref[...] = jnp.broadcast_to(row, known_ref.shape)

    @pl.when(y < Y // 2)
    def _():
        path = lax.fori_loop(
            0, 3 - in_block, lambda i, m: unit_product(block_ref[3 - i], m), start
        )
        path_ref[...] = lax.fori_loop(
            0, QUAD - 1 - mine, lambda i, m: unit_product(quad_ref[QUAD - 1 - i], m), path
        )
        row = lax.fori_loop(0, in_block, lambda i, row: row_times(row, block_ref[i], eye), ones)
        row = lax.fori_loop(0, mine, lambda i, row: row_times(row, quad_ref[i], eye), row)
        known_ref[...] = jnp.broadcast_to(row, known_ref.shape)


def relay_kernel(whole_ref, half_ref):
    core, _, _ = place()
    half = half_ref.shape[0]
    half_ref[...] = whole_ref[pl.ds(core * half, half), :]


def chip_kernel(own_ref, sibling_ref, both_ref, half_ref):
    core, _, _ = place()
    half = half_ref.shape[0]
    both_ref[...] = own_ref[...] + sibling_ref[...]
    half_ref[...] = both_ref[pl.ds(core * half, half), :]


def join_kernel(near_ref, far_ref, sum_ref):
    core, _, _ = place()
    half = far_ref.shape[0]
    sum_ref[...] = near_ref[...]
    sum_ref[pl.ds(core * half, half), :] += far_ref[...]


def final_kernel(
    scale, potential_ref, noise_ref, kernel_ref, path_ref, known_ref, message_ref, chip_ref,
    join_ref, sibling_join_ref, updated_ref, beliefs_ref, column_ref, row_ref
):
    _, y, _, _ = spots()
    size = potential_ref.shape[0]
    eye = diagonal(size)
    known, message = (known_ref[0:1, :], message_ref[0:1, :])

    @pl.when(y >= Y // 2)
    def _():
        forward = row_times(message, path_ref[...], eye)
        column_ref[...] = as_column(forward, eye) / jnp.sum(forward, axis=1, keepdims=True)
        row_ref[...] = known

    @pl.when(y < Y // 2)
    def _():
        column_ref[...] = as_column(known, eye) / jnp.sum(known, axis=1, keepdims=True)
        row_ref[...] = times_row(path_ref[...], message, eye)

    joint = column_ref[...] * kernel_ref[...] * row_ref[...]
    total = jnp.sum(jnp.sum(joint, axis=0, keepdims=True), axis=1, keepdims=True)
    beliefs = joint * (size * size / total)
    beliefs_ref[...] = beliefs
    counts = chip_ref[...] + join_ref[...] + sibling_join_ref[...]
    measured = (counts + noise_ref[...]) * scale
    updated_ref[...] = potential_ref[...] - step_size * (beliefs - measured)


def count_kernel(part, order_ref, left_ref, right_ref, total_ref):
    _, y, z = place()
    clique = y * Z + z
    size = total_ref.shape[0]

    @pl.when(pl.program_id(0) == 0)
    def _():
        total_ref[...] = jnp.zeros_like(total_ref)

    levels = lax.broadcasted_iota(jnp.int32, (size, part), 0).astype(jnp.bfloat16)
    one = jnp.ones((size, part), jnp.bfloat16)
    zero = jnp.zeros((size, part), jnp.bfloat16)

    def onehot(ref, attribute, begin):
        values = ref[pl.ds(lax.rem(attribute, 8), 1), begin : begin + part]
        values = values.astype(jnp.float32).astype(jnp.bfloat16)
        return jnp.where(values == levels, one, zero).astype(jnp.float8_e4m3fn)

    total = total_ref[...]
    for begin in range(0, left_ref.shape[1], part):
        total = total + lax.dot_general(
            onehot(left_ref, order_ref[clique], begin),
            onehot(right_ref, order_ref[clique + 1], begin),
            (((1,), (1,)), ((), ())),
            preferred_element_type=jnp.float32,
        )
    total_ref[...] = total


def shape(*dims):
    return jax.ShapeDtypeStruct(dims, jnp.float32)


PARAMS = pltpu.CompilerParams(vmem_limit_bytes=VMEM_LIMIT)


def count_pairs(order, table_rows, size):
    window, part = 16384, 8192

    def rows_of(offset):
        def block(step, order_ref):
            return (lax.div(order_ref[lax.axis_index("clique") + offset], 8), step)

        return pl.BlockSpec((8, window), block)

    return pl.pallas_call(
        functools.partial(count_kernel, part),
        out_shape=shape(size, size),
        grid_spec=pltpu.PrefetchScalarGridSpec(
            num_scalar_prefetch=1,
            grid=(table_rows.shape[1] // window,),
            in_specs=[rows_of(0), rows_of(1)],
            out_specs=pl.BlockSpec((size, size), lambda step, order_ref: (0, 0)),
        ),
        compiler_params=PARAMS,
        name="counts",
    )(order, table_rows, table_rows)


def everywhere(move):
    pairs = []
    for x in range(4):
        for c in range(2):
            for y in range(Y):
                for z in range(Z):
                    to_x, to_y, to_z = move(x, c, y, z)
                    source = (2 * x + c) * Y * Z + y * Z + z
                    pairs.append((source, (2 * to_x + c) * Y * Z + to_y * Z + to_z))
    return pairs


def exchange(whole, half, near_step, far_step):
    axes = ("dp", "clique")
    return (
        lax.ppermute(whole, axes, everywhere(near_step)),
        lax.ppermute(half, axes, everywhere(lambda x, c, y, z: far_step(x, y, z))),
    )


def per_device(table_rows, attribute_order, log_potential, measure_noise):
    size = log_potential.shape[1]
    potential = log_potential[0]
    call = functools.partial(pl.pallas_call, compiler_params=PARAMS)
    vmem = pl.BlockSpec(memory_space=pltpu.VMEM)
    hbm = pl.BlockSpec(memory_space=pltpu.HBM)
    whole, half = (shape(size, size), shape(size // 2, size))
    order, kernel, half_of_kernel = call(
        read_kernel,
        in_specs=[hbm, hbm],
        out_specs=(vmem, vmem, vmem),
        out_shape=(jax.ShapeDtypeStruct(attribute_order.shape, jnp.int32), whole, half),
        scratch_shapes=[pltpu.VMEM((size, size), jnp.float32), pltpu.SemaphoreType.DMA((2,))],
        name="read",
    )(
        pltpu.with_memory_space_constraint(attribute_order, pltpu.HBM),
        pltpu.with_memory_space_constraint(potential, pltpu.HBM),
    )
    near, far = exchange(
        kernel,
        half_of_kernel,
        lambda x, c, y, z: (x, y, z ^ (1 + 2 * c)),
        lambda x, y, z: (x, y, z ^ 2),
    )
    counts = count_pairs(order, table_rows, size)
    near, far, counts = lax.optimization_barrier((near, far, counts))
    quad, quad_product = call(
        quad_kernel, out_shape=(shape(QUAD, size, size), whole), name="quad"
    )(kernel, near, other_core(near), far, other_core(far))
    axes = ("dp", "clique")
    near = lax.ppermute(
        quad_product,
        axes,
        everywhere(lambda x, c, y, z: (x, y ^ 1, z) if c else (x, y, z ^ 6)),
    )
    counts, quad = lax.optimization_barrier((counts, quad))
    chip_counts, half_counts = call(chip_kernel, out_shape=(whole, half), name="chip")(
        counts, other_core(counts)
    )
    near_counts, far_counts = exchange(
        chip_counts,
        half_counts,
        lambda x, c, y, z: (x ^ (1 + 2 * c), y, z),
        lambda x, y, z: (x ^ 2, y, z),
    )
    half_near = call(relay_kernel, out_shape=half, name="relay")(near)
    far = lax.ppermute(
        half_near,
        axes,
        everywhere(lambda x, c, y, z: (x, y, z ^ 6) if c else (x, y ^ 1, z)),
    )
    held, near_counts, far_counts = lax.optimization_barrier((near, near_counts, far_counts))
    near_sibling = other_core(held)
    far_sibling = other_core(far)
    block, message = call(
        block_kernel, out_shape=(shape(4, size, size), shape(8, size)), name="block"
    )(quad_product, near, near_sibling, far, far_sibling)
    joined = call(join_kernel, out_shape=whole, name="join")(near_counts, far_counts)
    arrived = lax.ppermute(message, "clique", along_clique(lambda y, z: (y ^ 2, z)))
    path, known = call(sides_kernel, out_shape=(whole, shape(8, size)), name="sides")(quad, block)
    total_rows = table_rows.shape[1] * lax.axis_size("dp")
    updated, beliefs = call(
        functools.partial(final_kernel, size * size / total_rows),
        out_shape=(whole, whole),
        scratch_shapes=[
            pltpu.VMEM((size, 1), jnp.float32),
            pltpu.VMEM((1, size), jnp.float32),
        ],
        name="final",
    )(
        potential, measure_noise[0], kernel, path, known, arrived, chip_counts, joined,
        other_core(joined),
    )
    return (updated[None], beliefs[None])


def solution(mesh):
    in_specs = (P(None, "dp"), P(), P("clique", None, None), P("clique", None, None))
    out_specs = (P("clique", None, None), P("clique", None, None))
    return jax.shard_map(
        per_device, mesh=mesh, in_specs=in_specs, out_specs=out_specs, check_vma=False
    )
```

```python
import functools

import jax
import jax.numpy as jnp
from jax import lax
from jax.experimental import pallas as pl
from jax.experimental.pallas import tpu as pltpu
from jax.sharding import PartitionSpec as P

step_size = 0.25
shift = 7.0
Y, Z, QUAD = 4, 8, 4
VMEM_LIMIT = 50 << 20


def place():
    dp, clique = (lax.axis_index("dp"), lax.axis_index("clique"))
    return (lax.rem(dp, 2), lax.div(clique, Z), lax.rem(clique, Z))


def along_clique(where):
    return [(y * Z + z, where(y, z)[0] * Z + where(y, z)[1]) for y in range(Y) for z in range(Z)]


def along_dp(where):
    return [(2 * x + c, 2 * where(x, c)[0] + where(x, c)[1]) for x in range(4) for c in range(2)]


def other_core(value):
    return lax.ppermute(value, "dp", along_dp(lambda x, c: (x, 1 - c)))


def in_quad(z, step):
    return z // QUAD * QUAD + (z + step) % QUAD


def split(value):
    high = value.astype(jnp.bfloat16)
    low = (value - high.astype(jnp.float32)).astype(jnp.bfloat16)
    return (high, low)


def product(left, right):
    left_high, left_low = split(left)
    right_high, right_low = split(right)
    dot = functools.partial(jnp.dot, preferred_element_type=jnp.float32)
    return dot(left_high, right_high) + (dot(left_high, right_low) + dot(left_low, right_high))


def diagonal(size):
    rows = lax.broadcasted_iota(jnp.int32, (size, size), 0)
    return rows == lax.broadcasted_iota(jnp.int32, (size, size), 1)


def as_column(row, eye):
    return jnp.sum(jnp.where(eye, row, 0.0), axis=1, keepdims=True)


def as_row(column, eye):
    return jnp.sum(jnp.where(eye, column, 0.0), axis=0, keepdims=True)


def row_times(row, matrix, eye):
    column = as_column(row, eye) / jnp.sum(row, axis=1, keepdims=True)
    return jnp.sum(column * matrix, axis=0, keepdims=True)


def times_row(matrix, row, eye):
    column = jnp.sum(matrix * row, axis=1, keepdims=True)
    return as_row(column, eye) / jnp.sum(column, axis=0, keepdims=True)


def read_kernel(order_hbm, potential_hbm, order_ref, kernel_ref, half_ref, copied_ref, semaphores):
    core, _, _ = place()
    copies = (
        pltpu.make_async_copy(order_hbm, order_ref, semaphores.at[0]),
        pltpu.make_async_copy(potential_hbm, copied_ref, semaphores.at[1]),
    )
    for copy in copies:
        copy.start()
    for copy in copies:
        copy.wait()
    half = half_ref.shape[0]
    kernel_ref[...] = jnp.exp(copied_ref[...] - shift)
    half_ref[...] = kernel_ref[pl.ds(core * half, half), :]


def put_others(stack_ref, mine, near, near_sibling, far, far_sibling, core):
    half = far.shape[0]
    across = mine ^ 2
    stack_ref[mine ^ (1 + 2 * core)] = near[...]
    stack_ref[mine ^ (3 - 2 * core)] = near_sibling[...]
    stack_ref[across, pl.ds(core * half, half), :] = far[...]
    stack_ref[across, pl.ds((1 - core) * half, half), :] = far_sibling[...]


def quad_kernel(kernel_ref, near, near_sibling, far, far_sibling, quad_ref, product_ref, half_ref):
    core, _, z = place()
    mine = lax.rem(z, QUAD)
    half, size = half_ref.shape
    quad_ref[mine] = kernel_ref[...]
    put_others(quad_ref, mine, near, near_sibling, far, far_sibling, core)
    scale = 1.0 / size
    left = product(quad_ref[0], quad_ref[1]) * scale
    right = product(quad_ref[2], quad_ref[3]) * scale
    whole = product(left, right) * scale
    largest = jnp.max(jnp.max(whole, axis=0, keepdims=True), axis=1, keepdims=True)
    product_ref[...] = whole / largest
    half_ref[...] = product_ref[pl.ds(core * half, half), :]


def spots():
    core, y, z = place()
    return (core, y, 2 * lax.rem(y, 2) + lax.div(z, QUAD), lax.rem(z, QUAD))


def put_halves(stack_ref, slot, own, sibling, core):
    half = own.shape[0]
    stack_ref[slot, pl.ds(core * half, half), :] = own[...]
    stack_ref[slot, pl.ds((1 - core) * half, half), :] = sibling[...]


def block_kernel(product_ref, a1, a2, a3, b1, b2, b3, block_ref, message_ref):
    core, y, mine, _ = spots()
    size = product_ref.shape[0]
    block_ref[mine] = product_ref[...]
    for flip, (own, sibling) in enumerate(((a1, b1), (a2, b2), (a3, b3)), 1):
        put_halves(block_ref, mine ^ flip, own, sibling, core)
    eye = diagonal(size)
    ones = jnp.ones((1, size), jnp.float32)

    @pl.when(y < Y // 2)
    def _():
        row = ones
        for position in range(4):
            row = row_times(row, block_ref[position], eye)
        message_ref[...] = jnp.broadcast_to(row, message_ref.shape)

    @pl.when(y >= Y // 2)
    def _():
        row = ones
        for position in range(4):
            row = times_row(block_ref[3 - position], row, eye)
        message_ref[...] = jnp.broadcast_to(row, message_ref.shape)


def unit_product(left, right):
    moved = product(left, right)
    return moved / jnp.max(jnp.max(moved, axis=0, keepdims=True), axis=1, keepdims=True)


def sides_kernel(quad_ref, block_ref, path_ref, known_ref):
    _, y, in_block, mine = spots()
    size = path_ref.shape[0]
    eye = diagonal(size)
    ones = jnp.ones((1, size), jnp.float32)
    start = jnp.where(eye, 1.0, 0.0)

    @pl.when(y >= Y // 2)
    def _():
        path = lax.fori_loop(0, in_block, lambda i, m: unit_product(m, block_ref[i]), start)
        path_ref[...] = lax.fori_loop(0, mine, lambda i, m: unit_product(m, quad_ref[i]), path)
        row = lax.fori_loop(
            0, 3 - in_block, lambda i, row: times_row(block_ref[3 - i], row, eye), ones
        )
        row = lax.fori_loop(
            0, QUAD - 1 - mine, lambda i, row: times_row(quad_ref[QUAD - 1 - i], row, eye), row
        )
        known_ref[...] = jnp.broadcast_to(row, known_ref.shape)

    @pl.when(y < Y // 2)
    def _():
        path = lax.fori_loop(
            0, 3 - in_block, lambda i, m: unit_product(block_ref[3 - i], m), start
        )
        path_ref[...] = lax.fori_loop(
            0, QUAD - 1 - mine, lambda i, m: unit_product(quad_ref[QUAD - 1 - i], m), path
        )
        row = lax.fori_loop(0, in_block, lambda i, row: row_times(row, block_ref[i], eye), ones)
        row = lax.fori_loop(0, mine, lambda i, row: row_times(row, quad_ref[i], eye), row)
        known_ref[...] = jnp.broadcast_to(row, known_ref.shape)


def chip_kernel(own_ref, sibling_ref, both_ref, half_ref):
    core, _, _ = place()
    half = half_ref.shape[0]
    both_ref[...] = own_ref[...] + sibling_ref[...]
    half_ref[...] = both_ref[pl.ds(core * half, half), :]


def join_kernel(near_ref, far_ref, sum_ref):
    core, _, _ = place()
    half = far_ref.shape[0]
    sum_ref[...] = near_ref[...]
    sum_ref[pl.ds(core * half, half), :] += far_ref[...]


def final_kernel(
    scale, potential_ref, noise_ref, kernel_ref, path_ref, known_ref, message_ref, chip_ref,
    join_ref, sibling_join_ref, updated_ref, beliefs_ref, column_ref, row_ref
):
    _, y, _, _ = spots()
    size = potential_ref.shape[0]
    eye = diagonal(size)
    known, message = (known_ref[0:1, :], message_ref[0:1, :])

    @pl.when(y >= Y // 2)
    def _():
        forward = row_times(message, path_ref[...], eye)
        column_ref[...] = as_column(forward, eye) / jnp.sum(forward, axis=1, keepdims=True)
        row_ref[...] = known

    @pl.when(y < Y // 2)
    def _():
        column_ref[...] = as_column(known, eye) / jnp.sum(known, axis=1, keepdims=True)
        row_ref[...] = times_row(path_ref[...], message, eye)

    joint = column_ref[...] * kernel_ref[...] * row_ref[...]
    total = jnp.sum(jnp.sum(joint, axis=0, keepdims=True), axis=1, keepdims=True)
    beliefs = joint * (size * size / total)
    beliefs_ref[...] = beliefs
    counts = chip_ref[...] + join_ref[...] + sibling_join_ref[...]
    measured = (counts + noise_ref[...]) * scale
    updated_ref[...] = potential_ref[...] - step_size * (beliefs - measured)


def count_kernel(part, order_ref, left_ref, right_ref, total_ref):
    _, y, z = place()
    clique = y * Z + z
    size = total_ref.shape[0]

    @pl.when(pl.program_id(0) == 0)
    def _():
        total_ref[...] = jnp.zeros_like(total_ref)

    levels = lax.broadcasted_iota(jnp.int32, (size, part), 0).astype(jnp.bfloat16)
    one = jnp.ones((size, part), jnp.bfloat16)
    zero = jnp.zeros((size, part), jnp.bfloat16)

    def onehot(ref, attribute, begin):
        values = ref[pl.ds(lax.rem(attribute, 8), 1), begin : begin + part]
        values = values.astype(jnp.float32).astype(jnp.bfloat16)
        return jnp.where(values == levels, one, zero).astype(jnp.float8_e4m3fn)

    total = total_ref[...]
    for begin in range(0, left_ref.shape[1], part):
        total = total + lax.dot_general(
            onehot(left_ref, order_ref[clique], begin),
            onehot(right_ref, order_ref[clique + 1], begin),
            (((1,), (1,)), ((), ())),
            preferred_element_type=jnp.float32,
        )
    total_ref[...] = total


def shape(*dims):
    return jax.ShapeDtypeStruct(dims, jnp.float32)


PARAMS = pltpu.CompilerParams(vmem_limit_bytes=VMEM_LIMIT)


def count_pairs(order, table_rows, size):
    window, part = 16384, 8192

    def rows_of(offset):
        def block(step, order_ref):
            return (lax.div(order_ref[lax.axis_index("clique") + offset], 8), step)

        return pl.BlockSpec((8, window), block)

    return pl.pallas_call(
        functools.partial(count_kernel, part),
        out_shape=shape(size, size),
        grid_spec=pltpu.PrefetchScalarGridSpec(
            num_scalar_prefetch=1,
            grid=(table_rows.shape[1] // window,),
            in_specs=[rows_of(0), rows_of(1)],
            out_specs=pl.BlockSpec((size, size), lambda step, order_ref: (0, 0)),
        ),
        compiler_params=PARAMS,
        name="counts",
    )(order, table_rows, table_rows)


def everywhere(move):
    pairs = []
    for x in range(4):
        for c in range(2):
            for y in range(Y):
                for z in range(Z):
                    to_x, to_y, to_z = move(x, c, y, z)
                    source = (2 * x + c) * Y * Z + y * Z + z
                    pairs.append((source, (2 * to_x + c) * Y * Z + to_y * Z + to_z))
    return pairs


def exchange(whole, half, near_step, far_step):
    axes = ("dp", "clique")
    return (
        lax.ppermute(whole, axes, everywhere(near_step)),
        lax.ppermute(half, axes, everywhere(lambda x, c, y, z: far_step(x, y, z))),
    )


def per_device(table_rows, attribute_order, log_potential, measure_noise):
    size = log_potential.shape[1]
    potential = log_potential[0]
    call = functools.partial(pl.pallas_call, compiler_params=PARAMS)
    vmem = pl.BlockSpec(memory_space=pltpu.VMEM)
    hbm = pl.BlockSpec(memory_space=pltpu.HBM)
    whole, half = (shape(size, size), shape(size // 2, size))
    order, kernel, half_of_kernel = call(
        read_kernel,
        in_specs=[hbm, hbm],
        out_specs=(vmem, vmem, vmem),
        out_shape=(jax.ShapeDtypeStruct(attribute_order.shape, jnp.int32), whole, half),
        scratch_shapes=[pltpu.VMEM((size, size), jnp.float32), pltpu.SemaphoreType.DMA((2,))],
        name="read",
    )(
        pltpu.with_memory_space_constraint(attribute_order, pltpu.HBM),
        pltpu.with_memory_space_constraint(potential, pltpu.HBM),
    )
    near, far = exchange(
        kernel,
        half_of_kernel,
        lambda x, c, y, z: (x, y, z ^ (1 + 2 * c)),
        lambda x, y, z: (x, y, z ^ 2),
    )
    counts = count_pairs(order, table_rows, size)
    near, far, counts = lax.optimization_barrier((near, far, counts))
    quad, quad_product, half_product = call(
        quad_kernel, out_shape=(shape(QUAD, size, size), whole, half), name="quad"
    )(kernel, near, other_core(near), far, other_core(far))
    across = lax.ppermute(half_product, "clique", along_clique(lambda y, z: (y, z ^ 6)))
    beside = lax.ppermute(half_product, "clique", along_clique(lambda y, z: (y ^ 1, z)))
    counts, quad = lax.optimization_barrier((counts, quad))
    chip_counts, half_counts = call(chip_kernel, out_shape=(whole, half), name="chip")(
        counts, other_core(counts)
    )
    near_counts, far_counts = exchange(
        chip_counts,
        half_counts,
        lambda x, c, y, z: (x ^ (1 + 2 * c), y, z),
        lambda x, y, z: (x ^ 2, y, z),
    )
    relayed = lax.ppermute(across, "clique", along_clique(lambda y, z: (y ^ 1, z)))
    held, beside, far_counts = lax.optimization_barrier((across, beside, far_counts))
    relayed, near_counts = lax.optimization_barrier((relayed, near_counts))
    arrived = (held, beside, relayed)
    block, message = call(
        block_kernel, out_shape=(shape(4, size, size), shape(8, size)), name="block"
    )(quad_product, *arrived, *[other_core(value) for value in arrived])
    message, near_counts = lax.optimization_barrier((message, near_counts))
    joined = call(join_kernel, out_shape=whole, name="join")(near_counts, far_counts)
    arrived = lax.ppermute(message, "clique", along_clique(lambda y, z: (y ^ 2, z)))
    path, known = call(sides_kernel, out_shape=(whole, shape(8, size)), name="sides")(quad, block)
    total_rows = table_rows.shape[1] * lax.axis_size("dp")
    updated, beliefs = call(
        functools.partial(final_kernel, size * size / total_rows),
        out_shape=(whole, whole),
        scratch_shapes=[
            pltpu.VMEM((size, 1), jnp.float32),
            pltpu.VMEM((1, size), jnp.float32),
        ],
        name="final",
    )(
        potential, measure_noise[0], kernel, path, known, arrived, chip_counts, joined,
        other_core(joined),
    )
    return (updated[None], beliefs[None])


def solution(mesh):
    in_specs = (P(None, "dp"), P(), P("clique", None, None), P("clique", None, None))
    out_specs = (P("clique", None, None), P("clique", None, None))
    return jax.shard_map(
        per_device, mesh=mesh, in_specs=in_specs, out_specs=out_specs, check_vma=False
    )
```

```python
import functools

import jax
import jax.numpy as jnp
from jax import lax
from jax.experimental import pallas as pl
from jax.experimental.pallas import tpu as pltpu
from jax.sharding import PartitionSpec as P

step_size = 0.25
shift = 7.0
Y, Z, QUAD = 4, 8, 4
VMEM_LIMIT = 50 << 20


def place():
    dp, clique = (lax.axis_index("dp"), lax.axis_index("clique"))
    return (lax.rem(dp, 2), lax.div(clique, Z), lax.rem(clique, Z))


def along_clique(where):
    return [(y * Z + z, where(y, z)[0] * Z + where(y, z)[1]) for y in range(Y) for z in range(Z)]


def along_dp(where):
    return [(2 * x + c, 2 * where(x, c)[0] + where(x, c)[1]) for x in range(4) for c in range(2)]


def other_core(value):
    return lax.ppermute(value, "dp", along_dp(lambda x, c: (x, 1 - c)))


def in_quad(z, step):
    return z // QUAD * QUAD + (z + step) % QUAD


def split(value):
    high = value.astype(jnp.bfloat16)
    low = (value - high.astype(jnp.float32)).astype(jnp.bfloat16)
    return (high, low)


def product(left, right):
    left_high, left_low = split(left)
    right_high, right_low = split(right)
    dot = functools.partial(jnp.dot, preferred_element_type=jnp.float32)
    return dot(left_high, right_high) + (dot(left_high, right_low) + dot(left_low, right_high))


def diagonal(size):
    rows = lax.broadcasted_iota(jnp.int32, (size, size), 0)
    return rows == lax.broadcasted_iota(jnp.int32, (size, size), 1)


def as_column(row, eye):
    return jnp.sum(jnp.where(eye, row, 0.0), axis=1, keepdims=True)


def as_row(column, eye):
    return jnp.sum(jnp.where(eye, column, 0.0), axis=0, keepdims=True)


def row_times(row, matrix, eye):
    column = as_column(row, eye) / jnp.sum(row, axis=1, keepdims=True)
    return jnp.sum(column * matrix, axis=0, keepdims=True)


def times_row(matrix, row, eye):
    column = jnp.sum(matrix * row, axis=1, keepdims=True)
    return as_row(column, eye) / jnp.sum(column, axis=0, keepdims=True)


def read_kernel(order_hbm, potential_hbm, order_ref, kernel_ref, half_ref, copied_ref, semaphores):
    core, _, _ = place()
    copies = (
        pltpu.make_async_copy(order_hbm, order_ref, semaphores.at[0]),
        pltpu.make_async_copy(potential_hbm, copied_ref, semaphores.at[1]),
    )
    for copy in copies:
        copy.start()
    for copy in copies:
        copy.wait()
    half = half_ref.shape[0]
    kernel_ref[...] = jnp.exp(copied_ref[...] - shift)
    half_ref[...] = kernel_ref[pl.ds(core * half, half), :]


def put_others(stack_ref, mine, near, near_sibling, far, far_sibling, core):
    half = far.shape[0]
    across = mine ^ 2
    stack_ref[mine ^ (1 + 2 * core)] = near[...]
    stack_ref[mine ^ (3 - 2 * core)] = near_sibling[...]
    stack_ref[across, pl.ds(core * half, half), :] = far[...]
    stack_ref[across, pl.ds((1 - core) * half, half), :] = far_sibling[...]


def quad_kernel(kernel_ref, near, near_sibling, far, far_sibling, quad_ref, product_ref, half_ref):
    core, _, z = place()
    mine = lax.rem(z, QUAD)
    half, size = half_ref.shape
    quad_ref[mine] = kernel_ref[...]
    put_others(quad_ref, mine, near, near_sibling, far, far_sibling, core)
    scale = 1.0 / size
    left = product(quad_ref[0], quad_ref[1]) * scale
    right = product(quad_ref[2], quad_ref[3]) * scale
    whole = product(left, right) * scale
    largest = jnp.max(jnp.max(whole, axis=0, keepdims=True), axis=1, keepdims=True)
    product_ref[...] = whole / largest
    half_ref[...] = product_ref[pl.ds(core * half, half), :]


def spots():
    core, y, z = place()
    return (core, y, 2 * lax.rem(y, 2) + lax.div(z, QUAD), lax.rem(z, QUAD))


def put_halves(stack_ref, slot, own, sibling, core):
    half = own.shape[0]
    stack_ref[slot, pl.ds(core * half, half), :] = own[...]
    stack_ref[slot, pl.ds((1 - core) * half, half), :] = sibling[...]


def block_kernel(product_ref, a1, a2, a3, b1, b2, b3, block_ref, message_ref):
    core, y, mine, _ = spots()
    size = product_ref.shape[0]
    block_ref[mine] = product_ref[...]
    for flip, (own, sibling) in enumerate(((a1, b1), (a2, b2), (a3, b3)), 1):
        put_halves(block_ref, mine ^ flip, own, sibling, core)
    eye = diagonal(size)
    ones = jnp.ones((1, size), jnp.float32)

    @pl.when(y < Y // 2)
    def _():
        row = ones
        for position in range(4):
            row = row_times(row, block_ref[position], eye)
        message_ref[...] = jnp.broadcast_to(row, message_ref.shape)

    @pl.when(y >= Y // 2)
    def _():
        row = ones
        for position in range(4):
            row = times_row(block_ref[3 - position], row, eye)
        message_ref[...] = jnp.broadcast_to(row, message_ref.shape)


def unit_product(left, right):
    moved = product(left, right)
    return moved / jnp.max(jnp.max(moved, axis=0, keepdims=True), axis=1, keepdims=True)


def sides_kernel(quad_ref, block_ref, path_ref, known_ref):
    _, y, in_block, mine = spots()
    size = path_ref.shape[0]
    eye = diagonal(size)
    ones = jnp.ones((1, size), jnp.float32)
    start = jnp.where(eye, 1.0, 0.0)

    @pl.when(y >= Y // 2)
    def _():
        path = lax.fori_loop(0, in_block, lambda i, m: unit_product(m, block_ref[i]), start)
        path_ref[...] = lax.fori_loop(0, mine, lambda i, m: unit_product(m, quad_ref[i]), path)
        row = lax.fori_loop(
            0, 3 - in_block, lambda i, row: times_row(block_ref[3 - i], row, eye), ones
        )
        row = lax.fori_loop(
            0, QUAD - 1 - mine, lambda i, row: times_row(quad_ref[QUAD - 1 - i], row, eye), row
        )
        known_ref[...] = jnp.broadcast_to(row, known_ref.shape)

    @pl.when(y < Y // 2)
    def _():
        path = lax.fori_loop(
            0, 3 - in_block, lambda i, m: unit_product(block_ref[3 - i], m), start
        )
        path_ref[...] = lax.fori_loop(
            0, QUAD - 1 - mine, lambda i, m: unit_product(quad_ref[QUAD - 1 - i], m), path
        )
        row = lax.fori_loop(0, in_block, lambda i, row: row_times(row, block_ref[i], eye), ones)
        row = lax.fori_loop(0, mine, lambda i, row: row_times(row, quad_ref[i], eye), row)
        known_ref[...] = jnp.broadcast_to(row, known_ref.shape)


def chip_kernel(own_ref, sibling_ref, both_ref, half_ref):
    core, _, _ = place()
    half = half_ref.shape[0]
    both_ref[...] = own_ref[...] + sibling_ref[...]
    half_ref[...] = both_ref[pl.ds(core * half, half), :]


def join_kernel(near_ref, far_ref, sum_ref):
    core, _, _ = place()
    half = far_ref.shape[0]
    sum_ref[...] = near_ref[...]
    sum_ref[pl.ds(core * half, half), :] += far_ref[...]


def final_kernel(
    scale, potential_ref, noise_ref, kernel_ref, path_ref, known_ref, message_ref, chip_ref,
    join_ref, sibling_join_ref, updated_ref, beliefs_ref, column_ref, row_ref
):
    _, y, _, _ = spots()
    size = potential_ref.shape[0]
    eye = diagonal(size)
    known, message = (known_ref[0:1, :], message_ref[0:1, :])

    @pl.when(y >= Y // 2)
    def _():
        forward = row_times(message, path_ref[...], eye)
        column_ref[...] = as_column(forward, eye) / jnp.sum(forward, axis=1, keepdims=True)
        row_ref[...] = known

    @pl.when(y < Y // 2)
    def _():
        column_ref[...] = as_column(known, eye) / jnp.sum(known, axis=1, keepdims=True)
        row_ref[...] = times_row(path_ref[...], message, eye)

    joint = column_ref[...] * kernel_ref[...] * row_ref[...]
    total = jnp.sum(jnp.sum(joint, axis=0, keepdims=True), axis=1, keepdims=True)
    beliefs = joint * (size * size / total)
    beliefs_ref[...] = beliefs
    counts = chip_ref[...] + join_ref[...] + sibling_join_ref[...]
    measured = (counts + noise_ref[...]) * scale
    updated_ref[...] = potential_ref[...] - step_size * (beliefs - measured)


def count_kernel(part, order_ref, left_ref, right_ref, total_ref):
    _, y, z = place()
    clique = y * Z + z
    size = total_ref.shape[0]

    @pl.when(pl.program_id(0) == 0)
    def _():
        total_ref[...] = jnp.zeros_like(total_ref)

    levels = lax.broadcasted_iota(jnp.int32, (size, part), 0).astype(jnp.bfloat16)
    one = jnp.ones((size, part), jnp.bfloat16)
    zero = jnp.zeros((size, part), jnp.bfloat16)

    def onehot(ref, attribute, begin):
        values = ref[pl.ds(lax.rem(attribute, 8), 1), begin : begin + part]
        values = values.astype(jnp.float32).astype(jnp.bfloat16)
        return jnp.where(values == levels, one, zero).astype(jnp.float8_e4m3fn)

    total = total_ref[...]
    for begin in range(0, left_ref.shape[1], part):
        total = total + lax.dot_general(
            onehot(left_ref, order_ref[clique], begin),
            onehot(right_ref, order_ref[clique + 1], begin),
            (((1,), (1,)), ((), ())),
            preferred_element_type=jnp.float32,
        )
    total_ref[...] = total


def shape(*dims):
    return jax.ShapeDtypeStruct(dims, jnp.float32)


PARAMS = pltpu.CompilerParams(vmem_limit_bytes=VMEM_LIMIT)


def count_pairs(order, table_rows, size):
    window, part = 16384, 8192

    def rows_of(offset):
        def block(step, order_ref):
            return (lax.div(order_ref[lax.axis_index("clique") + offset], 8), step)

        return pl.BlockSpec((8, window), block)

    return pl.pallas_call(
        functools.partial(count_kernel, part),
        out_shape=shape(size, size),
        grid_spec=pltpu.PrefetchScalarGridSpec(
            num_scalar_prefetch=1,
            grid=(table_rows.shape[1] // window,),
            in_specs=[rows_of(0), rows_of(1)],
            out_specs=pl.BlockSpec((size, size), lambda step, order_ref: (0, 0)),
        ),
        compiler_params=PARAMS,
        name="counts",
    )(order, table_rows, table_rows)


def everywhere(move):
    pairs = []
    for x in range(4):
        for c in range(2):
            for y in range(Y):
                for z in range(Z):
                    to_x, to_y, to_z = move(x, c, y, z)
                    source = (2 * x + c) * Y * Z + y * Z + z
                    pairs.append((source, (2 * to_x + c) * Y * Z + to_y * Z + to_z))
    return pairs


def exchange(whole, half, near_step, far_step):
    axes = ("dp", "clique")
    return (
        lax.ppermute(whole, axes, everywhere(near_step)),
        lax.ppermute(half, axes, everywhere(lambda x, c, y, z: far_step(x, y, z))),
    )


def per_device(table_rows, attribute_order, log_potential, measure_noise):
    size = log_potential.shape[1]
    potential = log_potential[0]
    call = functools.partial(pl.pallas_call, compiler_params=PARAMS)
    vmem = pl.BlockSpec(memory_space=pltpu.VMEM)
    hbm = pl.BlockSpec(memory_space=pltpu.HBM)
    whole, half = (shape(size, size), shape(size // 2, size))
    order, kernel, half_of_kernel = call(
        read_kernel,
        in_specs=[hbm, hbm],
        out_specs=(vmem, vmem, vmem),
        out_shape=(jax.ShapeDtypeStruct(attribute_order.shape, jnp.int32), whole, half),
        scratch_shapes=[pltpu.VMEM((size, size), jnp.float32), pltpu.SemaphoreType.DMA((2,))],
        name="read",
    )(
        pltpu.with_memory_space_constraint(attribute_order, pltpu.HBM),
        pltpu.with_memory_space_constraint(potential, pltpu.HBM),
    )
    near, far = exchange(
        kernel,
        half_of_kernel,
        lambda x, c, y, z: (x, y, z ^ (1 + 2 * c)),
        lambda x, y, z: (x, y, z ^ 2),
    )
    counts = count_pairs(order, table_rows, size)
    near, far, counts = lax.optimization_barrier((near, far, counts))
    sibling_counts = other_core(counts)
    quad, quad_product, half_product = call(
        quad_kernel, out_shape=(shape(QUAD, size, size), whole, half), name="quad"
    )(kernel, near, other_core(near), far, other_core(far))
    across = lax.ppermute(half_product, "clique", along_clique(lambda y, z: (y, z ^ 6)))
    beside = lax.ppermute(half_product, "clique", along_clique(lambda y, z: (y ^ 1, z)))
    counts, sibling_counts, quad = lax.optimization_barrier((counts, sibling_counts, quad))
    chip_counts, half_counts = call(chip_kernel, out_shape=(whole, half), name="chip")(
        counts, sibling_counts
    )
    near_counts, far_counts = exchange(
        chip_counts,
        half_counts,
        lambda x, c, y, z: (x ^ (1 + 2 * c), y, z),
        lambda x, y, z: (x ^ 2, y, z),
    )
    relayed = lax.ppermute(across, "clique", along_clique(lambda y, z: (y ^ 1, z)))
    held, beside, far_counts = lax.optimization_barrier((across, beside, far_counts))
    relayed, near_counts = lax.optimization_barrier((relayed, near_counts))
    arrived = (held, beside, relayed)
    block, message = call(
        block_kernel, out_shape=(shape(4, size, size), shape(8, size)), name="block"
    )(quad_product, *arrived, *[other_core(value) for value in arrived])
    message, near_counts = lax.optimization_barrier((message, near_counts))
    joined = call(join_kernel, out_shape=whole, name="join")(near_counts, far_counts)
    arrived = lax.ppermute(message, "clique", along_clique(lambda y, z: (y ^ 2, z)))
    path, known = call(sides_kernel, out_shape=(whole, shape(8, size)), name="sides")(quad, block)
    total_rows = table_rows.shape[1] * lax.axis_size("dp")
    updated, beliefs = call(
        functools.partial(final_kernel, size * size / total_rows),
        out_shape=(whole, whole),
        scratch_shapes=[
            pltpu.VMEM((size, 1), jnp.float32),
            pltpu.VMEM((1, size), jnp.float32),
        ],
        name="final",
    )(
        potential, measure_noise[0], kernel, path, known, arrived, chip_counts, joined,
        other_core(joined),
    )
    return (updated[None], beliefs[None])


def solution(mesh):
    in_specs = (P(None, "dp"), P(), P("clique", None, None), P("clique", None, None))
    out_specs = (P("clique", None, None), P("clique", None, None))
    return jax.shard_map(
        per_device, mesh=mesh, in_specs=in_specs, out_specs=out_specs, check_vma=False
    )
```

```python
import functools

import jax
import jax.numpy as jnp
from jax import lax
from jax.experimental import pallas as pl
from jax.experimental.pallas import tpu as pltpu
from jax.sharding import PartitionSpec as P

step_size = 0.25
shift = 7.0
Y, Z, QUAD = 4, 8, 4
VMEM_LIMIT = 50 << 20


def place():
    dp, clique = (lax.axis_index("dp"), lax.axis_index("clique"))
    return (lax.rem(dp, 2), lax.div(clique, Z), lax.rem(clique, Z))


def along_clique(where):
    return [(y * Z + z, where(y, z)[0] * Z + where(y, z)[1]) for y in range(Y) for z in range(Z)]


def along_dp(where):
    return [(2 * x + c, 2 * where(x, c)[0] + where(x, c)[1]) for x in range(4) for c in range(2)]


def other_core(value):
    return lax.ppermute(value, "dp", along_dp(lambda x, c: (x, 1 - c)))


def in_quad(z, step):
    return z // QUAD * QUAD + (z + step) % QUAD


def split(value):
    high = value.astype(jnp.bfloat16)
    low = (value - high.astype(jnp.float32)).astype(jnp.bfloat16)
    return (high, low)


def product(left, right):
    left_high, left_low = split(left)
    right_high, right_low = split(right)
    dot = functools.partial(jnp.dot, preferred_element_type=jnp.float32)
    return dot(left_high, right_high) + (dot(left_high, right_low) + dot(left_low, right_high))


def diagonal(size):
    rows = lax.broadcasted_iota(jnp.int32, (size, size), 0)
    return rows == lax.broadcasted_iota(jnp.int32, (size, size), 1)


def as_column(row, eye):
    return jnp.sum(jnp.where(eye, row, 0.0), axis=1, keepdims=True)


def as_row(column, eye):
    return jnp.sum(jnp.where(eye, column, 0.0), axis=0, keepdims=True)


def row_times(row, matrix, eye):
    column = as_column(row, eye) / jnp.sum(row, axis=1, keepdims=True)
    return jnp.sum(column * matrix, axis=0, keepdims=True)


def times_row(matrix, row, eye):
    column = jnp.sum(matrix * row, axis=1, keepdims=True)
    return as_row(column, eye) / jnp.sum(column, axis=0, keepdims=True)


def read_kernel(order_hbm, potential_hbm, order_ref, kernel_ref, half_ref, copied_ref, semaphores):
    core, _, _ = place()
    pieces = semaphores.shape[0] - 1
    part = copied_ref.shape[0] // pieces
    copies = [pltpu.make_async_copy(order_hbm, order_ref, semaphores.at[pieces])]
    for piece in range(pieces):
        rows = pl.ds(piece * part, part)
        copies.append(
            pltpu.make_async_copy(
                potential_hbm.at[rows, :], copied_ref.at[rows, :], semaphores.at[piece]
            )
        )
    for copy in copies:
        copy.start()
    for copy in copies:
        copy.wait()
    half = half_ref.shape[0]
    kernel_ref[...] = jnp.exp(copied_ref[...] - shift)
    half_ref[...] = kernel_ref[pl.ds(core * half, half), :]


def put_others(stack_ref, mine, near, near_sibling, far, far_sibling, core):
    half = far.shape[0]
    across = mine ^ 2
    stack_ref[mine ^ (1 + 2 * core)] = near[...]
    stack_ref[mine ^ (3 - 2 * core)] = near_sibling[...]
    stack_ref[across, pl.ds(core * half, half), :] = far[...]
    stack_ref[across, pl.ds((1 - core) * half, half), :] = far_sibling[...]


def quad_kernel(kernel_ref, near, near_sibling, far, far_sibling, quad_ref, product_ref, half_ref):
    core, _, z = place()
    mine = lax.rem(z, QUAD)
    half, size = half_ref.shape
    quad_ref[mine] = kernel_ref[...]
    put_others(quad_ref, mine, near, near_sibling, far, far_sibling, core)
    scale = 1.0 / size
    left = product(quad_ref[0], quad_ref[1]) * scale
    right = product(quad_ref[2], quad_ref[3]) * scale
    whole = product(left, right) * scale
    largest = jnp.max(jnp.max(whole, axis=0, keepdims=True), axis=1, keepdims=True)
    product_ref[...] = whole / largest
    half_ref[...] = product_ref[pl.ds(core * half, half), :]


def spots():
    core, y, z = place()
    return (core, y, 2 * lax.rem(y, 2) + lax.div(z, QUAD), lax.rem(z, QUAD))


def put_halves(stack_ref, slot, own, sibling, core):
    half = own.shape[0]
    stack_ref[slot, pl.ds(core * half, half), :] = own[...]
    stack_ref[slot, pl.ds((1 - core) * half, half), :] = sibling[...]


def block_kernel(product_ref, a1, a2, a3, b1, b2, b3, block_ref, message_ref):
    core, y, mine, _ = spots()
    size = product_ref.shape[0]
    block_ref[mine] = product_ref[...]
    for flip, (own, sibling) in enumerate(((a1, b1), (a2, b2), (a3, b3)), 1):
        put_halves(block_ref, mine ^ flip, own, sibling, core)
    eye = diagonal(size)
    ones = jnp.ones((1, size), jnp.float32)

    @pl.when(y < Y // 2)
    def _():
        row = ones
        for position in range(4):
            row = row_times(row, block_ref[position], eye)
        message_ref[...] = jnp.broadcast_to(row, message_ref.shape)

    @pl.when(y >= Y // 2)
    def _():
        row = ones
        for position in range(4):
            row = times_row(block_ref[3 - position], row, eye)
        message_ref[...] = jnp.broadcast_to(row, message_ref.shape)


def unit_product(left, right):
    moved = product(left, right)
    return moved / jnp.max(jnp.max(moved, axis=0, keepdims=True), axis=1, keepdims=True)


def sides_kernel(quad_ref, block_ref, path_ref, known_ref):
    _, y, in_block, mine = spots()
    size = path_ref.shape[0]
    eye = diagonal(size)
    ones = jnp.ones((1, size), jnp.float32)
    start = jnp.where(eye, 1.0, 0.0)

    @pl.when(y >= Y // 2)
    def _():
        path = lax.fori_loop(0, in_block, lambda i, m: unit_product(m, block_ref[i]), start)
        path_ref[...] = lax.fori_loop(0, mine, lambda i, m: unit_product(m, quad_ref[i]), path)
        row = lax.fori_loop(
            0, 3 - in_block, lambda i, row: times_row(block_ref[3 - i], row, eye), ones
        )
        row = lax.fori_loop(
            0, QUAD - 1 - mine, lambda i, row: times_row(quad_ref[QUAD - 1 - i], row, eye), row
        )
        known_ref[...] = jnp.broadcast_to(row, known_ref.shape)

    @pl.when(y < Y // 2)
    def _():
        path = lax.fori_loop(
            0, 3 - in_block, lambda i, m: unit_product(block_ref[3 - i], m), start
        )
        path_ref[...] = lax.fori_loop(
            0, QUAD - 1 - mine, lambda i, m: unit_product(quad_ref[QUAD - 1 - i], m), path
        )
        row = lax.fori_loop(0, in_block, lambda i, row: row_times(row, block_ref[i], eye), ones)
        row = lax.fori_loop(0, mine, lambda i, row: row_times(row, quad_ref[i], eye), row)
        known_ref[...] = jnp.broadcast_to(row, known_ref.shape)


def chip_kernel(own_ref, sibling_ref, both_ref, half_ref):
    core, _, _ = place()
    half = half_ref.shape[0]
    both_ref[...] = own_ref[...] + sibling_ref[...]
    half_ref[...] = both_ref[pl.ds(core * half, half), :]


def join_kernel(near_ref, far_ref, sum_ref):
    core, _, _ = place()
    half = far_ref.shape[0]
    sum_ref[...] = near_ref[...]
    sum_ref[pl.ds(core * half, half), :] += far_ref[...]


def final_kernel(
    scale, potential_ref, noise_ref, kernel_ref, path_ref, known_ref, message_ref, chip_ref,
    join_ref, sibling_join_ref, updated_ref, beliefs_ref, column_ref, row_ref
):
    _, y, _, _ = spots()
    size = potential_ref.shape[0]
    eye = diagonal(size)
    known, message = (known_ref[0:1, :], message_ref[0:1, :])

    @pl.when(y >= Y // 2)
    def _():
        forward = row_times(message, path_ref[...], eye)
        column_ref[...] = as_column(forward, eye) / jnp.sum(forward, axis=1, keepdims=True)
        row_ref[...] = known

    @pl.when(y < Y // 2)
    def _():
        column_ref[...] = as_column(known, eye) / jnp.sum(known, axis=1, keepdims=True)
        row_ref[...] = times_row(path_ref[...], message, eye)

    joint = column_ref[...] * kernel_ref[...] * row_ref[...]
    total = jnp.sum(jnp.sum(joint, axis=0, keepdims=True), axis=1, keepdims=True)
    beliefs = joint * (size * size / total)
    beliefs_ref[...] = beliefs
    counts = chip_ref[...] + join_ref[...] + sibling_join_ref[...]
    measured = (counts + noise_ref[...]) * scale
    updated_ref[...] = potential_ref[...] - step_size * (beliefs - measured)


def count_kernel(part, order_ref, left_ref, right_ref, total_ref):
    _, y, z = place()
    clique = y * Z + z
    size = total_ref.shape[0]

    @pl.when(pl.program_id(0) == 0)
    def _():
        total_ref[...] = jnp.zeros_like(total_ref)

    levels = lax.broadcasted_iota(jnp.int32, (size, part), 0).astype(jnp.bfloat16)
    one = jnp.ones((size, part), jnp.bfloat16)
    zero = jnp.zeros((size, part), jnp.bfloat16)

    def onehot(ref, attribute, begin):
        values = ref[pl.ds(lax.rem(attribute, 8), 1), begin : begin + part]
        values = values.astype(jnp.float32).astype(jnp.bfloat16)
        return jnp.where(values == levels, one, zero).astype(jnp.float8_e4m3fn)

    total = total_ref[...]
    for begin in range(0, left_ref.shape[1], part):
        total = total + lax.dot_general(
            onehot(left_ref, order_ref[clique], begin),
            onehot(right_ref, order_ref[clique + 1], begin),
            (((1,), (1,)), ((), ())),
            preferred_element_type=jnp.float32,
        )
    total_ref[...] = total


def shape(*dims):
    return jax.ShapeDtypeStruct(dims, jnp.float32)


PARAMS = pltpu.CompilerParams(vmem_limit_bytes=VMEM_LIMIT)


def count_pairs(order, table_rows, size):
    window, part = 16384, 8192

    def rows_of(offset):
        def block(step, order_ref):
            return (lax.div(order_ref[lax.axis_index("clique") + offset], 8), step)

        return pl.BlockSpec((8, window), block)

    return pl.pallas_call(
        functools.partial(count_kernel, part),
        out_shape=shape(size, size),
        grid_spec=pltpu.PrefetchScalarGridSpec(
            num_scalar_prefetch=1,
            grid=(table_rows.shape[1] // window,),
            in_specs=[rows_of(0), rows_of(1)],
            out_specs=pl.BlockSpec((size, size), lambda step, order_ref: (0, 0)),
        ),
        compiler_params=PARAMS,
        name="counts",
    )(order, table_rows, table_rows)


def everywhere(move):
    pairs = []
    for x in range(4):
        for c in range(2):
            for y in range(Y):
                for z in range(Z):
                    to_x, to_y, to_z = move(x, c, y, z)
                    source = (2 * x + c) * Y * Z + y * Z + z
                    pairs.append((source, (2 * to_x + c) * Y * Z + to_y * Z + to_z))
    return pairs


def exchange(whole, half, near_step, far_step):
    axes = ("dp", "clique")
    return (
        lax.ppermute(whole, axes, everywhere(near_step)),
        lax.ppermute(half, axes, everywhere(lambda x, c, y, z: far_step(x, y, z))),
    )


def per_device(table_rows, attribute_order, log_potential, measure_noise):
    size = log_potential.shape[1]
    potential = log_potential[0]
    call = functools.partial(pl.pallas_call, compiler_params=PARAMS)
    vmem = pl.BlockSpec(memory_space=pltpu.VMEM)
    hbm = pl.BlockSpec(memory_space=pltpu.HBM)
    whole, half = (shape(size, size), shape(size // 2, size))
    order, kernel, half_of_kernel = call(
        read_kernel,
        in_specs=[hbm, hbm],
        out_specs=(vmem, vmem, vmem),
        out_shape=(jax.ShapeDtypeStruct(attribute_order.shape, jnp.int32), whole, half),
        scratch_shapes=[pltpu.VMEM((size, size), jnp.float32), pltpu.SemaphoreType.DMA((5,))],
        name="read",
    )(
        pltpu.with_memory_space_constraint(attribute_order, pltpu.HBM),
        pltpu.with_memory_space_constraint(potential, pltpu.HBM),
    )
    near, far = exchange(
        kernel,
        half_of_kernel,
        lambda x, c, y, z: (x, y, z ^ (1 + 2 * c)),
        lambda x, y, z: (x, y, z ^ 2),
    )
    counts = count_pairs(order, table_rows, size)
    near, far, counts = lax.optimization_barrier((near, far, counts))
    quad, quad_product, half_product = call(
        quad_kernel, out_shape=(shape(QUAD, size, size), whole, half), name="quad"
    )(kernel, near, other_core(near), far, other_core(far))
    across = lax.ppermute(half_product, "clique", along_clique(lambda y, z: (y, z ^ 6)))
    beside = lax.ppermute(half_product, "clique", along_clique(lambda y, z: (y ^ 1, z)))
    counts, quad = lax.optimization_barrier((counts, quad))
    chip_counts, half_counts = call(chip_kernel, out_shape=(whole, half), name="chip")(
        counts, other_core(counts)
    )
    near_counts, far_counts = exchange(
        chip_counts,
        half_counts,
        lambda x, c, y, z: (x ^ (1 + 2 * c), y, z),
        lambda x, y, z: (x ^ 2, y, z),
    )
    relayed = lax.ppermute(across, "clique", along_clique(lambda y, z: (y ^ 1, z)))
    held, beside = lax.optimization_barrier((across, beside))
    relayed, far_counts, near_counts = lax.optimization_barrier((relayed, far_counts, near_counts))
    arrived = (held, beside, relayed)
    block, message = call(
        block_kernel, out_shape=(shape(4, size, size), shape(8, size)), name="block"
    )(quad_product, *arrived, *[other_core(value) for value in arrived])
    message, near_counts = lax.optimization_barrier((message, near_counts))
    joined = call(join_kernel, out_shape=whole, name="join")(near_counts, far_counts)
    arrived = lax.ppermute(message, "clique", along_clique(lambda y, z: (y ^ 2, z)))
    path, known = call(sides_kernel, out_shape=(whole, shape(8, size)), name="sides")(quad, block)
    total_rows = table_rows.shape[1] * lax.axis_size("dp")
    updated, beliefs = call(
        functools.partial(final_kernel, size * size / total_rows),
        out_shape=(whole, whole),
        scratch_shapes=[
            pltpu.VMEM((size, 1), jnp.float32),
            pltpu.VMEM((1, size), jnp.float32),
        ],
        name="final",
    )(
        potential, measure_noise[0], kernel, path, known, arrived, chip_counts, joined,
        other_core(joined),
    )
    return (updated[None], beliefs[None])


def solution(mesh):
    in_specs = (P(None, "dp"), P(), P("clique", None, None), P("clique", None, None))
    out_specs = (P("clique", None, None), P("clique", None, None))
    return jax.shard_map(
        per_device, mesh=mesh, in_specs=in_specs, out_specs=out_specs, check_vma=False
    )
```

```python
import functools

import jax
import jax.numpy as jnp
from jax import lax
from jax.experimental import pallas as pl
from jax.experimental.pallas import tpu as pltpu
from jax.sharding import PartitionSpec as P

step_size = 0.25
shift = 7.0
Y, Z, QUAD = 4, 8, 4
VMEM_LIMIT = 50 << 20


def place():
    dp, clique = (lax.axis_index("dp"), lax.axis_index("clique"))
    return (lax.rem(dp, 2), lax.div(clique, Z), lax.rem(clique, Z))


def along_clique(where):
    return [(y * Z + z, where(y, z)[0] * Z + where(y, z)[1]) for y in range(Y) for z in range(Z)]


def along_dp(where):
    return [(2 * x + c, 2 * where(x, c)[0] + where(x, c)[1]) for x in range(4) for c in range(2)]


def other_core(value):
    return lax.ppermute(value, "dp", along_dp(lambda x, c: (x, 1 - c)))


def in_quad(z, step):
    return z // QUAD * QUAD + (z + step) % QUAD


def split(value):
    high = value.astype(jnp.bfloat16)
    low = (value - high.astype(jnp.float32)).astype(jnp.bfloat16)
    return (high, low)


def product(left, right):
    left_high, left_low = split(left)
    right_high, right_low = split(right)
    dot = functools.partial(jnp.dot, preferred_element_type=jnp.float32)
    return dot(left_high, right_high) + (dot(left_high, right_low) + dot(left_low, right_high))


def diagonal(size):
    rows = lax.broadcasted_iota(jnp.int32, (size, size), 0)
    return rows == lax.broadcasted_iota(jnp.int32, (size, size), 1)


def as_column(row, eye):
    return jnp.sum(jnp.where(eye, row, 0.0), axis=1, keepdims=True)


def as_row(column, eye):
    return jnp.sum(jnp.where(eye, column, 0.0), axis=0, keepdims=True)


def row_times(row, matrix, eye):
    column = as_column(row, eye) / jnp.sum(row, axis=1, keepdims=True)
    return jnp.sum(column * matrix, axis=0, keepdims=True)


def times_row(matrix, row, eye):
    column = jnp.sum(matrix * row, axis=1, keepdims=True)
    return as_row(column, eye) / jnp.sum(column, axis=0, keepdims=True)


def read_kernel(order_hbm, potential_hbm, order_ref, kernel_ref, half_ref, copied_ref, semaphores):
    core, _, _ = place()
    copies = (
        pltpu.make_async_copy(order_hbm, order_ref, semaphores.at[0]),
        pltpu.make_async_copy(potential_hbm, copied_ref, semaphores.at[1]),
    )
    for copy in copies:
        copy.start()
    for copy in copies:
        copy.wait()
    half = half_ref.shape[0]
    kernel_ref[...] = jnp.exp(copied_ref[...] - shift)
    half_ref[...] = kernel_ref[pl.ds(core * half, half), :]


def put_others(stack_ref, mine, near, near_sibling, far, far_sibling, core):
    half = far.shape[0]
    across = mine ^ 2
    stack_ref[mine ^ (1 + 2 * core)] = near[...]
    stack_ref[mine ^ (3 - 2 * core)] = near_sibling[...]
    stack_ref[across, pl.ds(core * half, half), :] = far[...]
    stack_ref[across, pl.ds((1 - core) * half, half), :] = far_sibling[...]


def quad_kernel(kernel_ref, near, near_sibling, far, far_sibling, quad_ref, product_ref, half_ref):
    core, _, z = place()
    mine = lax.rem(z, QUAD)
    half, size = half_ref.shape
    quad_ref[mine] = kernel_ref[...]
    put_others(quad_ref, mine, near, near_sibling, far, far_sibling, core)
    scale = 1.0 / size
    left = product(quad_ref[0], quad_ref[1]) * scale
    right = product(quad_ref[2], quad_ref[3]) * scale
    whole = product(left, right) * scale
    largest = jnp.max(jnp.max(whole, axis=0, keepdims=True), axis=1, keepdims=True)
    product_ref[...] = whole / largest
    half_ref[...] = product_ref[pl.ds(core * half, half), :]


def spots():
    core, y, z = place()
    return (core, y, 2 * lax.rem(y, 2) + lax.div(z, QUAD), lax.rem(z, QUAD))


def put_halves(stack_ref, slot, own, sibling, core):
    half = own.shape[0]
    stack_ref[slot, pl.ds(core * half, half), :] = own[...]
    stack_ref[slot, pl.ds((1 - core) * half, half), :] = sibling[...]


def block_kernel(product_ref, a1, a2, a3, b1, b2, b3, block_ref, message_ref):
    core, y, mine, _ = spots()
    size = product_ref.shape[0]
    block_ref[mine] = product_ref[...]
    for flip, (own, sibling) in enumerate(((a1, b1), (a2, b2), (a3, b3)), 1):
        put_halves(block_ref, mine ^ flip, own, sibling, core)
    eye = diagonal(size)
    ones = jnp.ones((1, size), jnp.float32)

    @pl.when(y < Y // 2)
    def _():
        row = ones
        for position in range(4):
            row = row_times(row, block_ref[position], eye)
        message_ref[...] = jnp.broadcast_to(row, message_ref.shape)

    @pl.when(y >= Y // 2)
    def _():
        row = ones
        for position in range(4):
            row = times_row(block_ref[3 - position], row, eye)
        message_ref[...] = jnp.broadcast_to(row, message_ref.shape)


def unit_product(left, right):
    moved = product(left, right)
    return moved / jnp.max(jnp.max(moved, axis=0, keepdims=True), axis=1, keepdims=True)


def sides_kernel(quad_ref, block_ref, path_ref, known_ref):
    _, y, in_block, mine = spots()
    size = path_ref.shape[0]
    eye = diagonal(size)
    ones = jnp.ones((1, size), jnp.float32)
    start = jnp.where(eye, 1.0, 0.0)

    @pl.when(y >= Y // 2)
    def _():
        path = lax.fori_loop(0, in_block, lambda i, m: unit_product(m, block_ref[i]), start)
        path_ref[...] = lax.fori_loop(0, mine, lambda i, m: unit_product(m, quad_ref[i]), path)
        row = lax.fori_loop(
            0, 3 - in_block, lambda i, row: times_row(block_ref[3 - i], row, eye), ones
        )
        row = lax.fori_loop(
            0, QUAD - 1 - mine, lambda i, row: times_row(quad_ref[QUAD - 1 - i], row, eye), row
        )
        known_ref[...] = jnp.broadcast_to(row, known_ref.shape)

    @pl.when(y < Y // 2)
    def _():
        path = lax.fori_loop(
            0, 3 - in_block, lambda i, m: unit_product(block_ref[3 - i], m), start
        )
        path_ref[...] = lax.fori_loop(
            0, QUAD - 1 - mine, lambda i, m: unit_product(quad_ref[QUAD - 1 - i], m), path
        )
        row = lax.fori_loop(0, in_block, lambda i, row: row_times(row, block_ref[i], eye), ones)
        row = lax.fori_loop(0, mine, lambda i, row: row_times(row, quad_ref[i], eye), row)
        known_ref[...] = jnp.broadcast_to(row, known_ref.shape)


def chip_kernel(own_ref, sibling_ref, both_ref, half_ref):
    core, _, _ = place()
    half = half_ref.shape[0]
    both_ref[...] = own_ref[...] + sibling_ref[...]
    half_ref[...] = both_ref[pl.ds(core * half, half), :]


def join_kernel(near_ref, far_ref, sum_ref):
    core, _, _ = place()
    half = far_ref.shape[0]
    sum_ref[...] = near_ref[...]
    sum_ref[pl.ds(core * half, half), :] += far_ref[...]


def final_kernel(
    scale, potential_ref, noise_ref, kernel_ref, path_ref, known_ref, message_ref, chip_ref,
    join_ref, sibling_join_ref, updated_ref, beliefs_ref, column_ref, row_ref
):
    _, y, _, _ = spots()
    size = potential_ref.shape[0]
    eye = diagonal(size)
    known, message = (known_ref[0:1, :], message_ref[0:1, :])

    @pl.when(y >= Y // 2)
    def _():
        forward = row_times(message, path_ref[...], eye)
        column_ref[...] = as_column(forward, eye) / jnp.sum(forward, axis=1, keepdims=True)
        row_ref[...] = known

    @pl.when(y < Y // 2)
    def _():
        column_ref[...] = as_column(known, eye) / jnp.sum(known, axis=1, keepdims=True)
        row_ref[...] = times_row(path_ref[...], message, eye)

    joint = column_ref[...] * kernel_ref[...] * row_ref[...]
    total = jnp.sum(jnp.sum(joint, axis=0, keepdims=True), axis=1, keepdims=True)
    beliefs = joint * (size * size / total)
    beliefs_ref[...] = beliefs
    counts = chip_ref[...] + join_ref[...] + sibling_join_ref[...]
    measured = (counts + noise_ref[...]) * scale
    updated_ref[...] = potential_ref[...] - step_size * (beliefs - measured)


def count_kernel(part, order_ref, left_ref, right_ref, total_ref):
    _, y, z = place()
    clique = y * Z + z
    size = total_ref.shape[0]

    @pl.when(pl.program_id(0) == 0)
    def _():
        total_ref[...] = jnp.zeros_like(total_ref)

    levels = lax.broadcasted_iota(jnp.int32, (size, part), 0).astype(jnp.bfloat16)
    one = jnp.ones((size, part), jnp.bfloat16)
    zero = jnp.zeros((size, part), jnp.bfloat16)

    def onehot(ref, attribute, begin):
        values = ref[pl.ds(lax.rem(attribute, 8), 1), begin : begin + part]
        values = values.astype(jnp.float32).astype(jnp.bfloat16)
        return jnp.where(values == levels, one, zero).astype(jnp.float8_e4m3fn)

    total = total_ref[...]
    for begin in range(0, left_ref.shape[1], part):
        total = total + lax.dot_general(
            onehot(left_ref, order_ref[clique], begin),
            onehot(right_ref, order_ref[clique + 1], begin),
            (((1,), (1,)), ((), ())),
            preferred_element_type=jnp.float32,
        )
    total_ref[...] = total


def shape(*dims):
    return jax.ShapeDtypeStruct(dims, jnp.float32)


PARAMS = pltpu.CompilerParams(vmem_limit_bytes=VMEM_LIMIT)


def count_pairs(order, table_rows, size):
    window, part = 16384, 8192

    def rows_of(offset):
        def block(step, order_ref):
            return (lax.div(order_ref[lax.axis_index("clique") + offset], 8), step)

        return pl.BlockSpec((8, window), block)

    return pl.pallas_call(
        functools.partial(count_kernel, part),
        out_shape=shape(size, size),
        grid_spec=pltpu.PrefetchScalarGridSpec(
            num_scalar_prefetch=1,
            grid=(table_rows.shape[1] // window,),
            in_specs=[rows_of(0), rows_of(1)],
            out_specs=pl.BlockSpec((size, size), lambda step, order_ref: (0, 0)),
        ),
        compiler_params=PARAMS,
        name="counts",
    )(order, table_rows, table_rows)


def everywhere(move):
    pairs = []
    for x in range(4):
        for c in range(2):
            for y in range(Y):
                for z in range(Z):
                    to_x, to_y, to_z = move(x, c, y, z)
                    source = (2 * x + c) * Y * Z + y * Z + z
                    pairs.append((source, (2 * to_x + c) * Y * Z + to_y * Z + to_z))
    return pairs


def exchange(whole, half, near_step, far_step):
    axes = ("dp", "clique")
    return (
        lax.ppermute(whole, axes, everywhere(near_step)),
        lax.ppermute(half, axes, everywhere(lambda x, c, y, z: far_step(x, y, z))),
    )


def per_device(table_rows, attribute_order, log_potential, measure_noise):
    size = log_potential.shape[1]
    potential = log_potential[0]
    call = functools.partial(pl.pallas_call, compiler_params=PARAMS)
    vmem = pl.BlockSpec(memory_space=pltpu.VMEM)
    hbm = pl.BlockSpec(memory_space=pltpu.HBM)
    whole, half = (shape(size, size), shape(size // 2, size))
    order, kernel, half_of_kernel = call(
        read_kernel,
        in_specs=[hbm, hbm],
        out_specs=(vmem, vmem, vmem),
        out_shape=(jax.ShapeDtypeStruct(attribute_order.shape, jnp.int32), whole, half),
        scratch_shapes=[pltpu.VMEM((size, size), jnp.float32), pltpu.SemaphoreType.DMA((2,))],
        name="read",
    )(
        pltpu.with_memory_space_constraint(attribute_order, pltpu.HBM),
        pltpu.with_memory_space_constraint(potential, pltpu.HBM),
    )
    near, far = exchange(
        kernel,
        half_of_kernel,
        lambda x, c, y, z: (x, y, z ^ (1 + 2 * c)),
        lambda x, y, z: (x, y, z ^ 2),
    )
    counts = count_pairs(order, table_rows, size)
    near, far, counts = lax.optimization_barrier((near, far, counts))
    quad, quad_product, half_product = call(
        quad_kernel, out_shape=(shape(QUAD, size, size), whole, half), name="quad"
    )(kernel, near, other_core(near), far, other_core(far))
    across = lax.ppermute(half_product, "clique", along_clique(lambda y, z: (y, z ^ 6)))
    beside = lax.ppermute(half_product, "clique", along_clique(lambda y, z: (y ^ 1, z)))
    counts, quad = lax.optimization_barrier((counts, quad))
    chip_counts, half_counts = call(chip_kernel, out_shape=(whole, half), name="chip")(
        counts, other_core(counts)
    )
    near_counts, far_counts = exchange(
        chip_counts,
        half_counts,
        lambda x, c, y, z: (x ^ (1 + 2 * c), y, z),
        lambda x, y, z: (x ^ 2, y, z),
    )
    relayed = lax.ppermute(across, "clique", along_clique(lambda y, z: (y ^ 1, z)))
    held, beside, far_counts = lax.optimization_barrier((across, beside, far_counts))
    relayed, near_counts = lax.optimization_barrier((relayed, near_counts))
    arrived = (held, beside, relayed)
    block, message = call(
        block_kernel, out_shape=(shape(4, size, size), shape(8, size)), name="block"
    )(quad_product, *arrived, *[other_core(value) for value in arrived])
    message, near_counts = lax.optimization_barrier((message, near_counts))
    joined = call(join_kernel, out_shape=whole, name="join")(near_counts, far_counts)
    arrived = lax.ppermute(message, "clique", along_clique(lambda y, z: (y ^ 3, z)))
    path, known = call(sides_kernel, out_shape=(whole, shape(8, size)), name="sides")(quad, block)
    total_rows = table_rows.shape[1] * lax.axis_size("dp")
    updated, beliefs = call(
        functools.partial(final_kernel, size * size / total_rows),
        out_shape=(whole, whole),
        scratch_shapes=[
            pltpu.VMEM((size, 1), jnp.float32),
            pltpu.VMEM((1, size), jnp.float32),
        ],
        name="final",
    )(
        potential, measure_noise[0], kernel, path, known, arrived, chip_counts, joined,
        other_core(joined),
    )
    return (updated[None], beliefs[None])


def solution(mesh):
    in_specs = (P(None, "dp"), P(), P("clique", None, None), P("clique", None, None))
    out_specs = (P("clique", None, None), P("clique", None, None))
    return jax.shard_map(
        per_device, mesh=mesh, in_specs=in_specs, out_specs=out_specs, check_vma=False
    )
```

```python
import functools

import jax
import jax.numpy as jnp
from jax import lax
from jax.experimental import pallas as pl
from jax.experimental.pallas import tpu as pltpu
from jax.sharding import PartitionSpec as P

step_size = 0.25
shift = 7.0
Y, Z, QUAD = 4, 8, 4
VMEM_LIMIT = 50 << 20


def place():
    dp, clique = (lax.axis_index("dp"), lax.axis_index("clique"))
    return (lax.rem(dp, 2), lax.div(clique, Z), lax.rem(clique, Z))


def along_clique(where):
    return [(y * Z + z, where(y, z)[0] * Z + where(y, z)[1]) for y in range(Y) for z in range(Z)]


def along_dp(where):
    return [(2 * x + c, 2 * where(x, c)[0] + where(x, c)[1]) for x in range(4) for c in range(2)]


def other_core(value):
    return lax.ppermute(value, "dp", along_dp(lambda x, c: (x, 1 - c)))


def in_quad(z, step):
    return z // QUAD * QUAD + (z + step) % QUAD


def split(value):
    high = value.astype(jnp.bfloat16)
    low = (value - high.astype(jnp.float32)).astype(jnp.bfloat16)
    return (high, low)


def product(left, right):
    left_high, left_low = split(left)
    right_high, right_low = split(right)
    dot = functools.partial(jnp.dot, preferred_element_type=jnp.float32)
    return dot(left_high, right_high) + (dot(left_high, right_low) + dot(left_low, right_high))


def diagonal(size):
    rows = lax.broadcasted_iota(jnp.int32, (size, size), 0)
    return rows == lax.broadcasted_iota(jnp.int32, (size, size), 1)


def as_column(row, eye):
    return jnp.sum(jnp.where(eye, row, 0.0), axis=1, keepdims=True)


def as_row(column, eye):
    return jnp.sum(jnp.where(eye, column, 0.0), axis=0, keepdims=True)


def row_times(row, matrix, eye):
    column = as_column(row, eye) / jnp.sum(row, axis=1, keepdims=True)
    return jnp.sum(column * matrix, axis=0, keepdims=True)


def times_row(matrix, row, eye):
    column = jnp.sum(matrix * row, axis=1, keepdims=True)
    return as_row(column, eye) / jnp.sum(column, axis=0, keepdims=True)


def read_kernel(order_hbm, potential_hbm, order_ref, kernel_ref, half_ref, copied_ref, semaphores):
    core, _, _ = place()
    copies = (
        pltpu.make_async_copy(order_hbm, order_ref, semaphores.at[0]),
        pltpu.make_async_copy(potential_hbm, copied_ref, semaphores.at[1]),
    )
    for copy in copies:
        copy.start()
    for copy in copies:
        copy.wait()
    half = half_ref.shape[0]
    kernel_ref[...] = jnp.exp(copied_ref[...] - shift)
    half_ref[...] = kernel_ref[pl.ds(core * half, half), :]


def quad_kernel(kernel_ref, a1, a2, a3, b1, b2, b3, quad_ref, product_ref, half_ref):
    core, _, z = place()
    mine = lax.rem(z, QUAD)
    half, size = half_ref.shape
    quad_ref[mine] = kernel_ref[...]
    for flip, (own, sibling) in enumerate(((a1, b1), (a2, b2), (a3, b3)), 1):
        put_halves(quad_ref, mine ^ flip, own, sibling, core)
    scale = 1.0 / size
    left = product(quad_ref[0], quad_ref[1]) * scale
    right = product(quad_ref[2], quad_ref[3]) * scale
    whole = product(left, right) * scale
    largest = jnp.max(jnp.max(whole, axis=0, keepdims=True), axis=1, keepdims=True)
    product_ref[...] = whole / largest
    half_ref[...] = product_ref[pl.ds(core * half, half), :]


def spots():
    core, y, z = place()
    return (core, y, 2 * lax.rem(y, 2) + lax.div(z, QUAD), lax.rem(z, QUAD))


def put_halves(stack_ref, slot, own, sibling, core):
    half = own.shape[0]
    stack_ref[slot, pl.ds(core * half, half), :] = own[...]
    stack_ref[slot, pl.ds((1 - core) * half, half), :] = sibling[...]


def block_kernel(product_ref, a1, a2, a3, b1, b2, b3, block_ref, message_ref):
    core, y, mine, _ = spots()
    size = product_ref.shape[0]
    block_ref[mine] = product_ref[...]
    for flip, (own, sibling) in enumerate(((a1, b1), (a2, b2), (a3, b3)), 1):
        put_halves(block_ref, mine ^ flip, own, sibling, core)
    eye = diagonal(size)
    ones = jnp.ones((1, size), jnp.float32)

    @pl.when(y < Y // 2)
    def _():
        row = ones
        for position in range(4):
            row = row_times(row, block_ref[position], eye)
        message_ref[...] = jnp.broadcast_to(row, message_ref.shape)

    @pl.when(y >= Y // 2)
    def _():
        row = ones
        for position in range(4):
            row = times_row(block_ref[3 - position], row, eye)
        message_ref[...] = jnp.broadcast_to(row, message_ref.shape)


def unit_product(left, right):
    moved = product(left, right)
    return moved / jnp.max(jnp.max(moved, axis=0, keepdims=True), axis=1, keepdims=True)


def sides_kernel(quad_ref, block_ref, path_ref, known_ref):
    _, y, in_block, mine = spots()
    size = path_ref.shape[0]
    eye = diagonal(size)
    ones = jnp.ones((1, size), jnp.float32)
    start = jnp.where(eye, 1.0, 0.0)

    @pl.when(y >= Y // 2)
    def _():
        path = lax.fori_loop(0, in_block, lambda i, m: unit_product(m, block_ref[i]), start)
        path_ref[...] = lax.fori_loop(0, mine, lambda i, m: unit_product(m, quad_ref[i]), path)
        row = lax.fori_loop(
            0, 3 - in_block, lambda i, row: times_row(block_ref[3 - i], row, eye), ones
        )
        row = lax.fori_loop(
            0, QUAD - 1 - mine, lambda i, row: times_row(quad_ref[QUAD - 1 - i], row, eye), row
        )
        known_ref[...] = jnp.broadcast_to(row, known_ref.shape)

    @pl.when(y < Y // 2)
    def _():
        path = lax.fori_loop(
            0, 3 - in_block, lambda i, m: unit_product(block_ref[3 - i], m), start
        )
        path_ref[...] = lax.fori_loop(
            0, QUAD - 1 - mine, lambda i, m: unit_product(quad_ref[QUAD - 1 - i], m), path
        )
        row = lax.fori_loop(0, in_block, lambda i, row: row_times(row, block_ref[i], eye), ones)
        row = lax.fori_loop(0, mine, lambda i, row: row_times(row, quad_ref[i], eye), row)
        known_ref[...] = jnp.broadcast_to(row, known_ref.shape)


def chip_kernel(own_ref, sibling_ref, both_ref, half_ref):
    core, _, _ = place()
    half = half_ref.shape[0]
    both_ref[...] = own_ref[...] + sibling_ref[...]
    half_ref[...] = both_ref[pl.ds(core * half, half), :]


def join_kernel(near_ref, far_ref, sum_ref):
    core, _, _ = place()
    half = far_ref.shape[0]
    sum_ref[...] = near_ref[...]
    sum_ref[pl.ds(core * half, half), :] += far_ref[...]


def final_kernel(
    scale, potential_ref, noise_ref, kernel_ref, path_ref, known_ref, message_ref, chip_ref,
    join_ref, sibling_join_ref, updated_ref, beliefs_ref, column_ref, row_ref
):
    _, y, _, _ = spots()
    size = potential_ref.shape[0]
    eye = diagonal(size)
    known, message = (known_ref[0:1, :], message_ref[0:1, :])

    @pl.when(y >= Y // 2)
    def _():
        forward = row_times(message, path_ref[...], eye)
        column_ref[...] = as_column(forward, eye) / jnp.sum(forward, axis=1, keepdims=True)
        row_ref[...] = known

    @pl.when(y < Y // 2)
    def _():
        column_ref[...] = as_column(known, eye) / jnp.sum(known, axis=1, keepdims=True)
        row_ref[...] = times_row(path_ref[...], message, eye)

    joint = column_ref[...] * kernel_ref[...] * row_ref[...]
    total = jnp.sum(jnp.sum(joint, axis=0, keepdims=True), axis=1, keepdims=True)
    beliefs = joint * (size * size / total)
    beliefs_ref[...] = beliefs
    counts = chip_ref[...] + join_ref[...] + sibling_join_ref[...]
    measured = (counts + noise_ref[...]) * scale
    updated_ref[...] = potential_ref[...] - step_size * (beliefs - measured)


def count_kernel(part, order_ref, left_ref, right_ref, total_ref):
    _, y, z = place()
    clique = y * Z + z
    size = total_ref.shape[0]

    @pl.when(pl.program_id(0) == 0)
    def _():
        total_ref[...] = jnp.zeros_like(total_ref)

    levels = lax.broadcasted_iota(jnp.int32, (size, part), 0).astype(jnp.bfloat16)
    one = jnp.ones((size, part), jnp.bfloat16)
    zero = jnp.zeros((size, part), jnp.bfloat16)

    def onehot(ref, attribute, begin):
        values = ref[pl.ds(lax.rem(attribute, 8), 1), begin : begin + part]
        values = values.astype(jnp.float32).astype(jnp.bfloat16)
        return jnp.where(values == levels, one, zero).astype(jnp.float8_e4m3fn)

    total = total_ref[...]
    for begin in range(0, left_ref.shape[1], part):
        total = total + lax.dot_general(
            onehot(left_ref, order_ref[clique], begin),
            onehot(right_ref, order_ref[clique + 1], begin),
            (((1,), (1,)), ((), ())),
            preferred_element_type=jnp.float32,
        )
    total_ref[...] = total


def shape(*dims):
    return jax.ShapeDtypeStruct(dims, jnp.float32)


PARAMS = pltpu.CompilerParams(vmem_limit_bytes=VMEM_LIMIT)


def count_pairs(order, table_rows, size):
    window, part = 16384, 8192

    def rows_of(offset):
        def block(step, order_ref):
            return (lax.div(order_ref[lax.axis_index("clique") + offset], 8), step)

        return pl.BlockSpec((8, window), block)

    return pl.pallas_call(
        functools.partial(count_kernel, part),
        out_shape=shape(size, size),
        grid_spec=pltpu.PrefetchScalarGridSpec(
            num_scalar_prefetch=1,
            grid=(table_rows.shape[1] // window,),
            in_specs=[rows_of(0), rows_of(1)],
            out_specs=pl.BlockSpec((size, size), lambda step, order_ref: (0, 0)),
        ),
        compiler_params=PARAMS,
        name="counts",
    )(order, table_rows, table_rows)


def everywhere(move):
    pairs = []
    for x in range(4):
        for c in range(2):
            for y in range(Y):
                for z in range(Z):
                    to_x, to_y, to_z = move(x, c, y, z)
                    source = (2 * x + c) * Y * Z + y * Z + z
                    pairs.append((source, (2 * to_x + c) * Y * Z + to_y * Z + to_z))
    return pairs


def exchange(whole, half, near_step, far_step):
    axes = ("dp", "clique")
    return (
        lax.ppermute(whole, axes, everywhere(near_step)),
        lax.ppermute(half, axes, everywhere(lambda x, c, y, z: far_step(x, y, z))),
    )


def per_device(table_rows, attribute_order, log_potential, measure_noise):
    size = log_potential.shape[1]
    potential = log_potential[0]
    call = functools.partial(pl.pallas_call, compiler_params=PARAMS)
    vmem = pl.BlockSpec(memory_space=pltpu.VMEM)
    hbm = pl.BlockSpec(memory_space=pltpu.HBM)
    whole, half = (shape(size, size), shape(size // 2, size))
    order, kernel, half_of_kernel = call(
        read_kernel,
        in_specs=[hbm, hbm],
        out_specs=(vmem, vmem, vmem),
        out_shape=(jax.ShapeDtypeStruct(attribute_order.shape, jnp.int32), whole, half),
        scratch_shapes=[pltpu.VMEM((size, size), jnp.float32), pltpu.SemaphoreType.DMA((2,))],
        name="read",
    )(
        pltpu.with_memory_space_constraint(attribute_order, pltpu.HBM),
        pltpu.with_memory_space_constraint(potential, pltpu.HBM),
    )
    quads = [
        lax.ppermute(half_of_kernel, "clique", along_clique(lambda y, z, f=f: (y, z ^ f)))
        for f in (1, 2, 3)
    ]
    counts = count_pairs(order, table_rows, size)
    quads, counts = lax.optimization_barrier((quads, counts))
    quad, quad_product, half_product = call(
        quad_kernel, out_shape=(shape(QUAD, size, size), whole, half), name="quad"
    )(kernel, *quads, *[other_core(value) for value in quads])
    across = lax.ppermute(half_product, "clique", along_clique(lambda y, z: (y, z ^ 6)))
    beside = lax.ppermute(half_product, "clique", along_clique(lambda y, z: (y ^ 1, z)))
    counts, quad = lax.optimization_barrier((counts, quad))
    chip_counts, half_counts = call(chip_kernel, out_shape=(whole, half), name="chip")(
        counts, other_core(counts)
    )
    near_counts, far_counts = exchange(
        chip_counts,
        half_counts,
        lambda x, c, y, z: (x ^ (1 + 2 * c), y, z),
        lambda x, y, z: (x ^ 2, y, z),
    )
    relayed = lax.ppermute(across, "clique", along_clique(lambda y, z: (y ^ 1, z)))
    held, beside, far_counts = lax.optimization_barrier((across, beside, far_counts))
    relayed, near_counts = lax.optimization_barrier((relayed, near_counts))
    arrived = (held, beside, relayed)
    block, message = call(
        block_kernel, out_shape=(shape(4, size, size), shape(8, size)), name="block"
    )(quad_product, *arrived, *[other_core(value) for value in arrived])
    message, near_counts = lax.optimization_barrier((message, near_counts))
    joined = call(join_kernel, out_shape=whole, name="join")(near_counts, far_counts)
    arrived = lax.ppermute(message, "clique", along_clique(lambda y, z: (y ^ 3, z)))
    path, known = call(sides_kernel, out_shape=(whole, shape(8, size)), name="sides")(quad, block)
    total_rows = table_rows.shape[1] * lax.axis_size("dp")
    updated, beliefs = call(
        functools.partial(final_kernel, size * size / total_rows),
        out_shape=(whole, whole),
        scratch_shapes=[
            pltpu.VMEM((size, 1), jnp.float32),
            pltpu.VMEM((1, size), jnp.float32),
        ],
        name="final",
    )(
        potential, measure_noise[0], kernel, path, known, arrived, chip_counts, joined,
        other_core(joined),
    )
    return (updated[None], beliefs[None])


def solution(mesh):
    in_specs = (P(None, "dp"), P(), P("clique", None, None), P("clique", None, None))
    out_specs = (P("clique", None, None), P("clique", None, None))
    return jax.shard_map(
        per_device, mesh=mesh, in_specs=in_specs, out_specs=out_specs, check_vma=False
    )
```
